32 devices in a mesh: row: 4 (over z), col: 8 (over y, x, core).
Axes of the slice: x: 2, y: 2, z: 4, core: 2. Of those that a mesh axis runs over, the one named last changes fastest.
Arguments:
- hidden_in: bfloat16 [8192, 2048], P('row', 'col'), may hold values from -6 to 6
- seg_ids: int32 [8192], P('row'), may hold values from 0 to 15, never falling along the last dimension, each value on 1 to 2000 neighbouring positions
- cotangent: bfloat16 [8192, 2048], P('row', 'col'), may hold values from -6 to 6
- norm_mixer: float32 [2048], P('col'), may hold values from 0.5 to 1.5
- w_query: bfloat16 [2048, 2048], P('row', 'col'), may hold values from -0.125 to 0.125
- w_key: bfloat16 [2048, 2048], P('row', 'col'), may hold values from -0.125 to 0.125
- w_value: bfloat16 [2048, 4096], P('row', 'col'), may hold values from -0.125 to 0.125
- w_gate: bfloat16 [2048, 4096], P('row', 'col'), may hold values from -0.125 to 0.125
- w_beta: bfloat16 [2048, 16], P('row', 'col'), may hold values from -0.125 to 0.125
- w_decay: bfloat16 [2048, 16], P('row', 'col'), may hold values from -0.125 to 0.125
- decay_log: float32 [16], P('col'), may hold values from -6.5 to -3
- conv_query: float32 [4, 2048], P(None, 'col'), may hold values from -3 to 3
- conv_key: float32 [4, 2048], P(None, 'col'), may hold values from -3 to 3
- conv_value: float32 [4, 4096], P(None, 'col'), may hold values from -3 to 3
- norm_gated: float32 [4096], P('col'), may hold values from 0.5 to 1.5
- w_out: bfloat16 [4096, 2048], P('col', 'row'), may hold values from -0.1875 to 0.1875
- norm_ffn: float32 [2048], P('col'), may hold values from 0.5 to 1.5
- w_ffn_gate: bfloat16 [2048, 5632], P('row', 'col'), may hold values from -0.125 to 0.125
- w_ffn_up: bfloat16 [2048, 5632], P('row', 'col'), may hold values from -0.125 to 0.125
- w_ffn_down: bfloat16 [5632, 2048], P('col', 'row'), may hold values from -0.078125 to 0.078125
Outputs:
- block_out: bfloat16 [8192, 2048], P('row', 'col')
- grad_input: float32 [8192, 2048], P('row', 'col')
- grad_norm_mixer: float32 [2048], P('col')
- grad_w_query: float32 [2048, 2048], P('row', 'col')
- grad_w_key: float32 [2048, 2048], P('row', 'col')
- grad_w_value: float32 [2048, 4096], P('row', 'col')
- grad_w_gate: float32 [2048, 4096], P('row', 'col')
- grad_w_beta: float32 [2048, 16], P('row', 'col')
- grad_w_decay: float32 [2048, 16], P('row', 'col')
- grad_decay_log: float32 [16], P('col')
- grad_conv_query: float32 [4, 2048], P(None, 'col')
- grad_conv_key: float32 [4, 2048], P(None, 'col')
- grad_conv_value: float32 [4, 4096], P(None, 'col')
- grad_norm_gated: float32 [4096], P('col')
- grad_w_out: float32 [4096, 2048], P('col', 'row')
- grad_norm_ffn: float32 [2048], P('col')
- grad_w_ffn_gate: float32 [2048, 5632], P('row', 'col')
- grad_w_ffn_up: float32 [2048, 5632], P('row', 'col')
- grad_w_ffn_down: float32 [5632, 2048], P('col', 'row')
The draws below stay inside these ranges and needn't reach their ends.
Inputs may be any that keep to these rules, and one draw needn't show every extreme that they name: `seg_ids`: document ids of the tokens, never falling; a document holds 1 to 2000 tokens and one holds exactly 2000.
All inputs are finite; a program needn't handle non-finite values.
Results may differ from the reference program's by a relative error of at most 0.02.
Values may be sent and summed in bfloat16 or wider, within the bound.
A program may use at most 384 MiB of HBM per device.

```python
import math
import jax
import jax.numpy as jnp
import numpy as np
from jax import lax

D = 2048
H = 16
DK = 128
DV = 256
FF = 5632
CONV = 4
BLOCK = 64
SEQ = 1024
TOKENS = 8192
KEYS = 2048
VALS = 4096
DOCS = 16
DOC_MOST = 2000


def block_levels(key, shape, shards, least, high):
    gain, own = 1.0, jax.random.fold_in(key, 6)
    for axis_at, parts in shards:
        draws = jnp.exp(jax.random.uniform(jax.random.fold_in(own, axis_at), (parts,), jnp.float32, least / len(shards), high / len(shards)))
        gain = gain * jnp.repeat(draws, shape[axis_at] // parts).reshape([-1 if axis == axis_at else 1 for axis in range(len(shape))])
    return gain


def split_up(number_of, total, bound, skew):
    portions = [(1 << 20) // math.isqrt(grade ** skew) + 1 for grade in range(2, number_of + 1)]
    rest, counts = total - bound - (number_of - 1), [1] * (number_of - 1)
    while rest > 0:
        movable = [i for i in range(number_of - 1) if counts[i] < bound]
        mass, remaining = sum([portions[i] for i in movable]), rest
        for i in movable:
            more = min(bound - counts[i], max(1, remaining * portions[i] // mass), rest)
            counts[i] = counts[i] + more
            rest = rest - more
    return np.array([bound] + counts)


def uneven(rng, number_of, total, reach, skew):
    if number_of == 2:
        one = jax.random.randint(rng, (), max(1, total - reach), min(reach, total - 1) + 1)
        return jnp.stack([one, total - one])
    sizes = jnp.asarray(split_up(number_of, total, reach, skew), jnp.int32)
    twos = (number_of - 1) // 2
    giver, taker = sizes[1:1 + 2 * twos:2], sizes[2:2 + 2 * twos:2]
    slack = jnp.minimum(giver - 1, reach - taker)
    passed = jax.random.randint(jax.random.fold_in(rng, 1), (twos,), 0, 1 << 20) % (slack + 1)
    sizes = sizes.at[1:1 + 2 * twos:2].set(giver - passed).at[2:2 + 2 * twos:2].set(taker + passed)
    return sizes[jax.random.permutation(jax.random.fold_in(rng, 2), number_of)]


def gaussian(key, dims, spread, limit, split=(), kind=jnp.bfloat16):
    result = jax.random.normal(key, dims, jnp.float32) * spread
    if len(split) > 0:
        result = block_levels(key, dims, split, -0.22, 0.18) * result
    return jnp.clip(result, min=-limit, max=limit).astype(kind)


def setup_inputs(seed: int = 0) -> dict:
    key_list = jax.random.split(jax.random.key(seed), 21)
    hidden_in = gaussian(key_list[0], (TOKENS, D), 1.0, 6.0, ((0, 4), (1, 8)))
    seg_ids = jnp.searchsorted(jnp.cumsum(uneven(key_list[1], DOCS, TOKENS, DOC_MOST, 1)), jnp.arange(TOKENS), side="right").astype(jnp.int32)
    cotangent = gaussian(key_list[2], (TOKENS, D), 1.0, 6.0, ((0, 4), (1, 8)))
    norm_mixer = jnp.clip(1.0 + 0.1 * jax.random.normal(key_list[3], (D,), jnp.float32), 0.5, 1.5)
    w_query = gaussian(key_list[4], (D, KEYS), D ** -0.5, 0.125, ((0, 4), (1, 8)))
    w_key = gaussian(key_list[5], (D, KEYS), D ** -0.5, 0.125, ((0, 4), (1, 8)))
    w_value = gaussian(key_list[6], (D, VALS), D ** -0.5, 0.125, ((0, 4), (1, 8)))
    w_gate = gaussian(key_list[7], (D, VALS), D ** -0.5, 0.125, ((0, 4), (1, 8)))
    w_beta = gaussian(key_list[8], (D, H), D ** -0.5, 0.125, ((0, 4), (1, 8)))
    w_decay = gaussian(key_list[9], (D, H), D ** -0.5, 0.125, ((0, 4), (1, 8)))
    decay_log = jnp.clip(-6.5 + 3.5 * jax.random.uniform(key_list[10], (H,), jnp.float32) ** block_levels(key_list[10], (H,), ((0, 8),), -0.2, 0.2), -6.5, -3.0)
    conv_query = gaussian(key_list[11], (CONV, KEYS), CONV ** -0.5, 3.0, ((1, 8),), jnp.float32)
    conv_key = gaussian(key_list[12], (CONV, KEYS), CONV ** -0.5, 3.0, ((1, 8),), jnp.float32)
    conv_value = gaussian(key_list[13], (CONV, VALS), CONV ** -0.5, 3.0, ((1, 8),), jnp.float32)
    norm_gated = jnp.clip(1.0 + 0.1 * jax.random.normal(key_list[14], (VALS,), jnp.float32), 0.5, 1.5)
    w_out = gaussian(key_list[15], (VALS, D), (VALS // 4) ** -0.5, 0.1875, ((0, 8), (1, 4)))
    norm_ffn = jnp.clip(1.0 + 0.1 * jax.random.normal(key_list[16], (D,), jnp.float32), 0.5, 1.5)
    w_ffn_gate = gaussian(key_list[17], (D, FF), D ** -0.5, 0.125, ((0, 4), (1, 8)))
    w_ffn_up = gaussian(key_list[18], (D, FF), D ** -0.5, 0.125, ((0, 4), (1, 8)))
    w_ffn_down = gaussian(key_list[19], (FF, D), FF ** -0.5, 0.078125, ((0, 8), (1, 4)))
    return dict(hidden_in=hidden_in, seg_ids=seg_ids, cotangent=cotangent, norm_mixer=norm_mixer, w_query=w_query, w_key=w_key, w_value=w_value, w_gate=w_gate, w_beta=w_beta, w_decay=w_decay, decay_log=decay_log, conv_query=conv_query, conv_key=conv_key, conv_value=conv_value, norm_gated=norm_gated, w_out=w_out, norm_ffn=norm_ffn, w_ffn_gate=w_ffn_gate, w_ffn_up=w_ffn_up, w_ffn_down=w_ffn_down)


EPSILON = 1e-06
TOP_PRECISION = lax.Precision.HIGHEST

@jax.custom_vjp
def low(v):
    return lax.optimization_barrier(v.astype(jnp.bfloat16)).astype(jnp.float32)

@jax.custom_vjp
def low_back(v):
    return v

def low_keep(v):
    return (low(v), None)

def low_pass(kept, grad):
    return (grad,)

def back_keep(v):
    return (v, None)

def back_low(kept, grad):
    return (low(grad),)
low.defvjp(low_keep, low_pass)
low_back.defvjp(back_keep, back_low)

def shifted(values, offset):
    if offset == 0:
        return values
    filler = jnp.zeros((offset,) + values.shape[1:], values.dtype)
    return jnp.concatenate([filler, values[:values.shape[0] - offset]], axis=0)

def tap_masks(seg_ids):
    position = jnp.arange(seg_ids.shape[0], dtype=jnp.int32) % SEQ
    return [((seg_ids == shifted(seg_ids, offset)) & (position >= offset)).astype(jnp.float32) for offset in range(CONV)]

def rms_norm(values, gains):
    return values * lax.rsqrt(lax.optimization_barrier(jnp.mean(values * values, axis=-1, keepdims=True)) + EPSILON) * gains

def short_conv(values, tap_weights, taps_valid):
    summed = jnp.zeros_like(values)
    for offset in range(CONV):
        summed = summed + tap_weights[offset] * shifted(values, offset) * taps_valid[offset][:, None]
    return jax.nn.silu(summed)

def unit_heads(values):
    shaped = values.reshape(values.shape[0], -1, DK)
    shaped = shaped * lax.rsqrt(lax.optimization_barrier(jnp.sum(shaped * shaped, axis=-1, keepdims=True)) + EPSILON)
    return shaped.reshape(values.shape)

def product(first_op, second_op):
    return jnp.dot(first_op, second_op, precision=TOP_PRECISION, preferred_element_type=jnp.float32)

def delta_rule(queries, key_rows, values, strength, retain):
    seq_count = TOKENS // SEQ

    def split_blocks(array):
        shaped = array.reshape((seq_count, SEQ // BLOCK, BLOCK) + array.shape[1:])
        return jnp.moveaxis(shaped, 1, 0)

    def one_block(carried_state, block_in):

        def one_token(state_now, token_in):
            query_t, key_t, value_t, beta_t, retain_t = token_in
            state_now = retain_t[:, :, None, None] * state_now
            predicted = jnp.einsum('shk,shkv->shv', key_t, state_now, precision=TOP_PRECISION)
            state_now = state_now + jnp.einsum('shk,shv->shkv', key_t, beta_t[:, :, None] * (value_t - predicted), precision=TOP_PRECISION)
            return (state_now, jnp.einsum('shk,shkv->shv', query_t, state_now, precision=TOP_PRECISION) * DK ** (-0.5))
        carried_state, output_rows = lax.scan(one_token, carried_state, tuple((jnp.moveaxis(member, 1, 0) for member in block_in)))
        return (carried_state, jnp.moveaxis(output_rows, 0, 1))
    initial = jnp.zeros((seq_count, H, DK, DV), jnp.float32)
    inputs_all = (queries.reshape(TOKENS, H, DK), key_rows.reshape(TOKENS, H, DK), values.reshape(TOKENS, H, DV), strength, retain)
    _, output_rows = lax.scan(jax.checkpoint(one_block), initial, tuple((split_blocks(member) for member in inputs_all)))
    return jnp.moveaxis(output_rows, 0, 1).reshape(TOKENS, VALS)

def gated_norm(mixed_out, gains, proj_gate):
    shaped = mixed_out.reshape(TOKENS, H, DV)
    shaped = shaped * lax.rsqrt(lax.optimization_barrier(jnp.mean(shaped * shaped, axis=-1, keepdims=True)) + EPSILON)
    shaped = shaped * gains.reshape(H, DV) * jax.nn.silu(proj_gate).reshape(TOKENS, H, DV)
    return shaped.reshape(TOKENS, VALS)

def reference(hidden_in, seg_ids, cotangent, norm_mixer, w_query, w_key, w_value, w_gate, w_beta, w_decay, decay_log, conv_query, conv_key, conv_value, norm_gated, w_out, norm_ffn, w_ffn_gate, w_ffn_up, w_ffn_down):
    taps_valid = tap_masks(seg_ids)

    def forward(hidden, norm_mixer, w_query, w_key, w_value, w_gate, w_beta, w_decay, decay_log, conv_query, conv_key, conv_value, norm_gated, w_out, norm_ffn, w_ffn_gate, w_ffn_up, w_ffn_down):
        normed = low(rms_norm(hidden, norm_mixer))
        proj_query = low_back(product(normed, w_query))
        proj_key = low_back(product(normed, w_key))
        proj_value = low_back(product(normed, w_value))
        proj_gate = low_back(product(normed, w_gate))
        proj_beta = low_back(product(normed, w_beta))
        proj_decay = low_back(product(normed, w_decay))
        queries = low(unit_heads(short_conv(proj_query, conv_query, taps_valid)))
        key_rows = low(unit_heads(short_conv(proj_key, conv_key, taps_valid)))
        values = low(short_conv(proj_value, conv_value, taps_valid))
        strength = jax.nn.sigmoid(proj_beta)
        log_decay = -jnp.exp(decay_log) * jax.nn.softplus(proj_decay)
        retain = jnp.exp(log_decay) * taps_valid[1][:, None]
        mixed_out = delta_rule(queries, key_rows, values, strength, retain)
        gated = low(gated_norm(mixed_out, norm_gated, proj_gate))
        middle = hidden + low_back(product(gated, w_out))
        normed_ffn = low(rms_norm(middle, norm_ffn))
        gate_pre = low_back(product(normed_ffn, w_ffn_gate))
        up_pre = low_back(product(normed_ffn, w_ffn_up))
        inner_act = low(jax.nn.silu(gate_pre) * up_pre)
        return middle + low_back(product(inner_act, w_ffn_down))
    floats = [member.astype(jnp.float32) for member in (hidden_in, norm_mixer, w_query, w_key, w_value, w_gate, w_beta, w_decay, decay_log, conv_query, conv_key, conv_value, norm_gated, w_out, norm_ffn, w_ffn_gate, w_ffn_up, w_ffn_down)]
    block_out, pullback = jax.vjp(forward, *floats)
    grad_input, grad_norm_mixer, grad_w_query, grad_w_key, grad_w_value, grad_w_gate, grad_w_beta, grad_w_decay, grad_decay_log, grad_conv_query, grad_conv_key, grad_conv_value, grad_norm_gated, grad_w_out, grad_norm_ffn, grad_w_ffn_gate, grad_w_ffn_up, grad_w_ffn_down = pullback(cotangent.astype(jnp.float32))
    return (block_out.astype(jnp.bfloat16), grad_input, grad_norm_mixer, grad_w_query, grad_w_key, grad_w_value, grad_w_gate, grad_w_beta, grad_w_decay, grad_decay_log, grad_conv_query, grad_conv_key, grad_conv_value, grad_norm_gated, grad_w_out, grad_norm_ffn, grad_w_ffn_gate, grad_w_ffn_up, grad_w_ffn_down)
```

```python
import functools

import jax
import jax.numpy as jnp
from jax import lax
from jax.experimental import pallas as pl
from jax.experimental.pallas import tpu as pltpu
from jax.sharding import PartitionSpec as P

D = 2048
DK = 128
DV = 256
CONV = 4
SEQ = 1024
CHUNK = 128
EPSILON = 1e-06
SCALE = DK ** (-0.5)
f32 = jnp.float32
bf16 = jnp.bfloat16


def mm(a, b, dims=((1,), (0,))):
    return lax.dot_general(a, b, (dims, ((), ())), preferred_element_type=f32)


def split(a):
    hi = a.astype(bf16)
    return hi, (a - hi.astype(f32)).astype(bf16)


def mm3(a, b):
    ah, al = split(a)
    bh, bl = split(b)
    return mm(ah, bh) + (mm(ah, bl) + mm(al, bh))


def sigmoid(u):
    return 1.0 / (1.0 + jnp.exp(-u))


def iotas(n):
    return (
        lax.broadcasted_iota(jnp.int32, (n, n), 0),
        lax.broadcasted_iota(jnp.int32, (n, n), 1),
    )


def unit_lower_inverse(a, row, col):
    n = a.shape[0]
    eye = (row == col).astype(f32)
    base = 8
    d = jnp.where(row // base == col // base, a, 0.0)
    d2 = mm3(d, d)
    x = eye - d
    x = x + mm3(x, d2)
    d4 = mm3(d2, d2)
    x = x + mm3(x, d4)
    size = base
    while size < n:
        off = jnp.where((row // (2 * size) == col // (2 * size)) & (row // size != col // size), a, 0.0)
        xh = x.astype(bf16)
        x = x - mm(xh, mm(off.astype(bf16), xh).astype(bf16))
        size *= 2
    return x


def conv_taps(buf, s, width, weights, masks):
    pre = weights[0:1] * buf[s, 8 : 8 + CHUNK, :]
    for j in range(1, CONV):
        pre = pre + weights[j : j + 1] * buf[s, 8 - j : 8 - j + CHUNK, :] * masks[j - 1]
    return pre


def forward_kernel(heads, seqs, pq, pk, pv, pg, cols, rows, wq, wk, wv, gain,
                   gated, inv_out, upd_out, state_out, state, bq, bk, bv):
    step = pl.program_id(0)

    @pl.when(step == 0)
    def _():
        state[...] = jnp.zeros_like(state)
        for buf in (bq, bk, bv):
            buf[:, 0:8, :] = jnp.zeros_like(buf[:, 0:8, :])

    row, col = iotas(CHUNK)
    lower = row >= col
    tril = lower.astype(bf16)
    for s in range(seqs):
        cc = cols[s]
        rr = rows[s]
        masks = [cc[:, j : j + 1] for j in range(CONV - 1)]
        ch, cl = split(cc)
        csum = mm(tril, ch) + mm(tril, cl)
        rh, rl = split(rr)
        rsum = mm(rh, tril, ((1,), (1,))) + mm(rl, tril, ((1,), (1,)))
        same = (cc[:, 6:7] == rr[6:7, :]) & lower
        for src, buf in ((pq, bq), (pk, bk), (pv, bv)):
            buf[s, 8 : 8 + CHUNK, :] = src[s]
        cq = conv_taps(bq, s, heads * DK, wq, masks)
        ck = conv_taps(bk, s, heads * DK, wk, masks)
        cv = conv_taps(bv, s, heads * DV, wv, masks)
        for buf in (bq, bk, bv):
            buf[s, 0:8, :] = buf[s, CHUNK : CHUNK + 8, :]
        aq = cq * sigmoid(cq)
        ak = ck * sigmoid(ck)
        av = cv * sigmoid(cv)
        for h in range(heads):
            keys = slice(h * DK, (h + 1) * DK)
            vals = slice(h * DV, (h + 1) * DV)
            q = aq[:, keys]
            q = (q * lax.rsqrt(jnp.sum(q * q, axis=1, keepdims=True) + EPSILON)).astype(bf16)
            k = ak[:, keys]
            k = (k * lax.rsqrt(jnp.sum(k * k, axis=1, keepdims=True) + EPSILON)).astype(bf16)
            v = av[:, vals].astype(bf16).astype(f32)
            beta = cc[:, 8 + h : 9 + h]
            at = 8 + heads + h
            gcol = csum[:, at : at + 1]
            grow = rsum[at : at + 1, :]
            decay = jnp.where(same, jnp.exp(jnp.minimum(gcol - grow, 0.0)), 0.0)
            start = jnp.exp(gcol) * cc[:, 7:8]
            end = jnp.exp(jnp.minimum(gcol[CHUNK - 1 :, :] - gcol, 0.0)) * jnp.where(
                cc[:, 6:7] == cc[CHUNK - 1 :, 6:7], 1.0, 0.0
            )
            kk = mm(k, k, ((1,), (1,)))
            qk = mm(q, k, ((1,), (1,)))
            coupling = jnp.where(row > col, beta * decay * kk, 0.0)
            inv = unit_lower_inverse(coupling, row, col).astype(bf16)
            inv_out[s, h] = inv
            begin = state[s, h]
            state_out[0, s, h] = begin
            low = begin.astype(bf16)
            right = beta * (v - start * mm(k, low))
            upd = mm(inv, right.astype(bf16)).astype(bf16)
            upd_out[s, :, vals] = upd
            mixed = (start * mm(q, low) + mm((decay * qk).astype(bf16), upd)) * SCALE
            kend = (end * k.astype(f32)).astype(bf16)
            state[s, h] = start[CHUNK - 1 :, :] * begin + mm(kend, upd, ((0,), (0,)))
            gate = pg[s, :, vals]
            scaled = mixed * lax.rsqrt(jnp.mean(mixed * mixed, axis=1, keepdims=True) + EPSILON)
            gated[s, :, vals] = (scaled * gain[:, vals] * (gate * sigmoid(gate))).astype(bf16)


def backward_kernel(heads, seqs, dgated, pq, pk, pv, pg, hq, hk, hv, cols, rows, inv_in, upd_in, state_in,
                    wq, wk, wv, gain,
                    dpq, dpk, dpv, dpg, dcols, dwq, dwk, dwv, dgain,
                    dstate, bq, bk, bv, tq, tk, tv):
    step = pl.program_id(0)

    @pl.when(step == 0)
    def _():
        dstate[...] = jnp.zeros_like(dstate)
        for buf in (tq, tk, tv):
            buf[:, CHUNK : CHUNK + 8, :] = jnp.zeros_like(buf[:, CHUNK : CHUNK + 8, :])
        for out in (dwq, dwk, dwv, dgain):
            out[...] = jnp.zeros_like(out)

    row, col = iotas(CHUNK)
    lower = row >= col
    tril = lower.astype(bf16)
    lane = lax.broadcasted_iota(jnp.int32, (CHUNK, 2 * heads), 1)
    last = lax.broadcasted_iota(jnp.int32, (CHUNK, 1), 0) == CHUNK - 1
    for s in range(seqs):
        cc = cols[s]
        rr = rows[s]
        masks = [cc[:, j : j + 1] for j in range(CONV - 1)]
        ahead = [cc[:, 3 + j : 4 + j] for j in range(CONV - 1)]
        ch, cl = split(cc)
        csum = mm(tril, ch) + mm(tril, cl)
        rh, rl = split(rr)
        rsum = mm(rh, tril, ((1,), (1,))) + mm(rl, tril, ((1,), (1,)))
        same = (cc[:, 6:7] == rr[6:7, :]) & lower
        pres = []
        for src, halo, buf, weights in ((pq, hq, bq, wq), (pk, hk, bk, wk), (pv, hv, bv, wv)):
            buf[s, 0:8, :] = halo[s]
            buf[s, 8 : 8 + CHUNK, :] = src[s]
            pres.append(conv_taps(buf, s, None, weights, masks))
        sigs = [sigmoid(pre) for pre in pres]
        acts = [pre * sig for pre, sig in zip(pres, sigs)]
        dcol = jnp.zeros((CHUNK, 2 * heads), f32)
        for h in range(heads):
            keys = slice(h * DK, (h + 1) * DK)
            vals = slice(h * DV, (h + 1) * DV)
            q = acts[0][:, keys]
            rq = lax.rsqrt(jnp.sum(q * q, axis=1, keepdims=True) + EPSILON)
            qn = q * rq
            q = qn.astype(bf16)
            k = acts[1][:, keys]
            rk = lax.rsqrt(jnp.sum(k * k, axis=1, keepdims=True) + EPSILON)
            kn = k * rk
            k = kn.astype(bf16)
            v = acts[2][:, vals].astype(bf16).astype(f32)
            beta = cc[:, 8 + h : 9 + h]
            at = 8 + heads + h
            gcol = csum[:, at : at + 1]
            grow = rsum[at : at + 1, :]
            decay = jnp.where(same, jnp.exp(jnp.minimum(gcol - grow, 0.0)), 0.0)
            start = jnp.exp(gcol) * cc[:, 7:8]
            end = jnp.exp(jnp.minimum(gcol[CHUNK - 1 :, :] - gcol, 0.0)) * jnp.where(
                cc[:, 6:7] == cc[CHUNK - 1 :, 6:7], 1.0, 0.0
            )
            kk = mm(k, k, ((1,), (1,)))
            qk = mm(q, k, ((1,), (1,)))
            plain = jnp.where(row > col, decay * kk, 0.0)
            scores = decay * qk
            scores_low = scores.astype(bf16)
            inv = inv_in[s, h]
            upd = upd_in[s, :, vals]
            begin = state_in[0, s, h]
            low = begin.astype(bf16)
            ks = mm(k, low)
            qs = mm(q, low)
            mixed = (start * qs + mm(scores_low, upd)) * SCALE
            gate = pg[s, :, vals]
            sg = sigmoid(gate)
            silu = gate * sg
            rm = lax.rsqrt(jnp.mean(mixed * mixed, axis=1, keepdims=True) + EPSILON)
            scaled = mixed * rm
            dy = dgated[s, :, vals]
            dyn = dy * scaled
            gains = gain[:, vals]
            dgain[:, vals] += jnp.sum(dyn * silu, axis=0, keepdims=True)
            dpg[s, :, vals] = (dyn * gains * (sg * (1.0 + gate * (1.0 - sg)))).astype(bf16)
            dscaled = dy * gains * silu
            dmixed = rm * (dscaled - scaled * jnp.mean(dscaled * scaled, axis=1, keepdims=True))
            dout = (dmixed * SCALE)
            dlow = dout.astype(bf16)
            ds = dstate[s, h]
            dsl = ds.astype(bf16)
            kf = k.astype(f32)
            kend = (end * kf).astype(bf16)
            dupd = mm(scores_low, dlow, ((0,), (0,))) + mm(kend, dsl)
            dright = mm(inv, dupd.astype(bf16), ((0,), (0,)))
            drl = dright.astype(bf16)
            dscore = mm(dlow, upd, ((1,), (1,)))
            dcoup = -mm(drl, upd, ((1,), (1,)))
            uds = mm(upd, dsl, ((1,), (1,)))
            w = beta * dright
            wa = (start * w).astype(bf16)
            dsc = (dscore * decay).astype(bf16)
            dqn = start * mm(dlow, low, ((1,), (1,))) + mm(dsc, k)
            g = jnp.where(row > col, beta * dcoup * decay, 0.0)
            dkn = (
                end * uds
                - mm(wa, low, ((1,), (1,)))
                + mm(dsc, q, ((0,), (0,)))
                + mm((g + g.T).astype(bf16), k)
            )
            dbeta = jnp.sum(dright * (v - start * ks), axis=1, keepdims=True) + jnp.sum(
                dcoup * plain, axis=1, keepdims=True
            )
            dstart = jnp.sum(dout * qs - w * ks, axis=1, keepdims=True)
            dend = jnp.sum(kf * uds, axis=1, keepdims=True) * end
            z = dscore * scores + dcoup * (beta * plain)
            final = start[CHUNK - 1 :, :]
            carried = jnp.sum(jnp.sum(ds * begin, axis=1, keepdims=True), axis=0, keepdims=True) * final
            carried = carried + jnp.sum(dend, axis=0, keepdims=True)
            dg = jnp.sum(z - z.T, axis=1, keepdims=True) + dstart * start - dend
            dg = dg + jnp.where(last, carried, 0.0)
            dcol = dcol + jnp.where(lane == h, dbeta, 0.0) + jnp.where(lane == heads + h, dg, 0.0)
            dstate[s, h] = (
                mm((start * q.astype(f32)).astype(bf16), dlow, ((0,), (0,)))
                + final * ds
                - mm(k, wa, ((0,), (0,)))
            )
            dq = rq * (dqn - qn * jnp.sum(dqn * qn, axis=1, keepdims=True))
            dk = rk * (dkn - kn * jnp.sum(dkn * kn, axis=1, keepdims=True))
            for grad, n, buf, part in ((dq, 0, tq, keys), (dk, 1, tk, keys), (w, 2, tv, vals)):
                sig = sigs[n][:, part]
                buf[s, 0:CHUNK, part] = grad * (sig * (1.0 + pres[n][:, part] * (1.0 - sig)))
        dh, dl = split(dcol)
        dl2 = (dcol - dh.astype(f32) - dl.astype(f32)).astype(bf16)
        tail = ((0,), (0,))
        rev = mm(tril, dh, tail) + (mm(tril, dl, tail) + mm(tril, dl2, tail))
        dcols[s] = jnp.where(lane < heads, dcol, rev)
        for buf, src, out, weights, dw in ((tq, bq, dpq, wq, dwq), (tk, bk, dpk, wk, dwk), (tv, bv, dpv, wv, dwv)):
            pre = buf[s, 0:CHUNK, :]
            total = weights[0:1] * pre
            dw[0:1, :] += jnp.sum(pre * src[s, 8 : 8 + CHUNK, :], axis=0, keepdims=True)
            for j in range(1, CONV):
                total = total + weights[j : j + 1] * buf[s, j : j + CHUNK, :] * ahead[j - 1]
                dw[j : j + 1, :] += jnp.sum(
                    pre * masks[j - 1] * src[s, 8 - j : 8 - j + CHUNK, :], axis=0, keepdims=True
                )
            out[s] = total.astype(bf16)
            buf[s, CHUNK : CHUNK + 8, :] = buf[s, 0:8, :]


def whole(shape):
    return pl.BlockSpec(shape, lambda c: (0,) * len(shape))


def mixer_forward(pq, pk, pv, pg, cols, rows, wq, wk, wv, gain):
    seqs = pq.shape[0]
    heads = pq.shape[2] // DK
    steps = SEQ // CHUNK
    kw, vw = heads * DK, heads * DV

    def tok(width):
        return pl.BlockSpec((seqs, CHUNK, width), lambda c: (0, c, 0))

    return pl.pallas_call(
        functools.partial(forward_kernel, heads, seqs),
        grid=(steps,),
        in_specs=[tok(kw), tok(kw), tok(vw), tok(vw), tok(cols.shape[2]),
                  pl.BlockSpec((seqs, rows.shape[1], CHUNK), lambda c: (0, 0, c)),
                  whole((CONV, kw)), whole((CONV, kw)), whole((CONV, vw)), whole((1, vw))],
        out_specs=[tok(vw),
                   pl.BlockSpec((seqs, heads, CHUNK, CHUNK), lambda c: (0, 0, c, 0)),
                   tok(vw),
                   pl.BlockSpec((1, seqs, heads, DK, DV), lambda c: (c, 0, 0, 0, 0))],
        out_shape=[jax.ShapeDtypeStruct((seqs, SEQ, vw), bf16),
                   jax.ShapeDtypeStruct((seqs, heads, SEQ, CHUNK), bf16),
                   jax.ShapeDtypeStruct((seqs, SEQ, vw), bf16),
                   jax.ShapeDtypeStruct((steps, seqs, heads, DK, DV), f32)],
        scratch_shapes=[pltpu.VMEM((seqs, heads, DK, DV), f32),
                        pltpu.VMEM((seqs, 8 + CHUNK, kw), f32),
                        pltpu.VMEM((seqs, 8 + CHUNK, kw), f32),
                        pltpu.VMEM((seqs, 8 + CHUNK, vw), f32)],
        compiler_params=pltpu.CompilerParams(dimension_semantics=("arbitrary",), vmem_limit_bytes=48 << 20),
        name="mixer_forward",
    )(pq, pk, pv, pg, cols, rows, wq, wk, wv, gain)


def mixer_backward(dgated, pq, pk, pv, pg, cols, rows, inv, upd, states, wq, wk, wv, gain):
    seqs = pq.shape[0]
    heads = pq.shape[2] // DK
    steps = SEQ // CHUNK
    kw, vw = heads * DK, heads * DV

    def tok(width):
        return pl.BlockSpec((seqs, CHUNK, width), lambda c: (0, steps - 1 - c, 0))

    def halo(width):
        return pl.BlockSpec(
            (seqs, 8, width),
            lambda c: (0, jnp.maximum((steps - 1 - c) * (CHUNK // 8) - 1, 0), 0),
        )

    return pl.pallas_call(
        functools.partial(backward_kernel, heads, seqs),
        grid=(steps,),
        in_specs=[tok(vw), tok(kw), tok(kw), tok(vw), tok(vw), halo(kw), halo(kw), halo(vw), tok(cols.shape[2]),
                  pl.BlockSpec((seqs, rows.shape[1], CHUNK), lambda c: (0, 0, steps - 1 - c)),
                  pl.BlockSpec((seqs, heads, CHUNK, CHUNK), lambda c: (0, 0, steps - 1 - c, 0)),
                  tok(vw),
                  pl.BlockSpec((1, seqs, heads, DK, DV), lambda c: (steps - 1 - c, 0, 0, 0, 0)),
                  whole((CONV, kw)), whole((CONV, kw)), whole((CONV, vw)), whole((1, vw))],
        out_specs=[tok(kw), tok(kw), tok(vw), tok(vw), tok(2 * heads),
                   whole((CONV, kw)), whole((CONV, kw)), whole((CONV, vw)), whole((1, vw))],
        out_shape=[jax.ShapeDtypeStruct((seqs, SEQ, kw), bf16),
                   jax.ShapeDtypeStruct((seqs, SEQ, kw), bf16),
                   jax.ShapeDtypeStruct((seqs, SEQ, vw), bf16),
                   jax.ShapeDtypeStruct((seqs, SEQ, vw), bf16),
                   jax.ShapeDtypeStruct((seqs, SEQ, 2 * heads), f32),
                   jax.ShapeDtypeStruct((CONV, kw), f32),
                   jax.ShapeDtypeStruct((CONV, kw), f32),
                   jax.ShapeDtypeStruct((CONV, vw), f32),
                   jax.ShapeDtypeStruct((1, vw), f32)],
        scratch_shapes=[pltpu.VMEM((seqs, heads, DK, DV), f32)]
        + [pltpu.VMEM((seqs, 8 + CHUNK, width), f32) for width in (kw, kw, vw)] * 2,
        compiler_params=pltpu.CompilerParams(dimension_semantics=("arbitrary",), vmem_limit_bytes=56 << 20),
        name="mixer_backward",
    )(dgated, pq, pk, pv, pg, pq, pk, pv, cols, rows, inv, upd, states, wq, wk, wv, gain)


def token_tables(seg_ids, strength, log_decay):
    seqs = seg_ids.shape[0] // SEQ
    seg = seg_ids.reshape(seqs, 1, SEQ)
    position = lax.broadcasted_iota(jnp.int32, (1, 1, SEQ), 2)
    back, ahead = [], []
    for j in range(1, CONV):
        same = seg[:, :, j:] == seg[:, :, : SEQ - j]
        none = jnp.zeros((seqs, 1, j), jnp.bool_)
        back.append(jnp.concatenate([none, same], axis=2))
        ahead.append(jnp.concatenate([same, none], axis=2))
    before = jnp.concatenate([jnp.full((seqs, 1, 1), -1, jnp.int32), seg[:, :, CHUNK - 1 : SEQ - 1 : CHUNK]], axis=2)
    carry = seg == jnp.repeat(before, CHUNK, axis=2)
    heads = strength.shape[0]
    tables = [m.astype(f32) for m in back + ahead] + [seg.astype(f32), carry.astype(f32)]
    tables += [
        jnp.swapaxes(strength.reshape(heads, seqs, SEQ), 0, 1),
        jnp.swapaxes(log_decay.reshape(heads, seqs, SEQ), 0, 1),
    ]
    pad = 16 - 8 - 2 * heads
    if pad:
        tables.append(jnp.zeros((seqs, pad, SEQ), f32))
    rows = jnp.concatenate(tables, axis=1)
    return rows, jnp.swapaxes(rows, 1, 2)


def rows_product(first_op, second_op):
    return lax.dot_general(
        first_op, second_op, (((0,), (0,)), ((), ())), preferred_element_type=f32
    )


def cols_product(first_op, second_op):
    return lax.dot_general(
        first_op, second_op, (((1,), (1,)), ((), ())), preferred_element_type=f32
    )


def shard_norm(values, gains):
    squares = lax.psum(jnp.sum(values * values, axis=1), "col")
    scales = lax.rsqrt(squares / D + EPSILON)
    return (scales, values * scales[:, None] * gains)


def shard_norm_back(values, gains, scales, grad_out):
    weighted = grad_out * gains
    totals = lax.psum(jnp.sum(weighted * values, axis=1), "col")
    grad_values = (
        scales[:, None] * weighted - values * (scales * scales * scales * totals / D)[:, None]
    )
    grad_gains = jnp.sum(grad_out * values * scales[:, None], axis=0)
    return (grad_values, grad_gains)


def gather_cols(values):
    return lax.all_gather(values, "col", axis=1, tiled=True)


def gather_rows(values, axis):
    return lax.all_gather(values, "row", axis=axis, tiled=True)


def sum_columns(term):
    return lax.psum_scatter(
        term.astype(bf16), "col", scatter_dimension=1, tiled=True
    ).astype(f32)


def sum_rows(term, axis):
    return lax.psum_scatter(
        term.astype(bf16), "row", scatter_dimension=axis, tiled=True
    ).astype(f32)


def on_device(
    hidden_in,
    seg_ids,
    cotangent,
    norm_mixer,
    w_query,
    w_key,
    w_value,
    w_gate,
    w_beta,
    w_decay,
    decay_log,
    conv_query,
    conv_key,
    conv_value,
    norm_gated,
    w_out,
    norm_ffn,
    w_ffn_gate,
    w_ffn_up,
    w_ffn_down,
):
    tokens = seg_ids.shape[0]
    seqs = tokens // SEQ
    heads = decay_log.shape[0]

    def by_seq(values):
        return values.reshape(seqs, SEQ, values.shape[1])

    def flat(values):
        return values.reshape(tokens, values.shape[2])

    small_in = gather_rows(jnp.concatenate([w_beta, w_decay], axis=1).T, 1)
    full = [gather_rows(w, 0) for w in (w_query, w_key, w_value, w_gate)]
    full_out = gather_rows(w_out, 1)
    full_gate = gather_rows(w_ffn_gate, 0)
    full_up = gather_rows(w_ffn_up, 0)
    full_down = gather_rows(w_ffn_down, 1)

    hidden = hidden_in.astype(f32)
    scale_mixer, normed_shard = shard_norm(hidden, norm_mixer)
    normed = gather_cols(normed_shard.astype(bf16))
    projected = [by_seq(jnp.dot(normed, w, preferred_element_type=f32)) for w in full]
    proj_small = cols_product(small_in, normed)
    proj_beta, proj_decay = proj_small[:heads], proj_small[heads:]
    strength = jax.nn.sigmoid(proj_beta)
    rate = -jnp.exp(decay_log)[:, None]
    log_decay = rate * jax.nn.softplus(proj_decay)
    rows, cols = token_tables(seg_ids, strength, log_decay)
    gains = norm_gated[None]
    gated, inv, upd, states = mixer_forward(
        *projected, cols, rows, conv_query, conv_key, conv_value, gains
    )
    gated = flat(gated)
    middle = hidden + sum_columns(jnp.dot(gated, full_out, preferred_element_type=f32))
    scale_ffn, normed_mid = shard_norm(middle, norm_ffn)
    normed_ffn = gather_cols(normed_mid.astype(bf16))
    gate_pre = jnp.dot(normed_ffn, full_gate, preferred_element_type=f32)
    up_pre = jnp.dot(normed_ffn, full_up, preferred_element_type=f32)
    sig_gate = jax.nn.sigmoid(gate_pre)
    inner_act = (gate_pre * sig_gate * up_pre).astype(bf16)
    block_out = (
        middle + sum_columns(jnp.dot(inner_act, full_down, preferred_element_type=f32))
    ).astype(bf16)

    grad_top = gather_cols(cotangent)
    grad_inner = cols_product(grad_top, full_down)
    grad_gate = (grad_inner * up_pre * sig_gate * (1.0 + gate_pre * (1.0 - sig_gate))).astype(bf16)
    grad_up = (grad_inner * gate_pre * sig_gate).astype(bf16)
    grad_normed_ffn = sum_columns(
        cols_product(grad_gate, full_gate) + cols_product(grad_up, full_up)
    )
    grad_from_ffn, grad_norm_ffn = shard_norm_back(middle, norm_ffn, scale_ffn, grad_normed_ffn)
    grad_middle = cotangent.astype(f32) + grad_from_ffn
    grad_mid_full = gather_cols(grad_middle.astype(bf16))
    grad_gated = cols_product(grad_mid_full, full_out)
    dpq, dpk, dpv, dpg, dcols, dwq, dwk, dwv, dgain = mixer_backward(
        by_seq(grad_gated), *projected, cols, rows, inv, upd, states,
        conv_query, conv_key, conv_value, gains,
    )
    grad_proj = [flat(g) for g in (dpq, dpk, dpv, dpg)]
    dsmall = flat(dcols).T
    dstrength, dlog = dsmall[:heads], dsmall[heads:]
    grad_small = jnp.concatenate(
        [dstrength * strength * (1.0 - strength), dlog * rate * jax.nn.sigmoid(proj_decay)], axis=0
    ).astype(bf16)
    grad_decay_log = jnp.sum(dlog * log_decay, axis=1)
    term = rows_product(grad_small, small_in)
    for g, w in zip(grad_proj, full):
        term = term + cols_product(g, w)
    grad_normed = sum_columns(term)
    grad_from_mixer, grad_norm_mixer = shard_norm_back(hidden, norm_mixer, scale_mixer, grad_normed)
    grad_input = grad_middle + grad_from_mixer

    in_grads = [sum_rows(rows_product(normed, g), 0) for g in grad_proj]
    small_grads = sum_rows(jnp.dot(grad_small, normed, preferred_element_type=f32), 1).T
    gate_grad = sum_rows(rows_product(normed_ffn, grad_gate), 0)
    up_grad = sum_rows(rows_product(normed_ffn, grad_up), 0)
    out_grad = sum_rows(rows_product(gated, grad_mid_full), 1)
    down_grad = sum_rows(rows_product(inner_act, grad_top), 1)
    small = lax.psum(
        (grad_norm_mixer, grad_norm_ffn, grad_decay_log, dwq, dwk, dwv, dgain[0]), "row"
    )
    return (
        block_out,
        grad_input,
        small[0],
        in_grads[0],
        in_grads[1],
        in_grads[2],
        in_grads[3],
        small_grads[:, :heads],
        small_grads[:, heads:],
        small[2],
        small[3],
        small[4],
        small[5],
        small[6],
        out_grad,
        small[1],
        gate_grad,
        up_grad,
        down_grad,
    )


def solution(mesh):
    placed = (
        P("row", "col"),
        P("row"),
        P("row", "col"),
        P("col"),
        P("row", "col"),
        P("row", "col"),
        P("row", "col"),
        P("row", "col"),
        P("row", "col"),
        P("row", "col"),
        P("col"),
        P(None, "col"),
        P(None, "col"),
        P(None, "col"),
        P("col"),
        P("col", "row"),
        P("col"),
        P("row", "col"),
        P("row", "col"),
        P("col", "row"),
    )
    return jax.shard_map(
        on_device,
        mesh=mesh,
        in_specs=placed,
        out_specs=(
            P("row", "col"),
            P("row", "col"),
            P("col"),
            P("row", "col"),
            P("row", "col"),
            P("row", "col"),
            P("row", "col"),
            P("row", "col"),
            P("row", "col"),
            P("col"),
            P(None, "col"),
            P(None, "col"),
            P(None, "col"),
            P("col"),
            P("col", "row"),
            P("col"),
            P("row", "col"),
            P("row", "col"),
            P("col", "row"),
        ),
        check_vma=False,
    )
```

```python
import functools

import jax
import jax.numpy as jnp
from jax import lax
from jax.experimental import pallas as pl
from jax.experimental.pallas import tpu as pltpu
from jax.sharding import PartitionSpec as P

D = 2048
DK = 128
DV = 256
CONV = 4
SEQ = 1024
CHUNK = 128
EPSILON = 1e-06
SCALE = DK ** (-0.5)
f32 = jnp.float32
bf16 = jnp.bfloat16


def mm(a, b, dims=((1,), (0,))):
    return lax.dot_general(a, b, (dims, ((), ())), preferred_element_type=f32)


def split(a):
    hi = a.astype(bf16)
    return hi, (a - hi.astype(f32)).astype(bf16)


def mm3(a, b):
    ah, al = split(a)
    bh, bl = split(b)
    return mm(ah, bh) + (mm(ah, bl) + mm(al, bh))


def sigmoid(u):
    return 1.0 / (1.0 + jnp.exp(-u))


def iotas(n):
    return (
        lax.broadcasted_iota(jnp.int32, (n, n), 0),
        lax.broadcasted_iota(jnp.int32, (n, n), 1),
    )


def unit_lower_inverse(a, row, col):
    n = a.shape[0]
    eye = (row == col).astype(f32)
    base = 8
    d = jnp.where(row // base == col // base, a, 0.0)
    d2 = mm3(d, d)
    x = eye - d
    x = x + mm3(x, d2)
    d4 = mm3(d2, d2)
    x = x + mm3(x, d4)
    size = base
    while size < n:
        off = jnp.where((row // (2 * size) == col // (2 * size)) & (row // size != col // size), a, 0.0)
        xh = x.astype(bf16)
        x = x - mm(xh, mm(off.astype(bf16), xh).astype(bf16))
        size *= 2
    return x


def conv_taps(buf, s, width, weights, masks):
    pre = weights[0:1] * buf[s, 8 : 8 + CHUNK, :]
    for j in range(1, CONV):
        pre = pre + weights[j : j + 1] * buf[s, 8 - j : 8 - j + CHUNK, :] * masks[j - 1]
    return pre


def forward_kernel(heads, seqs, pq, pk, pv, pg, cols, rows, wq, wk, wv, gain,
                   gated, inv_out, upd_out, state_out, state, bq, bk, bv):
    step = pl.program_id(0)

    @pl.when(step == 0)
    def _():
        state[...] = jnp.zeros_like(state)
        for buf in (bq, bk, bv):
            buf[:, 0:8, :] = jnp.zeros_like(buf[:, 0:8, :])

    row, col = iotas(CHUNK)
    lower = row >= col
    tril = lower.astype(bf16)
    for s in range(seqs):
        cc = cols[s]
        rr = rows[s]
        masks = [cc[:, j : j + 1] for j in range(CONV - 1)]
        ch, cl = split(cc)
        csum = mm(tril, ch) + mm(tril, cl)
        rh, rl = split(rr)
        rsum = mm(rh, tril, ((1,), (1,))) + mm(rl, tril, ((1,), (1,)))
        same = (cc[:, 6:7] == rr[6:7, :]) & lower
        for src, buf in ((pq, bq), (pk, bk), (pv, bv)):
            buf[s, 8 : 8 + CHUNK, :] = src[s]
        cq = conv_taps(bq, s, heads * DK, wq, masks)
        ck = conv_taps(bk, s, heads * DK, wk, masks)
        cv = conv_taps(bv, s, heads * DV, wv, masks)
        for buf in (bq, bk, bv):
            buf[s, 0:8, :] = buf[s, CHUNK : CHUNK + 8, :]
        aq = cq * sigmoid(cq)
        ak = ck * sigmoid(ck)
        av = cv * sigmoid(cv)
        for h in range(heads):
            keys = slice(h * DK, (h + 1) * DK)
            vals = slice(h * DV, (h + 1) * DV)
            q = aq[:, keys]
            q = (q * lax.rsqrt(jnp.sum(q * q, axis=1, keepdims=True) + EPSILON)).astype(bf16)
            k = ak[:, keys]
            k = (k * lax.rsqrt(jnp.sum(k * k, axis=1, keepdims=True) + EPSILON)).astype(bf16)
            v = av[:, vals].astype(bf16).astype(f32)
            beta = cc[:, 8 + h : 9 + h]
            at = 8 + heads + h
            gcol = csum[:, at : at + 1]
            grow = rsum[at : at + 1, :]
            decay = jnp.where(same, jnp.exp(jnp.minimum(gcol - grow, 0.0)), 0.0)
            start = jnp.exp(gcol) * cc[:, 7:8]
            end = jnp.exp(jnp.minimum(gcol[CHUNK - 1 :, :] - gcol, 0.0)) * jnp.where(
                cc[:, 6:7] == cc[CHUNK - 1 :, 6:7], 1.0, 0.0
            )
            kk = mm(k, k, ((1,), (1,)))
            qk = mm(q, k, ((1,), (1,)))
            coupling = jnp.where(row > col, beta * decay * kk, 0.0)
            inv = unit_lower_inverse(coupling, row, col).astype(bf16)
            inv_out[s, h] = inv
            begin = state[s, h]
            state_out[0, s, h] = begin
            low = begin.astype(bf16)
            right = beta * (v - start * mm(k, low))
            upd = mm(inv, right.astype(bf16)).astype(bf16)
            upd_out[s, :, vals] = upd
            mixed = (start * mm(q, low) + mm((decay * qk).astype(bf16), upd)) * SCALE
            kend = (end * k.astype(f32)).astype(bf16)
            state[s, h] = start[CHUNK - 1 :, :] * begin + mm(kend, upd, ((0,), (0,)))
            gate = pg[s, :, vals]
            scaled = mixed * lax.rsqrt(jnp.mean(mixed * mixed, axis=1, keepdims=True) + EPSILON)
            gated[s, :, vals] = (scaled * gain[:, vals] * (gate * sigmoid(gate))).astype(bf16)


def backward_kernel(heads, seqs, dgated, pq, pk, pv, pg, hq, hk, hv, cols, rows, inv_in, upd_in, state_in,
                    wq, wk, wv, gain,
                    dpq, dpk, dpv, dpg, dcols, dwq, dwk, dwv, dgain,
                    dstate, bq, bk, bv, tq, tk, tv):
    step = pl.program_id(0)

    @pl.when(step == 0)
    def _():
        dstate[...] = jnp.zeros_like(dstate)
        for buf in (tq, tk, tv):
            buf[:, CHUNK : CHUNK + 8, :] = jnp.zeros_like(buf[:, CHUNK : CHUNK + 8, :])
        for out in (dwq, dwk, dwv, dgain):
            out[...] = jnp.zeros_like(out)

    row, col = iotas(CHUNK)
    lower = row >= col
    tril = lower.astype(bf16)
    lane = lax.broadcasted_iota(jnp.int32, (CHUNK, 2 * heads + 1), 1)
    last = lax.broadcasted_iota(jnp.int32, (CHUNK, 1), 0) == CHUNK - 1
    for s in range(seqs):
        cc = cols[s]
        rr = rows[s]
        masks = [cc[:, j : j + 1] for j in range(CONV - 1)]
        ahead = [cc[:, 3 + j : 4 + j] for j in range(CONV - 1)]
        ch, cl = split(cc)
        csum = mm(tril, ch) + mm(tril, cl)
        rh, rl = split(rr)
        rsum = mm(rh, tril, ((1,), (1,))) + mm(rl, tril, ((1,), (1,)))
        same = (cc[:, 6:7] == rr[6:7, :]) & lower
        pres = []
        for src, halo, buf, weights in ((pq, hq, bq, wq), (pk, hk, bk, wk), (pv, hv, bv, wv)):
            buf[s, 0:8, :] = halo[s]
            buf[s, 8 : 8 + CHUNK, :] = src[s]
            pres.append(conv_taps(buf, s, None, weights, masks))
        sigs = [sigmoid(pre) for pre in pres]
        acts = [pre * sig for pre, sig in zip(pres, sigs)]
        dcol = jnp.zeros((CHUNK, 2 * heads + 1), f32)
        weigh = jnp.zeros((CHUNK, 1), f32)
        for h in range(heads):
            keys = slice(h * DK, (h + 1) * DK)
            vals = slice(h * DV, (h + 1) * DV)
            q = acts[0][:, keys]
            rq = lax.rsqrt(jnp.sum(q * q, axis=1, keepdims=True) + EPSILON)
            qn = q * rq
            q = qn.astype(bf16)
            k = acts[1][:, keys]
            rk = lax.rsqrt(jnp.sum(k * k, axis=1, keepdims=True) + EPSILON)
            kn = k * rk
            k = kn.astype(bf16)
            v = acts[2][:, vals].astype(bf16).astype(f32)
            beta = cc[:, 8 + h : 9 + h]
            at = 8 + heads + h
            gcol = csum[:, at : at + 1]
            grow = rsum[at : at + 1, :]
            decay = jnp.where(same, jnp.exp(jnp.minimum(gcol - grow, 0.0)), 0.0)
            start = jnp.exp(gcol) * cc[:, 7:8]
            end = jnp.exp(jnp.minimum(gcol[CHUNK - 1 :, :] - gcol, 0.0)) * jnp.where(
                cc[:, 6:7] == cc[CHUNK - 1 :, 6:7], 1.0, 0.0
            )
            kk = mm(k, k, ((1,), (1,)))
            qk = mm(q, k, ((1,), (1,)))
            plain = jnp.where(row > col, decay * kk, 0.0)
            scores = decay * qk
            scores_low = scores.astype(bf16)
            inv = inv_in[s, h]
            upd = upd_in[s, :, vals]
            begin = state_in[0, s, h]
            low = begin.astype(bf16)
            ks = mm(k, low)
            qs = mm(q, low)
            mixed = (start * qs + mm(scores_low, upd)) * SCALE
            gate = pg[s, :, vals]
            sg = sigmoid(gate)
            silu = gate * sg
            rm = lax.rsqrt(jnp.mean(mixed * mixed, axis=1, keepdims=True) + EPSILON)
            scaled = mixed * rm
            dy = dgated[s, :, vals]
            dyn = dy * scaled
            gains = gain[:, vals]
            dgain[:, vals] += jnp.sum(dyn * silu, axis=0, keepdims=True)
            dgate = dyn * gains * (sg * (1.0 + gate * (1.0 - sg)))
            dpg[s, :, vals] = dgate.astype(bf16)
            weigh = weigh + jnp.sum(dgate * gate, axis=1, keepdims=True)
            dscaled = dy * gains * silu
            dmixed = rm * (dscaled - scaled * jnp.mean(dscaled * scaled, axis=1, keepdims=True))
            dout = (dmixed * SCALE)
            dlow = dout.astype(bf16)
            ds = dstate[s, h]
            dsl = ds.astype(bf16)
            kf = k.astype(f32)
            kend = (end * kf).astype(bf16)
            dupd = mm(scores_low, dlow, ((0,), (0,))) + mm(kend, dsl)
            dright = mm(inv, dupd.astype(bf16), ((0,), (0,)))
            drl = dright.astype(bf16)
            dscore = mm(dlow, upd, ((1,), (1,)))
            dcoup = -mm(drl, upd, ((1,), (1,)))
            uds = mm(upd, dsl, ((1,), (1,)))
            w = beta * dright
            wa = (start * w).astype(bf16)
            dsc = (dscore * decay).astype(bf16)
            dqn = start * mm(dlow, low, ((1,), (1,))) + mm(dsc, k)
            g = jnp.where(row > col, beta * dcoup * decay, 0.0)
            dkn = (
                end * uds
                - mm(wa, low, ((1,), (1,)))
                + mm(dsc, q, ((0,), (0,)))
                + mm((g + g.T).astype(bf16), k)
            )
            dbeta = jnp.sum(dright * (v - start * ks), axis=1, keepdims=True) + jnp.sum(
                dcoup * plain, axis=1, keepdims=True
            )
            dstart = jnp.sum(dout * qs - w * ks, axis=1, keepdims=True)
            dend = jnp.sum(kf * uds, axis=1, keepdims=True) * end
            z = dscore * scores + dcoup * (beta * plain)
            final = start[CHUNK - 1 :, :]
            carried = jnp.sum(jnp.sum(ds * begin, axis=1, keepdims=True), axis=0, keepdims=True) * final
            carried = carried + jnp.sum(dend, axis=0, keepdims=True)
            dg = jnp.sum(z - z.T, axis=1, keepdims=True) + dstart * start - dend
            dg = dg + jnp.where(last, carried, 0.0)
            dcol = dcol + jnp.where(lane == h, dbeta, 0.0) + jnp.where(lane == heads + h, dg, 0.0)
            dstate[s, h] = (
                mm((start * q.astype(f32)).astype(bf16), dlow, ((0,), (0,)))
                + final * ds
                - mm(k, wa, ((0,), (0,)))
            )
            dq = rq * (dqn - qn * jnp.sum(dqn * qn, axis=1, keepdims=True))
            dk = rk * (dkn - kn * jnp.sum(dkn * kn, axis=1, keepdims=True))
            for grad, n, buf, part in ((dq, 0, tq, keys), (dk, 1, tk, keys), (w, 2, tv, vals)):
                sig = sigs[n][:, part]
                buf[s, 0:CHUNK, part] = grad * (sig * (1.0 + pres[n][:, part] * (1.0 - sig)))
        dh, dl = split(dcol)
        dl2 = (dcol - dh.astype(f32) - dl.astype(f32)).astype(bf16)
        tail = ((0,), (0,))
        rev = mm(tril, dh, tail) + (mm(tril, dl, tail) + mm(tril, dl2, tail))
        for buf, src, out, weights, dw in ((tq, bq, dpq, wq, dwq), (tk, bk, dpk, wk, dwk), (tv, bv, dpv, wv, dwv)):
            pre = buf[s, 0:CHUNK, :]
            total = weights[0:1] * pre
            dw[0:1, :] += jnp.sum(pre * src[s, 8 : 8 + CHUNK, :], axis=0, keepdims=True)
            for j in range(1, CONV):
                total = total + weights[j : j + 1] * buf[s, j : j + CHUNK, :] * ahead[j - 1]
                dw[j : j + 1, :] += jnp.sum(
                    pre * masks[j - 1] * src[s, 8 - j : 8 - j + CHUNK, :], axis=0, keepdims=True
                )
            out[s] = total.astype(bf16)
            weigh = weigh + jnp.sum(total * src[s, 8 : 8 + CHUNK, :], axis=1, keepdims=True)
            buf[s, CHUNK : CHUNK + 8, :] = buf[s, 0:8, :]
        dcols[s] = jnp.where(lane < heads, dcol, jnp.where(lane < 2 * heads, rev, weigh))


def whole(shape):
    return pl.BlockSpec(shape, lambda c: (0,) * len(shape))


def mixer_forward(pq, pk, pv, pg, cols, rows, wq, wk, wv, gain):
    seqs = pq.shape[0]
    heads = pq.shape[2] // DK
    steps = SEQ // CHUNK
    kw, vw = heads * DK, heads * DV

    def tok(width):
        return pl.BlockSpec((seqs, CHUNK, width), lambda c: (0, c, 0))

    return pl.pallas_call(
        functools.partial(forward_kernel, heads, seqs),
        grid=(steps,),
        in_specs=[tok(kw), tok(kw), tok(vw), tok(vw), tok(cols.shape[2]),
                  pl.BlockSpec((seqs, rows.shape[1], CHUNK), lambda c: (0, 0, c)),
                  whole((CONV, kw)), whole((CONV, kw)), whole((CONV, vw)), whole((1, vw))],
        out_specs=[tok(vw),
                   pl.BlockSpec((seqs, heads, CHUNK, CHUNK), lambda c: (0, 0, c, 0)),
                   tok(vw),
                   pl.BlockSpec((1, seqs, heads, DK, DV), lambda c: (c, 0, 0, 0, 0))],
        out_shape=[jax.ShapeDtypeStruct((seqs, SEQ, vw), bf16),
                   jax.ShapeDtypeStruct((seqs, heads, SEQ, CHUNK), bf16),
                   jax.ShapeDtypeStruct((seqs, SEQ, vw), bf16),
                   jax.ShapeDtypeStruct((steps, seqs, heads, DK, DV), f32)],
        scratch_shapes=[pltpu.VMEM((seqs, heads, DK, DV), f32),
                        pltpu.VMEM((seqs, 8 + CHUNK, kw), f32),
                        pltpu.VMEM((seqs, 8 + CHUNK, kw), f32),
                        pltpu.VMEM((seqs, 8 + CHUNK, vw), f32)],
        compiler_params=pltpu.CompilerParams(dimension_semantics=("arbitrary",), vmem_limit_bytes=48 << 20),
        name="mixer_forward",
    )(pq, pk, pv, pg, cols, rows, wq, wk, wv, gain)


def mixer_backward(dgated, pq, pk, pv, pg, cols, rows, inv, upd, states, wq, wk, wv, gain):
    seqs = pq.shape[0]
    heads = pq.shape[2] // DK
    steps = SEQ // CHUNK
    kw, vw = heads * DK, heads * DV

    def tok(width):
        return pl.BlockSpec((seqs, CHUNK, width), lambda c: (0, steps - 1 - c, 0))

    def halo(width):
        return pl.BlockSpec(
            (seqs, 8, width),
            lambda c: (0, jnp.maximum((steps - 1 - c) * (CHUNK // 8) - 1, 0), 0),
        )

    return pl.pallas_call(
        functools.partial(backward_kernel, heads, seqs),
        grid=(steps,),
        in_specs=[tok(vw), tok(kw), tok(kw), tok(vw), tok(vw), halo(kw), halo(kw), halo(vw), tok(cols.shape[2]),
                  pl.BlockSpec((seqs, rows.shape[1], CHUNK), lambda c: (0, 0, steps - 1 - c)),
                  pl.BlockSpec((seqs, heads, CHUNK, CHUNK), lambda c: (0, 0, steps - 1 - c, 0)),
                  tok(vw),
                  pl.BlockSpec((1, seqs, heads, DK, DV), lambda c: (steps - 1 - c, 0, 0, 0, 0)),
                  whole((CONV, kw)), whole((CONV, kw)), whole((CONV, vw)), whole((1, vw))],
        out_specs=[tok(kw), tok(kw), tok(vw), tok(vw), tok(2 * heads + 1),
                   whole((CONV, kw)), whole((CONV, kw)), whole((CONV, vw)), whole((1, vw))],
        out_shape=[jax.ShapeDtypeStruct((seqs, SEQ, kw), bf16),
                   jax.ShapeDtypeStruct((seqs, SEQ, kw), bf16),
                   jax.ShapeDtypeStruct((seqs, SEQ, vw), bf16),
                   jax.ShapeDtypeStruct((seqs, SEQ, vw), bf16),
                   jax.ShapeDtypeStruct((seqs, SEQ, 2 * heads + 1), f32),
                   jax.ShapeDtypeStruct((CONV, kw), f32),
                   jax.ShapeDtypeStruct((CONV, kw), f32),
                   jax.ShapeDtypeStruct((CONV, vw), f32),
                   jax.ShapeDtypeStruct((1, vw), f32)],
        scratch_shapes=[pltpu.VMEM((seqs, heads, DK, DV), f32)]
        + [pltpu.VMEM((seqs, 8 + CHUNK, width), f32) for width in (kw, kw, vw)] * 2,
        compiler_params=pltpu.CompilerParams(dimension_semantics=("arbitrary",), vmem_limit_bytes=56 << 20),
        name="mixer_backward",
    )(dgated, pq, pk, pv, pg, pq, pk, pv, cols, rows, inv, upd, states, wq, wk, wv, gain)


def token_tables(seg_ids, strength, log_decay):
    seqs = seg_ids.shape[0] // SEQ
    seg = seg_ids.reshape(seqs, 1, SEQ)
    position = lax.broadcasted_iota(jnp.int32, (1, 1, SEQ), 2)
    back, ahead = [], []
    for j in range(1, CONV):
        same = seg[:, :, j:] == seg[:, :, : SEQ - j]
        none = jnp.zeros((seqs, 1, j), jnp.bool_)
        back.append(jnp.concatenate([none, same], axis=2))
        ahead.append(jnp.concatenate([same, none], axis=2))
    before = jnp.concatenate([jnp.full((seqs, 1, 1), -1, jnp.int32), seg[:, :, CHUNK - 1 : SEQ - 1 : CHUNK]], axis=2)
    carry = seg == jnp.repeat(before, CHUNK, axis=2)
    heads = strength.shape[0]
    tables = [m.astype(f32) for m in back + ahead] + [seg.astype(f32), carry.astype(f32)]
    tables += [
        jnp.swapaxes(strength.reshape(heads, seqs, SEQ), 0, 1),
        jnp.swapaxes(log_decay.reshape(heads, seqs, SEQ), 0, 1),
    ]
    pad = 16 - 8 - 2 * heads
    if pad:
        tables.append(jnp.zeros((seqs, pad, SEQ), f32))
    rows = jnp.concatenate(tables, axis=1)
    return rows, jnp.swapaxes(rows, 1, 2)

TILE = 256
MESH = pl.DeviceIdType.MESH


def flip(value, bits):
    bit = 1
    while bit <= bits:
        if bits & bit:
            value = value + bit - 2 * bit * ((value // bit) % 2)
        bit *= 2
    return value


class Grid:
    def __init__(self):
        self.rows = lax.axis_size("row")
        self.cols = lax.axis_size("col")
        self.shard = D // self.rows
        self.block = D // self.cols
        self.parts = self.cols // self.rows
        self.half = self.cols // 2
        self.me = lax.axis_index("col")
        self.at = lax.axis_index("row")
        self.ids = jnp.stack([self.me, self.at]).astype(jnp.int32)
        self.slots = list(range(0, self.cols, 2)) + list(range(1, self.cols, 2))

    def swap(self, values, axis, bits):
        count = self.rows if axis == "row" else self.cols
        return lax.ppermute(values, axis, [(i, i ^ bits) for i in range(count)])

    def total(self, values, axis):
        bits = 1
        while bits < (self.rows if axis == "row" else self.cols):
            values = values + self.swap(values, axis, bits)
            bits *= 2
        return values

    def gather_cols(self, values):
        same = [values] + [self.swap(values, "col", k) for k in range(2, self.cols, 2)]
        return same + [self.swap(v, "col", 1) for v in same]

    def gather_rows(self, values):
        return lax.all_gather(values, "row", axis=0, tiled=True)

    def sum_rows(self, term, axis):
        return lax.psum_scatter(term.astype(bf16), "row", scatter_dimension=axis, tiled=True).astype(f32)


def fixed(array):
    return pl.BlockSpec(array.shape, lambda i, ids: (0,) * array.ndim, pipeline_mode=pl.Buffered(1))


def tokens_of(width, tile=TILE):
    return pl.BlockSpec((tile, width), lambda i, ids: (i, 0))


def cost(flops, operands, outs):
    moved = sum(o.size * o.dtype.itemsize for o in operands)
    moved += sum(o.size * o.dtype.itemsize for o in outs)
    return pl.CostEstimate(flops=flops, bytes_accessed=moved, transcendentals=0)


def launch(kernel, grid, ids, operands, in_specs, out_specs, out_shape, scratch, name, flops):
    return pl.pallas_call(
        kernel,
        grid_spec=pltpu.PrefetchScalarGridSpec(
            num_scalar_prefetch=1, grid=grid, in_specs=in_specs, out_specs=out_specs, scratch_shapes=scratch
        ),
        out_shape=out_shape,
        compiler_params=pltpu.CompilerParams(
            dimension_semantics=("arbitrary",) * len(grid), vmem_limit_bytes=56 << 20
        ),
        cost_estimate=cost(flops, operands, out_shape),
        name=name,
    )(ids, *operands)


def place(g, ids, k):
    return pl.multiple_of((ids[0] ^ k) * g.block, g.block)


def dot_back(g, x, weights):
    return sum(
        mm(x[:, s * g.shard : (s + 1) * g.shard], weights[s], ((1,), (1,))) for s in range(g.rows)
    )


def project_kernel(g, widths, ids, *refs):
    blocks, refs = refs[: g.cols], refs[g.cols :]
    gain, weight, small_weight, normed, scale, pq, pk, pv, pg, small = refs
    values = [b[...].astype(f32) for b in blocks]
    squares = sum(jnp.sum(v * v, axis=1, keepdims=True) for v in values)
    scales = lax.rsqrt(squares / D + EPSILON)
    scale[...] = scales
    for k, v in zip(g.slots, values):
        at = place(g, ids, k)
        normed[:, pl.ds(at, g.block)] = (v * scales * gain[:, pl.ds(at, g.block)]).astype(bf16)
    x = normed[...]
    at = 0
    for out, width in zip((pq, pk, pv, pg), widths):
        out[...] = mm(x, weight[:, at : at + width])
        at += width
    small[...] = mm(small_weight[...], x, ((1,), (1,)))


def project(g, blocks, gains, weight, small_weight, widths):
    tokens = blocks[0].shape[0]
    few = small_weight.shape[0]
    return launch(
        functools.partial(project_kernel, g, widths),
        (tokens // TILE,),
        g.ids,
        blocks + [gains, weight, small_weight],
        [tokens_of(g.block)] * g.cols + [fixed(gains), fixed(weight), fixed(small_weight)],
        [tokens_of(D), tokens_of(1)] + [tokens_of(w) for w in widths] + [pl.BlockSpec((few, TILE), lambda i, ids: (0, i))],
        [jax.ShapeDtypeStruct((tokens, D), bf16), jax.ShapeDtypeStruct((tokens, 1), f32)]
        + [jax.ShapeDtypeStruct((tokens, w), f32) for w in widths]
        + [jax.ShapeDtypeStruct((few, tokens), f32)],
        [],
        "project",
        2 * tokens * D * (sum(widths) + few),
    )


def ffn_kernel(g, ids, *refs):
    xs, refs = refs[0], refs[1:]
    ts, refs = refs[: g.cols], refs[g.cols :]
    undo, wg, wu, wd, xr, tr, inner, dgate, dup, total, scale = refs
    squares = 0.0
    for k, t in zip(g.slots, ts):
        at = place(g, ids, k)
        x = xs[k]
        xr[:, pl.ds(at, g.block)] = x
        tr[:, pl.ds(at, g.block)] = t[...]
        v = x.astype(f32)
        squares = squares + jnp.sum(v * v * undo[:, pl.ds(at, g.block)], axis=1, keepdims=True)
    scales = lax.rsqrt(squares / D + EPSILON)
    scale[...] = scales
    x = xr[...]
    gate = mm(x, wg[...]) * scales
    up = mm(x, wu[...]) * scales
    grad = dot_back(g, tr, wd)
    sig = sigmoid(gate)
    silu = gate * sig
    inner[...] = (silu * up).astype(bf16)
    dg = grad * up * (sig * (1.0 + gate * (1.0 - sig)))
    du = grad * silu
    total[...] = jnp.sum(dg * gate + du * up, axis=1, keepdims=True)
    dgate[...] = (dg * scales).astype(bf16)
    dup[...] = (du * scales).astype(bf16)


def ffn(g, xs, ts, undo, wg, wu, wd):
    tokens = xs.shape[1]
    width = wg.shape[1]
    return launch(
        functools.partial(ffn_kernel, g),
        (tokens // TILE,),
        g.ids,
        [xs] + ts + [undo, wg, wu, wd],
        [pl.BlockSpec((g.cols, TILE, g.block), lambda i, ids: (0, i, 0))]
        + [tokens_of(g.block)] * g.cols
        + [fixed(w) for w in (undo, wg, wu, wd)],
        [tokens_of(D)] * 2 + [tokens_of(width)] * 3 + [tokens_of(1)] * 2,
        [jax.ShapeDtypeStruct((tokens, D), bf16)] * 2
        + [jax.ShapeDtypeStruct((tokens, width), bf16)] * 3
        + [jax.ShapeDtypeStruct((tokens, 1), f32)] * 2,
        [],
        "ffn",
        6 * tokens * D * width,
    )


def back_gate_kernel(g, ids, ms, wo, mr, out):
    for k in g.slots:
        mr[:, pl.ds(place(g, ids, k), g.block)] = ms[k]
    out[...] = dot_back(g, mr, wo)


def back_gate(g, ms, wo):
    tokens = ms.shape[1]
    width = wo.shape[1]
    return launch(
        functools.partial(back_gate_kernel, g),
        (tokens // TILE,),
        g.ids,
        [ms, wo],
        [pl.BlockSpec((g.cols, TILE, g.block), lambda i, ids: (0, i, 0)), fixed(wo)],
        [tokens_of(D), tokens_of(width)],
        [jax.ShapeDtypeStruct((tokens, D), bf16), jax.ShapeDtypeStruct((tokens, width), f32)],
        [],
        "back_gate",
        2 * tokens * D * width,
    )


class Sizes:
    def __init__(self, cols, block, parts, shard):
        self.cols, self.block, self.parts, self.shard = cols, block, parts, shard
        self.half = cols // 2


def piece(z, kind, y, weight, owner):
    if kind == "rows":
        return mm(y, weight[pl.ds(pl.multiple_of(owner * z.block, z.block), z.block), :], ((1,), (1,)))
    part = pl.multiple_of((owner % z.parts) * z.block, z.block)
    return mm(y, weight[owner // z.parts, :, pl.ds(part, z.block)])


def exchange_kernel(z, kinds, finish, gathers, extras, outs, steps, tile, *refs):
    count = len(kinds)
    ys, refs = refs[:count], refs[count:]
    ws, refs = refs[:count], refs[count:]
    extra, refs = refs[:extras], refs[extras:]
    out, refs = refs[:outs], refs[outs:]
    if gathers:
        slots, refs = refs[0], refs[1:]
    near, far, far_got, pair, pair_got, refs = *refs[:5], refs[5:]
    far_s, far_r, pair_s, pair_r, refs = *refs[:4], refs[4:]
    if gathers:
        block, own_s, same_s, same_r, turn_s, turn_r, part_s, part_r = refs
    me = lax.axis_index("col")
    partner = flip(me, 1)
    peers = [flip(me, 2 * j) for j in range(1, z.half)]

    barrier = pltpu.get_barrier_semaphore()
    for device in [partner] + peers:
        pl.semaphore_signal(barrier, inc=1, device_id={"col": device}, device_id_type=MESH)
    pl.semaphore_wait(barrier, z.half)

    def remote(source, target, send, receive, device):
        return pltpu.make_async_remote_copy(
            src_ref=source, dst_ref=target, send_sem=send, recv_sem=receive,
            device_id={"col": device}, device_id_type=MESH,
        )

    def rows_at(i):
        return pl.ds(pl.multiple_of(i * tile, tile), tile)

    def send_far(i):
        return remote(far.at[i], far_got.at[i], far_s.at[i], far_r.at[i], partner)

    def send_pair(i, j):
        return remote(pair.at[i, j], pair_got.at[i, j], pair_s.at[i, j], pair_r.at[i, j], peers[j - 1])

    def keep(i):
        return pltpu.make_async_copy(block.at[i], slots.at[0, rows_at(i), :], own_s.at[i])

    def send_part(i):
        return remote(block.at[i], slots.at[1, rows_at(i), :], part_s.at[i], part_r.at[i], partner)

    def send_same(i, j):
        return remote(block.at[i], slots.at[2 * j, rows_at(i), :], same_s.at[i, j], same_r.at[i, j], peers[j - 1])

    def send_turn(i, j):
        return remote(
            slots.at[2 * j, rows_at(i), :], slots.at[2 * j + 1, rows_at(i), :],
            turn_s.at[i, j], turn_r.at[i, j], partner,
        )

    lag = 4 if gathers else 3

    @pl.loop(0, steps + lag - 1)
    def _(it):
        @pl.when(it < steps)
        def _():
            tiles = [y[rows_at(it), :] for y in ys]
            for side, held in ((1, far), (0, near)):
                for j in range(z.half):
                    owner = flip(me, 2 * j + side)
                    total = sum(piece(z, kind, y, w, owner) for kind, y, w in zip(kinds, tiles, ws))
                    held[it, j] = total.astype(bf16)
                if side == 1:
                    send_far(it).start()

        @pl.when((it >= 1) & (it < steps + 1))
        def _():
            i = it - 1
            send_far(i).wait_recv()
            for j in range(1, z.half):
                pair[i, j] = (near[i, j].astype(f32) + far_got[i, j].astype(f32)).astype(bf16)
                send_pair(i, j).start()

        @pl.when((it >= 2) & (it < steps + 2))
        def _():
            i = it - 2
            total = near[i, 0].astype(f32) + far_got[i, 0].astype(f32)
            for j in range(1, z.half):
                send_pair(i, j).wait_recv()
                total = total + pair_got[i, j].astype(f32)
            result = finish(rows_at(i), i, total, extra, out)
            if gathers:
                block[i] = result
                for j in range(1, z.half):
                    send_same(i, j).start()
                send_part(i).start()
                keep(i).start()

        if gathers:
            @pl.when(it >= 3)
            def _():
                i = it - 3
                for j in range(1, z.half):
                    send_same(i, j).wait_recv()
                    send_turn(i, j).start()

    @pl.loop(0, steps)
    def _(i):
        send_far(i).wait_send()
        for j in range(1, z.half):
            send_pair(i, j).wait_send()
        if gathers:
            keep(i).wait()
            send_part(i).wait()
            for j in range(1, z.half):
                send_same(i, j).wait_send()
                send_turn(i, j).wait()


def finish_middle(rows, i, total, extra, out):
    hidden, gain = extra
    middle = hidden[rows, :].astype(f32) + total
    out[0][rows, :] = middle
    return (middle * gain[...]).astype(bf16)


def finish_gradient(rows, i, total, extra, out):
    top, middle, gain, weigh = extra
    before = middle[rows, :]
    grad = top[rows, :].astype(f32) + gain[...] * total - before * weigh[rows, :]
    out[0][rows, :] = grad
    out[1][i] = jnp.sum(total * before, axis=0, keepdims=True)
    return grad.astype(bf16)


def finish_input(rows, i, total, extra, out):
    above, hidden, gain, scale, weigh = extra
    before = hidden[rows, :].astype(f32)
    scaled = scale[rows, :] * total
    out[0][rows, :] = above[rows, :] + gain[...] * scaled - before * weigh[rows, :]
    out[1][i] = jnp.sum(scaled * before, axis=0, keepdims=True)


def finish_out(rows, i, total, extra, out):
    (middle,) = extra
    out[0][rows, :] = (middle[rows, :] + total).astype(bf16)


def exchange(z, kinds, ys, ws, finish, extras, outs, gathers, number, tile=TILE):
    tokens = ys[0].shape[0]
    steps = tokens // tile
    half, block = z.half, z.block
    vmem = pl.BlockSpec(memory_space=pltpu.VMEM)
    shapes = list(outs)
    specs = [vmem] * len(outs)
    wide = (steps, half, tile, block)
    dma = pltpu.SemaphoreType.DMA
    scratch = [pltpu.VMEM(wide, bf16)] * 5
    scratch += [dma((steps,))] * 2 + [dma((steps, half))] * 2
    if gathers:
        shapes.append(jax.ShapeDtypeStruct((z.cols, tokens, block), bf16))
        specs.append(pl.BlockSpec(memory_space=pl.ANY))
        scratch += [pltpu.VMEM((steps, tile, block), bf16), dma((steps,))]
        scratch += [dma((steps, half))] * 4 + [dma((steps,))] * 2
    operands = [*ys, *ws, *extras]
    depth = sum(y.shape[1] for y in ys)
    return pl.pallas_call(
        functools.partial(exchange_kernel, z, kinds, finish, gathers, len(extras), len(outs), steps, tile),
        in_specs=[vmem] * len(operands),
        out_specs=specs,
        out_shape=shapes,
        scratch_shapes=scratch,
        compiler_params=pltpu.CompilerParams(
            collective_id=number, has_side_effects=True, vmem_limit_bytes=58 << 20
        ),
        cost_estimate=cost(2 * tokens * z.cols * block * depth + 50 * 10**9, operands, shapes),
        name="exchange",
    )(*operands)


def rows_product(first_op, second_op):
    return lax.dot_general(
        first_op, second_op, (((0,), (0,)), ((), ())), preferred_element_type=f32
    )


def on_device(
    hidden_in,
    seg_ids,
    cotangent,
    norm_mixer,
    w_query,
    w_key,
    w_value,
    w_gate,
    w_beta,
    w_decay,
    decay_log,
    conv_query,
    conv_key,
    conv_value,
    norm_gated,
    w_out,
    norm_ffn,
    w_ffn_gate,
    w_ffn_up,
    w_ffn_down,
):
    g = Grid()
    z = Sizes(g.cols, g.block, g.parts, g.shard)
    tokens = seg_ids.shape[0]
    seqs = tokens // SEQ
    heads = decay_log.shape[0]
    local = jax.ShapeDtypeStruct((tokens, g.block), f32)
    sums = jax.ShapeDtypeStruct((tokens // TILE, 1, g.block), f32)

    def by_seq(values):
        return values.reshape(seqs, SEQ, values.shape[1])

    def flat(values):
        return values.reshape(tokens, values.shape[2])

    ins = (w_query, w_key, w_value, w_gate)
    widths = [w.shape[1] for w in ins]
    inw = g.gather_rows(jnp.concatenate(ins, axis=1))
    ow = g.gather_rows(w_out[None])
    ew, uw = g.gather_rows(w_ffn_gate), g.gather_rows(w_ffn_up)
    dw = g.gather_rows(w_ffn_down[None])
    few = 2 * heads
    small_own = jnp.concatenate([w_beta, w_decay], axis=1).T
    small_in = g.total(
        lax.dynamic_update_slice(jnp.zeros((few, D), bf16), small_own, (0, g.at * g.shard)), "row"
    )
    gains = jnp.zeros((2, D), f32)
    gains = lax.dynamic_update_slice(gains, jnp.stack([norm_mixer, norm_ffn]), (0, g.me * g.block))
    gains = g.total(gains, "col")
    blocks = g.gather_cols(hidden_in)
    tops = g.gather_cols(cotangent)

    normed, scale_mixer, pq, pk, pv, pg, proj_small = project(g, blocks, gains[:1], inw, small_in, widths)
    projected = [by_seq(p) for p in (pq, pk, pv, pg)]
    proj_beta, proj_decay = proj_small[:heads], proj_small[heads:]
    strength = jax.nn.sigmoid(proj_beta)
    rate = -jnp.exp(decay_log)[:, None]
    log_decay = rate * jax.nn.softplus(proj_decay)
    rows, cols = token_tables(seg_ids, strength, log_decay)
    gain_gated = norm_gated[None]
    gated, inv, upd, states = mixer_forward(
        *projected, cols, rows, conv_query, conv_key, conv_value, gain_gated
    )
    gated = flat(gated)
    middle, mids = exchange(
        z, ("cols",), [gated], [ow], finish_middle, [hidden_in, norm_ffn[None]], [local], True, 0
    )
    undo = 1.0 / (gains[1:] * gains[1:])
    xr, tr, inner, dgate, dup, weigh, scale_ffn = ffn(g, mids, tops, undo, ew, uw, dw)
    gate_grad = g.sum_rows(rows_product(xr, dgate), 0)
    up_grad = g.sum_rows(rows_product(xr, dup), 0)
    down_grad = g.sum_rows(rows_product(inner, tr), 1)
    weigh = scale_ffn * scale_ffn * g.total(weigh[:, 0], "col")[:, None] / D
    grad_middle, norm_sums, downs = exchange(
        z, ("rows", "rows"), [dgate, dup], [ew, uw], finish_gradient,
        [cotangent, middle, norm_ffn[None], weigh], [local, sums], True, 1,
    )
    grad_norm_ffn = jnp.sum(norm_sums, axis=(0, 1))
    mr, grad_gated = back_gate(g, downs, ow)
    out_grad = g.sum_rows(rows_product(gated, mr), 1)
    dpq, dpk, dpv, dpg, dcols, dwq, dwk, dwv, dgain = mixer_backward(
        by_seq(grad_gated), *projected, cols, rows, inv, upd, states,
        conv_query, conv_key, conv_value, gain_gated,
    )
    dproj = jnp.concatenate([flat(d) for d in (dpq, dpk, dpv, dpg)], axis=1)
    in_grads = g.sum_rows(rows_product(normed, dproj), 0)
    dsmall = flat(dcols).T
    dstrength, dlog = dsmall[:heads], dsmall[heads:few]
    grad_small = jnp.concatenate(
        [dstrength * strength * (1.0 - strength), dlog * rate * jax.nn.sigmoid(proj_decay)], axis=0
    )
    weigh = g.total(dsmall[few] + jnp.sum(grad_small * proj_small, axis=0), "col")[:, None]
    weigh = scale_mixer * scale_mixer * weigh / D
    grad_small = grad_small.astype(bf16)
    small_grads = jnp.dot(grad_small, normed, preferred_element_type=f32)
    grad_decay_log = jnp.sum(dlog * log_decay, axis=1)
    small_rows = small_in.T
    grad_input, mixer_sums = exchange(
        z, ("rows", "rows"), [dproj, grad_small.T], [inw, small_rows], finish_input,
        [grad_middle, hidden_in, norm_mixer[None], scale_mixer, weigh], [local, sums], False, 2,
    )
    (block_out,) = exchange(
        z, ("cols",), [inner], [dw], finish_out, [middle],
        [jax.ShapeDtypeStruct((tokens, g.block), bf16)], False, 3,
    )
    grad_norm_mixer = jnp.sum(mixer_sums, axis=(0, 1))
    pieces = [dwq, dwk, dwv, dgain, grad_norm_ffn, grad_decay_log, small_grads]
    joined = g.total(jnp.concatenate([p.reshape(-1) for p in pieces]), "row")
    summed, at = [], 0
    for p in pieces:
        summed.append(joined[at : at + p.size].reshape(p.shape))
        at += p.size
    small_grads = lax.dynamic_slice(summed[6], (0, g.at * g.shard), (few, g.shard)).T
    grad_norm_mixer = g.total(grad_norm_mixer, "row")
    grads, at = [], 0
    for w in widths:
        grads.append(in_grads[:, at : at + w])
        at += w
    return (
        block_out,
        grad_input,
        grad_norm_mixer,
        *grads,
        small_grads[:, :heads],
        small_grads[:, heads:],
        summed[5],
        summed[0],
        summed[1],
        summed[2],
        summed[3][0],
        out_grad,
        summed[4],
        gate_grad,
        up_grad,
        down_grad,
    )


def solution(mesh):
    placed = (
        P("row", "col"),
        P("row"),
        P("row", "col"),
        P("col"),
        P("row", "col"),
        P("row", "col"),
        P("row", "col"),
        P("row", "col"),
        P("row", "col"),
        P("row", "col"),
        P("col"),
        P(None, "col"),
        P(None, "col"),
        P(None, "col"),
        P("col"),
        P("col", "row"),
        P("col"),
        P("row", "col"),
        P("row", "col"),
        P("col", "row"),
    )
    return jax.shard_map(
        on_device,
        mesh=mesh,
        in_specs=placed,
        out_specs=(
            P("row", "col"),
            P("row", "col"),
            P("col"),
            P("row", "col"),
            P("row", "col"),
            P("row", "col"),
            P("row", "col"),
            P("row", "col"),
            P("row", "col"),
            P("col"),
            P(None, "col"),
            P(None, "col"),
            P(None, "col"),
            P("col"),
            P("col", "row"),
            P("col"),
            P("row", "col"),
            P("row", "col"),
            P("col", "row"),
        ),
        check_vma=False,
    )
```

```python
import functools

import jax
import jax.numpy as jnp
from jax import lax
from jax.experimental import pallas as pl
from jax.experimental.pallas import tpu as pltpu
from jax.sharding import PartitionSpec as P

D = 2048
DK = 128
DV = 256
CONV = 4
SEQ = 1024
CHUNK = 128
EPSILON = 1e-06
SCALE = DK ** (-0.5)
f32 = jnp.float32
bf16 = jnp.bfloat16


def mm(a, b, dims=((1,), (0,))):
    return lax.dot_general(a, b, (dims, ((), ())), preferred_element_type=f32)


def split(a):
    hi = a.astype(bf16)
    return hi, (a - hi.astype(f32)).astype(bf16)


def mm3(a, b):
    ah, al = split(a)
    bh, bl = split(b)
    return mm(ah, bh) + (mm(ah, bl) + mm(al, bh))


def sigmoid(u):
    return 1.0 / (1.0 + jnp.exp(-u))


def iotas(n):
    return (
        lax.broadcasted_iota(jnp.int32, (n, n), 0),
        lax.broadcasted_iota(jnp.int32, (n, n), 1),
    )


def unit_lower_inverses(many, row, col):
    n = many[0].shape[0]
    eye = (row == col).astype(f32)
    base = 8
    inside = row // base == col // base
    ds = [jnp.where(inside, a, 0.0) for a in many]
    squares = [mm3(d, d) for d in ds]
    xs = [eye - d for d in ds]
    xs = [x + mm3(x, d) for x, d in zip(xs, squares)]
    fourths = [mm3(d, d) for d in squares]
    xs = [x + mm3(x, d) for x, d in zip(xs, fourths)]
    size = base
    while size < n:
        at = (row // (2 * size) == col // (2 * size)) & (row // size != col // size)
        offs = [jnp.where(at, a, 0.0).astype(bf16) for a in many]
        highs = [x.astype(bf16) for x in xs]
        steps = [mm(off, x).astype(bf16) for off, x in zip(offs, highs)]
        xs = [x - mm(h, step) for x, h, step in zip(xs, highs, steps)]
        size *= 2
    return xs


def conv_taps(buf, s, width, weights, masks):
    pre = weights[0:1] * buf[s, 8 : 8 + CHUNK, :]
    for j in range(1, CONV):
        pre = pre + weights[j : j + 1] * buf[s, 8 - j : 8 - j + CHUNK, :] * masks[j - 1]
    return pre


def forward_kernel(heads, seqs, pq, pk, pv, pg, cols, rows, wq, wk, wv, gain,
                   gated, inv_out, upd_out, state_out, state, bq, bk, bv):
    step = pl.program_id(0)

    @pl.when(step == 0)
    def _():
        state[...] = jnp.zeros_like(state)
        for buf in (bq, bk, bv):
            buf[:, 0:8, :] = jnp.zeros_like(buf[:, 0:8, :])

    row, col = iotas(CHUNK)
    lower = row >= col
    tril = lower.astype(bf16)
    chains = []
    for s in range(seqs):
        cc = cols[s]
        rr = rows[s]
        masks = [cc[:, j : j + 1] for j in range(CONV - 1)]
        ch, cl = split(cc)
        csum = mm(tril, ch) + mm(tril, cl)
        rh, rl = split(rr)
        rsum = mm(rh, tril, ((1,), (1,))) + mm(rl, tril, ((1,), (1,)))
        same = (cc[:, 6:7] == rr[6:7, :]) & lower
        for src, buf in ((pq, bq), (pk, bk), (pv, bv)):
            buf[s, 8 : 8 + CHUNK, :] = src[s]
        cq = conv_taps(bq, s, heads * DK, wq, masks)
        ck = conv_taps(bk, s, heads * DK, wk, masks)
        cv = conv_taps(bv, s, heads * DV, wv, masks)
        for buf in (bq, bk, bv):
            buf[s, 0:8, :] = buf[s, CHUNK : CHUNK + 8, :]
        aq = cq * sigmoid(cq)
        ak = ck * sigmoid(ck)
        av = cv * sigmoid(cv)
        for h in range(heads):
            keys = slice(h * DK, (h + 1) * DK)
            vals = slice(h * DV, (h + 1) * DV)
            q = aq[:, keys]
            q = (q * lax.rsqrt(jnp.sum(q * q, axis=1, keepdims=True) + EPSILON)).astype(bf16)
            k = ak[:, keys]
            k = (k * lax.rsqrt(jnp.sum(k * k, axis=1, keepdims=True) + EPSILON)).astype(bf16)
            v = av[:, vals].astype(bf16).astype(f32)
            beta = cc[:, 8 + h : 9 + h]
            at = 8 + heads + h
            gcol = csum[:, at : at + 1]
            grow = rsum[at : at + 1, :]
            decay = jnp.where(same, jnp.exp(jnp.minimum(gcol - grow, 0.0)), 0.0)
            start = jnp.exp(gcol) * cc[:, 7:8]
            end = jnp.exp(jnp.minimum(gcol[CHUNK - 1 :, :] - gcol, 0.0)) * jnp.where(
                cc[:, 6:7] == cc[CHUNK - 1 :, 6:7], 1.0, 0.0
            )
            kk = mm(k, k, ((1,), (1,)))
            scores = (decay * mm(q, k, ((1,), (1,)))).astype(bf16)
            coupling = jnp.where(row > col, beta * decay * kk, 0.0)
            kend = (end * k.astype(f32)).astype(bf16)
            chains.append((s, h, vals, q, k, v, beta, start, scores, kend, coupling))
    inverses = unit_lower_inverses([c[-1] for c in chains], row, col)
    inverses = [x.astype(bf16) for x in inverses]
    begins = [state[c[0], c[1]] for c in chains]
    lows = [x.astype(bf16) for x in begins]
    rights = []
    for (s, h, vals, q, k, v, beta, start, scores, kend, _), inv, begin, low in zip(chains, inverses, begins, lows):
        inv_out[s, h] = inv
        state_out[0, s, h] = begin
        rights.append((beta * (v - start * mm(k, low))).astype(bf16))
    upds = [mm(inv, right).astype(bf16) for inv, right in zip(inverses, rights)]
    for (s, h, vals, q, k, v, beta, start, scores, kend, _), begin, low, upd in zip(chains, begins, lows, upds):
        upd_out[s, :, vals] = upd
        state[s, h] = start[CHUNK - 1 :, :] * begin + mm(kend, upd, ((0,), (0,)))
        mixed = (start * mm(q, low) + mm(scores, upd)) * SCALE
        gate = pg[s, :, vals]
        scaled = mixed * lax.rsqrt(jnp.mean(mixed * mixed, axis=1, keepdims=True) + EPSILON)
        gated[s, :, vals] = (scaled * gain[:, vals] * (gate * sigmoid(gate))).astype(bf16)


def backward_kernel(heads, seqs, dgated, pq, pk, pv, pg, hq, hk, hv, cols, rows, inv_in, upd_in, state_in,
                    wq, wk, wv, gain,
                    dproj, dcols, dwq, dwk, dwv, dgain,
                    dstate, bq, bk, bv, tq, tk, tv):
    step = pl.program_id(0)

    @pl.when(step == 0)
    def _():
        dstate[...] = jnp.zeros_like(dstate)
        for buf in (tq, tk, tv):
            buf[:, CHUNK : CHUNK + 8, :] = jnp.zeros_like(buf[:, CHUNK : CHUNK + 8, :])
        for out in (dwq, dwk, dwv, dgain):
            out[...] = jnp.zeros_like(out)

    row, col = iotas(CHUNK)
    lower = row >= col
    tril = lower.astype(bf16)
    lane = lax.broadcasted_iota(jnp.int32, (CHUNK, 2 * heads + 1), 1)
    last = lax.broadcasted_iota(jnp.int32, (CHUNK, 1), 0) == CHUNK - 1
    shared = []
    for s in range(seqs):
        cc = cols[s]
        rr = rows[s]
        masks = [cc[:, j : j + 1] for j in range(CONV - 1)]
        ch, cl = split(cc)
        csum = mm(tril, ch) + mm(tril, cl)
        rh, rl = split(rr)
        rsum = mm(rh, tril, ((1,), (1,))) + mm(rl, tril, ((1,), (1,)))
        same = (cc[:, 6:7] == rr[6:7, :]) & lower
        pres = []
        for src, halo, buf, weights in ((pq, hq, bq, wq), (pk, hk, bk, wk), (pv, hv, bv, wv)):
            buf[s, 0:8, :] = halo[s]
            buf[s, 8 : 8 + CHUNK, :] = src[s]
            pres.append(conv_taps(buf, s, None, weights, masks))
        sigs = [sigmoid(pre) for pre in pres]
        acts = [pre * sig for pre, sig in zip(pres, sigs)]
        shared.append((cc, masks, csum, rsum, same, pres, sigs, acts))
    found = {}

    def chain(s, h):
        cc, _, csum, rsum, same, pres, sigs, acts = shared[s]
        keys = slice(h * DK, (h + 1) * DK)
        vals = slice(h * DV, (h + 1) * DV)
        q = acts[0][:, keys]
        rq = lax.rsqrt(jnp.sum(q * q, axis=1, keepdims=True) + EPSILON)
        qn = q * rq
        q = qn.astype(bf16)
        k = acts[1][:, keys]
        rk = lax.rsqrt(jnp.sum(k * k, axis=1, keepdims=True) + EPSILON)
        kn = k * rk
        k = kn.astype(bf16)
        v = acts[2][:, vals].astype(bf16).astype(f32)
        beta = cc[:, 8 + h : 9 + h]
        at = 8 + heads + h
        gcol = csum[:, at : at + 1]
        grow = rsum[at : at + 1, :]
        decay = jnp.where(same, jnp.exp(jnp.minimum(gcol - grow, 0.0)), 0.0)
        start = jnp.exp(gcol) * cc[:, 7:8]
        end = jnp.exp(jnp.minimum(gcol[CHUNK - 1 :, :] - gcol, 0.0)) * jnp.where(
            cc[:, 6:7] == cc[CHUNK - 1 :, 6:7], 1.0, 0.0
        )
        begin = state_in[0, s, h]
        low = begin.astype(bf16)
        inv = inv_in[s, h]
        upd = upd_in[s, :, vals]
        ds = dstate[s, h]
        dsl = ds.astype(bf16)
        kf = k.astype(f32)
        kend = (end * kf).astype(bf16)
        kk = mm(k, k, ((1,), (1,)))
        qk = mm(q, k, ((1,), (1,)))
        ks = mm(k, low)
        qs = mm(q, low)
        uds = mm(upd, dsl, ((1,), (1,)))
        kds = mm(kend, dsl)
        yield
        plain = jnp.where(row > col, decay * kk, 0.0)
        scores = decay * qk
        scores_low = scores.astype(bf16)
        mixed = (start * qs + mm(scores_low, upd)) * SCALE
        yield
        gate = pg[s, :, vals]
        sg = sigmoid(gate)
        silu = gate * sg
        rm = lax.rsqrt(jnp.mean(mixed * mixed, axis=1, keepdims=True) + EPSILON)
        scaled = mixed * rm
        dy = dgated[s, :, vals]
        dyn = dy * scaled
        gains = gain[:, vals]
        dgain[:, vals] += jnp.sum(dyn * silu, axis=0, keepdims=True)
        dgate = dyn * gains * (sg * (1.0 + gate * (1.0 - sg)))
        dproj[s, :, 2 * heads * DK + h * DV : 2 * heads * DK + (h + 1) * DV] = dgate.astype(bf16)
        weigh = jnp.sum(dgate * gate, axis=1, keepdims=True)
        dscaled = dy * gains * silu
        dmixed = rm * (dscaled - scaled * jnp.mean(dscaled * scaled, axis=1, keepdims=True))
        dout = dmixed * SCALE
        dlow = dout.astype(bf16)
        dupd = mm(scores_low, dlow, ((0,), (0,))) + kds
        dscore = mm(dlow, upd, ((1,), (1,)))
        dqs = mm(dlow, low, ((1,), (1,)))
        dfirst = mm((start * q.astype(f32)).astype(bf16), dlow, ((0,), (0,)))
        yield
        dright = mm(inv, dupd.astype(bf16), ((0,), (0,)))
        dsc = (dscore * decay).astype(bf16)
        dqn = start * dqs + mm(dsc, k)
        dkn = end * uds + mm(dsc, q, ((0,), (0,)))
        yield
        drl = dright.astype(bf16)
        dcoup = -mm(drl, upd, ((1,), (1,)))
        w = beta * dright
        wa = (start * w).astype(bf16)
        dkn = dkn - mm(wa, low, ((1,), (1,)))
        final = start[CHUNK - 1 :, :]
        dstate[s, h] = dfirst + final * ds - mm(k, wa, ((0,), (0,)))
        yield
        g = jnp.where(row > col, beta * dcoup * decay, 0.0)
        dkn = dkn + mm((g + g.T).astype(bf16), k)
        dbeta = jnp.sum(dright * (v - start * ks), axis=1, keepdims=True) + jnp.sum(
            dcoup * plain, axis=1, keepdims=True
        )
        dstart = jnp.sum(dout * qs - w * ks, axis=1, keepdims=True)
        dend = jnp.sum(kf * uds, axis=1, keepdims=True) * end
        z = dscore * scores + dcoup * (beta * plain)
        carried = jnp.sum(jnp.sum(ds * begin, axis=1, keepdims=True), axis=0, keepdims=True) * final
        carried = carried + jnp.sum(dend, axis=0, keepdims=True)
        dg = jnp.sum(z - z.T, axis=1, keepdims=True) + dstart * start - dend
        dg = dg + jnp.where(last, carried, 0.0)
        found[s, h] = (dbeta, dg, weigh)
        yield
        dq = rq * (dqn - qn * jnp.sum(dqn * qn, axis=1, keepdims=True))
        dk = rk * (dkn - kn * jnp.sum(dkn * kn, axis=1, keepdims=True))
        for grad, n, buf, part in ((dq, 0, tq, keys), (dk, 1, tk, keys), (w, 2, tv, vals)):
            sig = sigs[n][:, part]
            buf[s, 0:CHUNK, part] = grad * (sig * (1.0 + pres[n][:, part] * (1.0 - sig)))

    chains = [chain(s, h) for s in range(seqs) for h in range(heads)]
    while chains:
        chains = [c for c in chains if next(c, chains) is None]

    kw, vw = heads * DK, heads * DV
    for s in range(seqs):
        cc, masks = shared[s][:2]
        ahead = [cc[:, 3 + j : 4 + j] for j in range(CONV - 1)]
        dcol = jnp.zeros((CHUNK, 2 * heads + 1), f32)
        weigh = jnp.zeros((CHUNK, 1), f32)
        for h in range(heads):
            dbeta, dg, more = found[s, h]
            dcol = dcol + jnp.where(lane == h, dbeta, 0.0) + jnp.where(lane == heads + h, dg, 0.0)
            weigh = weigh + more
        dh, dl = split(dcol)
        dl2 = (dcol - dh.astype(f32) - dl.astype(f32)).astype(bf16)
        tail = ((0,), (0,))
        rev = mm(tril, dh, tail) + (mm(tril, dl, tail) + mm(tril, dl2, tail))
        for buf, src, at, weights, dw in ((tq, bq, 0, wq, dwq), (tk, bk, kw, wk, dwk), (tv, bv, 2 * kw + vw, wv, dwv)):
            pre = buf[s, 0:CHUNK, :]
            total = weights[0:1] * pre
            dw[0:1, :] += jnp.sum(pre * src[s, 8 : 8 + CHUNK, :], axis=0, keepdims=True)
            for j in range(1, CONV):
                total = total + weights[j : j + 1] * buf[s, j : j + CHUNK, :] * ahead[j - 1]
                dw[j : j + 1, :] += jnp.sum(
                    pre * masks[j - 1] * src[s, 8 - j : 8 - j + CHUNK, :], axis=0, keepdims=True
                )
            dproj[s, :, at : at + total.shape[1]] = total.astype(bf16)
            weigh = weigh + jnp.sum(total * src[s, 8 : 8 + CHUNK, :], axis=1, keepdims=True)
            buf[s, CHUNK : CHUNK + 8, :] = buf[s, 0:8, :]
        dcols[s] = jnp.where(lane < heads, dcol, jnp.where(lane < 2 * heads, rev, weigh))


def whole(shape):
    return pl.BlockSpec(shape, lambda c: (0,) * len(shape))


def mixer_forward(pq, pk, pv, pg, cols, rows, wq, wk, wv, gain):
    seqs = pq.shape[0]
    heads = pq.shape[2] // DK
    steps = SEQ // CHUNK
    kw, vw = heads * DK, heads * DV

    def tok(width):
        return pl.BlockSpec((seqs, CHUNK, width), lambda c: (0, c, 0))

    return pl.pallas_call(
        functools.partial(forward_kernel, heads, seqs),
        grid=(steps,),
        in_specs=[tok(kw), tok(kw), tok(vw), tok(vw), tok(cols.shape[2]),
                  pl.BlockSpec((seqs, rows.shape[1], CHUNK), lambda c: (0, 0, c)),
                  whole((CONV, kw)), whole((CONV, kw)), whole((CONV, vw)), whole((1, vw))],
        out_specs=[tok(vw),
                   pl.BlockSpec((seqs, heads, CHUNK, CHUNK), lambda c: (0, 0, c, 0)),
                   tok(vw),
                   pl.BlockSpec((1, seqs, heads, DK, DV), lambda c: (c, 0, 0, 0, 0))],
        out_shape=[jax.ShapeDtypeStruct((seqs, SEQ, vw), bf16),
                   jax.ShapeDtypeStruct((seqs, heads, SEQ, CHUNK), bf16),
                   jax.ShapeDtypeStruct((seqs, SEQ, vw), bf16),
                   jax.ShapeDtypeStruct((steps, seqs, heads, DK, DV), f32)],
        scratch_shapes=[pltpu.VMEM((seqs, heads, DK, DV), f32),
                        pltpu.VMEM((seqs, 8 + CHUNK, kw), f32),
                        pltpu.VMEM((seqs, 8 + CHUNK, kw), f32),
                        pltpu.VMEM((seqs, 8 + CHUNK, vw), f32)],
        compiler_params=pltpu.CompilerParams(dimension_semantics=("arbitrary",), vmem_limit_bytes=48 << 20),
        name="mixer_forward",
    )(pq, pk, pv, pg, cols, rows, wq, wk, wv, gain)


def mixer_backward(dgated, pq, pk, pv, pg, cols, rows, inv, upd, states, wq, wk, wv, gain):
    seqs = pq.shape[0]
    heads = pq.shape[2] // DK
    steps = SEQ // CHUNK
    kw, vw = heads * DK, heads * DV

    def tok(width):
        return pl.BlockSpec((seqs, CHUNK, width), lambda c: (0, steps - 1 - c, 0))

    def halo(width):
        return pl.BlockSpec(
            (seqs, 8, width),
            lambda c: (0, jnp.maximum((steps - 1 - c) * (CHUNK // 8) - 1, 0), 0),
        )

    return pl.pallas_call(
        functools.partial(backward_kernel, heads, seqs),
        grid=(steps,),
        in_specs=[tok(vw), tok(kw), tok(kw), tok(vw), tok(vw), halo(kw), halo(kw), halo(vw), tok(cols.shape[2]),
                  pl.BlockSpec((seqs, rows.shape[1], CHUNK), lambda c: (0, 0, steps - 1 - c)),
                  pl.BlockSpec((seqs, heads, CHUNK, CHUNK), lambda c: (0, 0, steps - 1 - c, 0)),
                  tok(vw),
                  pl.BlockSpec((1, seqs, heads, DK, DV), lambda c: (steps - 1 - c, 0, 0, 0, 0)),
                  whole((CONV, kw)), whole((CONV, kw)), whole((CONV, vw)), whole((1, vw))],
        out_specs=[tok(2 * kw + 2 * vw), tok(2 * heads + 1),
                   whole((CONV, kw)), whole((CONV, kw)), whole((CONV, vw)), whole((1, vw))],
        out_shape=[jax.ShapeDtypeStruct((seqs, SEQ, 2 * kw + 2 * vw), bf16),
                   jax.ShapeDtypeStruct((seqs, SEQ, 2 * heads + 1), f32),
                   jax.ShapeDtypeStruct((CONV, kw), f32),
                   jax.ShapeDtypeStruct((CONV, kw), f32),
                   jax.ShapeDtypeStruct((CONV, vw), f32),
                   jax.ShapeDtypeStruct((1, vw), f32)],
        scratch_shapes=[pltpu.VMEM((seqs, heads, DK, DV), f32)]
        + [pltpu.VMEM((seqs, 8 + CHUNK, width), f32) for width in (kw, kw, vw)] * 2,
        compiler_params=pltpu.CompilerParams(dimension_semantics=("arbitrary",), vmem_limit_bytes=56 << 20),
        name="mixer_backward",
    )(dgated, pq, pk, pv, pg, pq, pk, pv, cols, rows, inv, upd, states, wq, wk, wv, gain)


def token_tables(seg_ids, strength, log_decay):
    seqs = seg_ids.shape[0] // SEQ
    seg = seg_ids.reshape(seqs, 1, SEQ)
    position = lax.broadcasted_iota(jnp.int32, (1, 1, SEQ), 2)
    back, ahead = [], []
    for j in range(1, CONV):
        same = seg[:, :, j:] == seg[:, :, : SEQ - j]
        none = jnp.zeros((seqs, 1, j), jnp.bool_)
        back.append(jnp.concatenate([none, same], axis=2))
        ahead.append(jnp.concatenate([same, none], axis=2))
    before = jnp.concatenate([jnp.full((seqs, 1, 1), -1, jnp.int32), seg[:, :, CHUNK - 1 : SEQ - 1 : CHUNK]], axis=2)
    carry = seg == jnp.repeat(before, CHUNK, axis=2)
    heads = strength.shape[0]
    tables = [m.astype(f32) for m in back + ahead] + [seg.astype(f32), carry.astype(f32)]
    tables += [
        jnp.swapaxes(strength.reshape(heads, seqs, SEQ), 0, 1),
        jnp.swapaxes(log_decay.reshape(heads, seqs, SEQ), 0, 1),
    ]
    pad = 16 - 8 - 2 * heads
    if pad:
        tables.append(jnp.zeros((seqs, pad, SEQ), f32))
    rows = jnp.concatenate(tables, axis=1)
    return rows, jnp.swapaxes(rows, 1, 2)

TILE = 256
MESH = pl.DeviceIdType.MESH


def flip(value, bits):
    bit = 1
    while bit <= bits:
        if bits & bit:
            value = value + bit - 2 * bit * ((value // bit) % 2)
        bit *= 2
    return value


class Grid:
    def __init__(self):
        self.rows = lax.axis_size("row")
        self.cols = lax.axis_size("col")
        self.shard = D // self.rows
        self.block = D // self.cols
        self.parts = self.cols // self.rows
        self.half = self.cols // 2
        self.me = lax.axis_index("col")
        self.at = lax.axis_index("row")
        self.ids = jnp.stack([self.me, self.at]).astype(jnp.int32)
        self.slots = list(range(0, self.cols, 2)) + list(range(1, self.cols, 2))

    def swap(self, values, axis, bits):
        count = self.rows if axis == "row" else self.cols
        return lax.ppermute(values, axis, [(i, i ^ bits) for i in range(count)])

    def total(self, values, axis):
        bits = 1
        while bits < (self.rows if axis == "row" else self.cols):
            values = values + self.swap(values, axis, bits)
            bits *= 2
        return values

    def spread(self, values):
        return jnp.stack(
            [values]
            + [
                lax.ppermute(values, "row", [(i, (i + n) % self.rows) for i in range(self.rows)])
                for n in range(1, self.rows)
            ]
        )

    def gather_rows(self, values):
        return lax.all_gather(values, "row", axis=0, tiled=True)

    def sum_rows(self, term, axis):
        return lax.psum_scatter(term, "row", scatter_dimension=axis, tiled=True)


def fixed(array):
    return pl.BlockSpec(array.shape, lambda i, ids: (0,) * array.ndim, pipeline_mode=pl.Buffered(1))


def tokens_of(width, tile=TILE):
    return pl.BlockSpec((tile, width), lambda i, ids: (i, 0))


def slots_of(g):
    return pl.BlockSpec((g.cols, TILE, g.block), lambda i, ids: (0, i, 0))


def cost(flops, operands, outs):
    moved = sum(o.size * o.dtype.itemsize for o in operands)
    moved += sum(o.size * o.dtype.itemsize for o in outs)
    return pl.CostEstimate(flops=flops, bytes_accessed=moved, transcendentals=0)


def launch(kernel, grid, ids, operands, in_specs, out_specs, out_shape, scratch, name, flops):
    return pl.pallas_call(
        kernel,
        grid_spec=pltpu.PrefetchScalarGridSpec(
            num_scalar_prefetch=1, grid=grid, in_specs=in_specs, out_specs=out_specs, scratch_shapes=scratch
        ),
        out_shape=out_shape,
        compiler_params=pltpu.CompilerParams(
            dimension_semantics=("arbitrary",) * len(grid), vmem_limit_bytes=56 << 20
        ),
        cost_estimate=cost(flops, operands, out_shape),
        name=name,
    )(ids, *operands)


def place(g, ids, k):
    return pl.multiple_of((ids[0] ^ k) * g.block, g.block)


def dot_back(g, x, weights):
    return sum(
        mm(x[:, s * g.shard : (s + 1) * g.shard], weights[s], ((1,), (1,))) for s in range(g.rows)
    )


def dot_back_ring(g, ids, x, weights):
    total = 0.0
    for s in range(g.rows):
        shard = lax.rem(ids[1] - s + g.rows, g.rows)
        part = pl.ds(pl.multiple_of(shard * g.shard, g.shard), g.shard)
        total = total + mm(x[:, part], weights[s], ((1,), (1,)))
    return total


def project_kernel(g, widths, few, ids, blocks, gain, weight, ring, normed, scale, pq, pk, pg, pv, small):
    values = [blocks[k].astype(f32) for k in g.slots]
    squares = sum(jnp.sum(v * v, axis=1, keepdims=True) for v in values)
    scales = lax.rsqrt(squares / D + EPSILON)
    scale[...] = scales
    for k, v in zip(g.slots, values):
        at = place(g, ids, k)
        normed[:, pl.ds(at, g.block)] = (v * scales * gain[:, pl.ds(at, g.block)]).astype(bf16)
    x = normed[...]
    at = 0
    for out, width in zip((pq, pk, pg), widths):
        out[...] = mm(x, weight[:, at : at + width])
        at += width
    parts = [x[:, r * g.shard : (r + 1) * g.shard] for r in range(g.rows)]
    pv[...] = sum(mm(p, ring[r, : g.shard, :]) for r, p in enumerate(parts))
    small[...] = sum(
        mm(ring[r, g.shard : g.shard + few, : g.shard], p, ((1,), (1,))) for r, p in enumerate(parts)
    )


def project(g, blocks, gains, weight, ring, widths, few):
    tokens = blocks.shape[1]
    last = ring.shape[2]
    return launch(
        functools.partial(project_kernel, g, widths, few),
        (tokens // TILE,),
        g.ids,
        [blocks, gains, weight, ring],
        [slots_of(g)] + [fixed(w) for w in (gains, weight, ring)],
        [tokens_of(D), tokens_of(1)]
        + [tokens_of(w) for w in widths + [last]]
        + [pl.BlockSpec((few, TILE), lambda i, ids: (0, i))],
        [jax.ShapeDtypeStruct((tokens, D), bf16), jax.ShapeDtypeStruct((tokens, 1), f32)]
        + [jax.ShapeDtypeStruct((tokens, w), f32) for w in widths + [last]]
        + [jax.ShapeDtypeStruct((few, tokens), f32)],
        [],
        "project",
        2 * tokens * D * (sum(widths) + last + few),
    )


def ffn_kernel(g, ids, xs, ts, undo, wg, wu, wd, xr, tr, inner, dgate, dup, total, scale):
    squares = 0.0
    for k in g.slots:
        at = place(g, ids, k)
        x = xs[k]
        xr[:, pl.ds(at, g.block)] = x
        tr[:, pl.ds(at, g.block)] = ts[k]
        v = x.astype(f32)
        squares = squares + jnp.sum(v * v * undo[:, pl.ds(at, g.block)], axis=1, keepdims=True)
    scales = lax.rsqrt(squares / D + EPSILON)
    scale[...] = scales
    x = xr[...]
    gate = mm(x, wg[...]) * scales
    up = mm(x, wu[...]) * scales
    grad = dot_back_ring(g, ids, tr, wd)
    sig = sigmoid(gate)
    silu = gate * sig
    inner[...] = (silu * up).astype(bf16)
    dg = grad * up * (sig * (1.0 + gate * (1.0 - sig)))
    du = grad * silu
    total[...] = jnp.sum(dg * gate + du * up, axis=1, keepdims=True)
    dgate[...] = (dg * scales).astype(bf16)
    dup[...] = (du * scales).astype(bf16)


def ffn(g, xs, ts, undo, wg, wu, wd):
    tokens = xs.shape[1]
    width = wg.shape[1]
    return launch(
        functools.partial(ffn_kernel, g),
        (tokens // TILE,),
        g.ids,
        [xs, ts, undo, wg, wu, wd],
        [slots_of(g)] * 2 + [fixed(w) for w in (undo, wg, wu, wd)],
        [tokens_of(D)] * 2 + [tokens_of(width)] * 3 + [tokens_of(1)] * 2,
        [jax.ShapeDtypeStruct((tokens, D), bf16)] * 2
        + [jax.ShapeDtypeStruct((tokens, width), bf16)] * 3
        + [jax.ShapeDtypeStruct((tokens, 1), f32)] * 2,
        [],
        "ffn",
        6 * tokens * D * width,
    )


def back_gate_kernel(g, ids, ms, wo, mr, out):
    for k in g.slots:
        mr[:, pl.ds(place(g, ids, k), g.block)] = ms[k]
    out[...] = dot_back(g, mr, wo)


def back_gate(g, ms, wo):
    tokens = ms.shape[1]
    width = wo.shape[1]
    return launch(
        functools.partial(back_gate_kernel, g),
        (tokens // TILE,),
        g.ids,
        [ms, wo],
        [slots_of(g), fixed(wo)],
        [tokens_of(D), tokens_of(width)],
        [jax.ShapeDtypeStruct((tokens, D), bf16), jax.ShapeDtypeStruct((tokens, width), f32)],
        [],
        "back_gate",
        2 * tokens * D * width,
    )


class Sizes:
    def __init__(self, g):
        self.rows, self.cols, self.block, self.parts, self.shard, self.half = (
            g.rows, g.cols, g.block, g.parts, g.shard, g.half
        )


def piece(z, kind, y, weight, owner):
    if kind == "rows":
        return mm(y, weight[pl.ds(pl.multiple_of(owner * z.block, z.block), z.block), :], ((1,), (1,)))
    shard = owner // z.parts
    part = pl.ds(pl.multiple_of((owner % z.parts) * z.block, z.block), z.block)
    if kind == "cols":
        return mm(y, weight[shard, :, part])
    if kind == "ring":
        return mm(y, weight[(lax.axis_index("row") - shard + z.rows) % z.rows, :, part])
    if kind == "shards":
        return mm(y, weight[shard, part, :], ((1,), (1,)))
    return mm(y, weight[shard, z.shard : z.shard + y.shape[1], part])


def greet(devices):
    barrier = pltpu.get_barrier_semaphore()
    for axis, index in devices:
        pl.semaphore_signal(barrier, inc=1, device_id={axis: index}, device_id_type=MESH)
    pl.semaphore_wait(barrier, len(devices))


def remote(source, target, send, receive, axis, index):
    return pltpu.make_async_remote_copy(
        src_ref=source, dst_ref=target, send_sem=send, recv_sem=receive,
        device_id={axis: index}, device_id_type=MESH,
    )


class Ride:
    def __init__(self, z, own, whole, keep, send, receive):
        self.z, self.own, self.whole, self.kept, self.send, self.receive = z, own, whole, keep, send, receive
        self.at = lax.axis_index("row")

    def neighbours(self):
        rows = self.z.rows
        return [("row", (self.at + 1) % rows), ("row", (self.at + rows - 1) % rows)]

    def keep(self):
        return pltpu.make_async_copy(self.own, self.whole.at[self.at], self.kept)

    def step(self, n):
        rows = self.z.rows
        shard = (self.at + rows + 1 - n) % rows
        source = self.own if n == 1 else self.whole.at[shard]
        return remote(
            source, self.whole.at[shard], self.send.at[n], self.receive.at[n], "row", (self.at + 1) % rows
        )


class Rider:
    def __init__(self, z, kind, own, given, refs):
        self.z, self.kind, self.own, self.given = z, kind, own, given
        self.at = lax.axis_index("row")
        self.send, self.receive, self.spare = refs

    def step(self, n):
        rows = self.z.rows
        to = (self.at + n) % rows
        if self.kind == "spread":
            source, target = self.own, self.given.at[self.at]
        elif self.kind == "share":
            source = target = self.spare.at[self.at]
        else:
            part = pl.ds(pl.multiple_of(to * self.z.shard, self.z.shard), self.z.shard)
            source = self.own.at[:, part] if self.kind == "deal" else self.own.at[part, :]
            target = self.given.at[n - 1]
        return remote(source, target, self.send.at[n], self.receive.at[n], "row", to)

    def keep(self):
        return pltpu.make_async_copy(self.own, self.given.at[self.at], self.spare)

    def begin(self):
        if self.kind == "share":
            self.spare[self.at] = self.own[...]
        if self.kind == "spread":
            self.keep().start()
        for n in range(1, self.z.rows):
            self.step(n).start()

    def end(self):
        for n in range(1, self.z.rows):
            self.step(n).wait()
        if self.kind == "spread":
            self.keep().wait()
        if self.kind == "share":
            total = self.spare[0]
            for n in range(1, self.z.rows):
                total = total + self.spare[n]
            self.given[...] = total


DEEP = 4


def exchange_kernel(z, plan, steps, tile, *refs):
    groups, arrays, weights, gathers, kinds = plan
    ys, refs = refs[:arrays], refs[arrays:]
    ws, refs = refs[:weights], refs[weights:]
    extras, outs = [], []
    for group in groups:
        extras.append(refs[: group[2]])
        refs = refs[group[2] :]
    own, refs = refs[: len(kinds)], refs[len(kinds) :]
    for group in groups:
        outs.append(refs[: group[3]])
        refs = refs[group[3] :]
    if gathers:
        slots, refs = refs[0], refs[1:]
    given, refs = refs[: len(kinds)], refs[len(kinds) :]
    near, far, far_got, pair_got, refs = *refs[:4], refs[4:]
    far_s, far_r, pair_s, pair_r, refs = *refs[:4], refs[4:]
    if gathers:
        block, own_s, same_s, same_r, turn_s, turn_r, part_s, part_r, refs = *refs[:8], refs[8:]
    me = lax.axis_index("col")
    partner = flip(me, 1)
    peers = [flip(me, 2 * j) for j in range(1, z.half)]
    met = [("col", device) for device in [partner] + peers]
    riders = [
        Rider(z, kind, own[n], given[n], refs[3 * n : 3 * n + 3]) for n, kind in enumerate(kinds)
    ]
    if riders:
        met = met + [("row", (riders[0].at + n) % z.rows) for n in range(1, z.rows)]
    greet(met)

    def rows_at(i):
        return pl.ds(pl.multiple_of(i * tile, tile), tile)

    def send_far(n, i):
        return remote(far.at[n, i % DEEP], far_got.at[n, i], far_s.at[n, i], far_r.at[n, i], "col", partner)

    def send_pair(n, i, j):
        return remote(
            near.at[n, i % DEEP, j], pair_got.at[n, i, j - 1], pair_s.at[n, i, j], pair_r.at[n, i, j],
            "col", peers[j - 1],
        )

    def keep(i):
        return pltpu.make_async_copy(block.at[i], slots.at[0, rows_at(i), :], own_s.at[i])

    def send_part(i):
        return remote(block.at[i], slots.at[1, rows_at(i), :], part_s.at[i], part_r.at[i], "col", partner)

    def send_same(i, j):
        return remote(
            block.at[i], slots.at[2 * j, rows_at(i), :], same_s.at[i, j], same_r.at[i, j], "col", peers[j - 1]
        )

    def send_turn(i, j):
        return remote(
            slots.at[2 * j, rows_at(i), :], slots.at[2 * j + 1, rows_at(i), :],
            turn_s.at[i, j], turn_r.at[i, j], "col", partner,
        )

    def sent(i):
        for n in range(len(groups)):
            send_far(n, i).wait_send()
            for j in range(1, z.half):
                send_pair(n, i, j).wait_send()

    lag = 4 if gathers else 3
    loops = steps + lag - 1
    for rider in riders:
        rider.begin()

    @pl.loop(0, loops)
    def _(it):
        @pl.when((it >= DEEP) & (it < steps))
        def _():
            sent(it - DEEP)

        @pl.when(it < steps)
        def _():
            for n, group in enumerate(groups):
                terms = group[0]
                tiles = [ys[t[1]][rows_at(it), t[2] : t[3]] for t in terms]
                for side, held in ((1, far), (0, near)):
                    for j in range(z.half):
                        owner = flip(me, 2 * j + side)
                        total = sum(piece(z, t[0], y, ws[t[4]], owner) for t, y in zip(terms, tiles))
                        held[n, it % DEEP, j] = total.astype(bf16)
                    if side == 1:
                        send_far(n, it).start()

        @pl.when((it >= 1) & (it < steps + 1))
        def _():
            i = it - 1
            for n in range(len(groups)):
                send_far(n, i).wait_recv()
                for j in range(1, z.half):
                    near[n, i % DEEP, j] = (
                        near[n, i % DEEP, j].astype(f32) + far_got[n, i, j].astype(f32)
                    ).astype(bf16)
                    send_pair(n, i, j).start()

        @pl.when((it >= 2) & (it < steps + 2))
        def _():
            i = it - 2
            for n, group in enumerate(groups):
                total = near[n, i % DEEP, 0].astype(f32) + far_got[n, i, 0].astype(f32)
                for j in range(1, z.half):
                    send_pair(n, i, j).wait_recv()
                    total = total + pair_got[n, i, j - 1].astype(f32)
                result = group[1](rows_at(i), i, total, extras[n], outs[n])
                if gathers and n == 0:
                    block[i] = result
                    for j in range(1, z.half):
                        send_same(i, j).start()
                    send_part(i).start()
                    keep(i).start()

        if gathers:
            @pl.when(it >= 3)
            def _():
                i = it - 3
                for j in range(1, z.half):
                    send_same(i, j).wait_recv()
                    send_turn(i, j).start()

    @pl.loop(max(0, steps - DEEP), steps)
    def _(i):
        sent(i)

    if gathers:
        @pl.loop(0, steps)
        def _(i):
            keep(i).wait()
            send_part(i).wait()
            for j in range(1, z.half):
                send_same(i, j).wait_send()
                send_turn(i, j).wait()

    for rider in riders:
        rider.end()


def finish_middle(rows, i, total, extra, out):
    hidden, gain = extra
    middle = hidden[rows, :].astype(f32) + total
    out[0][rows, :] = middle
    return (middle * gain[...]).astype(bf16)


def finish_gradient(rows, i, total, extra, out):
    top, middle, gain, weigh = extra
    before = middle[rows, :]
    grad = top[rows, :].astype(f32) + gain[...] * total - before * weigh[rows, :]
    out[0][rows, :] = grad
    out[1][i] = jnp.sum(total * before, axis=0, keepdims=True)
    return grad.astype(bf16)


def finish_input(rows, i, total, extra, out):
    above, hidden, gain, scale, weigh = extra
    before = hidden[rows, :].astype(f32)
    scaled = scale[rows, :] * total
    out[0][rows, :] = above[rows, :] + gain[...] * scaled - before * weigh[rows, :]
    out[1][i] = jnp.sum(scaled * before, axis=0, keepdims=True)


def finish_out(rows, i, total, extra, out):
    (middle,) = extra
    out[0][rows, :] = (middle[rows, :] + total).astype(bf16)


def exchange(z, ys, ws, groups, gathers, number, riders=(), tile=TILE):
    tokens = ys[0].shape[0]
    steps = tokens // tile
    half, block, count = z.half, z.block, len(groups)
    vmem = pl.BlockSpec(memory_space=pltpu.VMEM)
    anywhere = pl.BlockSpec(memory_space=pl.ANY)
    dma = pltpu.SemaphoreType.DMA
    operands = [*ys, *ws]
    shapes = []
    for group in groups:
        operands += group[2]
        shapes += group[3]
    in_specs = [vmem] * len(operands)
    specs = [vmem] * len(shapes)
    scratch = [pltpu.VMEM((count, DEEP, half, tile, block), bf16)] * 2
    scratch += [pltpu.VMEM((count, steps, half, tile, block), bf16)]
    scratch += [pltpu.VMEM((count, steps, half - 1, tile, block), bf16)]
    scratch += [dma((count, steps))] * 2 + [dma((count, steps, half))] * 2
    if gathers:
        shapes.append(jax.ShapeDtypeStruct((z.cols, tokens, block), bf16))
        specs.append(anywhere)
        scratch += [pltpu.VMEM((steps, tile, block), bf16), dma((steps,))]
        scratch += [dma((steps, half))] * 4 + [dma((steps,))] * 2
    by_row = dma((z.rows,))
    for kind, own in riders:
        operands.append(own)
        in_specs.append(vmem if kind == "share" else anywhere)
        specs.append(in_specs[-1])
        scratch += [by_row] * 2
        if kind == "spread":
            shapes.append(jax.ShapeDtypeStruct((z.rows,) + own.shape, bf16))
            scratch.append(dma(()))
        elif kind == "share":
            shapes.append(jax.ShapeDtypeStruct(own.shape, f32))
            scratch.append(pltpu.VMEM((z.rows,) + own.shape, f32))
        else:
            part = (own.shape[0], z.shard) if kind == "deal" else (z.shard, own.shape[1])
            shapes.append(jax.ShapeDtypeStruct((z.rows - 1,) + part, bf16))
            scratch.append(dma(()))
    kinds = [(group[0], group[1], len(group[2]), len(group[3])) for group in groups]
    depth = sum(t[3] - t[2] for group in groups for t in group[0])
    return pl.pallas_call(
        functools.partial(
            exchange_kernel, z, (kinds, len(ys), len(ws), gathers, [kind for kind, _ in riders]), steps, tile
        ),
        in_specs=in_specs,
        out_specs=specs,
        out_shape=shapes,
        scratch_shapes=scratch,
        compiler_params=pltpu.CompilerParams(
            collective_id=number, has_side_effects=True, vmem_limit_bytes=60 << 20
        ),
        cost_estimate=cost(2 * tokens * z.cols * block * depth, operands, shapes),
        name="exchange",
    )(*operands)


def begin_kernel(z, count, *refs):
    owns, own, slots, whole = refs[:count], refs[count], refs[count + 1 : 2 * count + 1], refs[2 * count + 1]
    kept, same_s, same_r, part_s, part_r, turn_s, turn_r, keep_s, step_s, step_r = refs[2 * count + 2 :]
    me = lax.axis_index("col")
    partner = flip(me, 1)
    peers = [flip(me, 2 * j) for j in range(1, z.half)]
    ride = Ride(z, own, whole, keep_s, step_s, step_r)
    greet([("col", device) for device in [partner] + peers] + ride.neighbours())

    def keep(n):
        return pltpu.make_async_copy(owns[n], slots[n].at[0], kept.at[n])

    def send_same(n, j):
        return remote(owns[n], slots[n].at[2 * j], same_s.at[n, j], same_r.at[n, j], "col", peers[j - 1])

    def send_part(n):
        return remote(owns[n], slots[n].at[1], part_s.at[n], part_r.at[n], "col", partner)

    def send_turn(n, j):
        return remote(slots[n].at[2 * j], slots[n].at[2 * j + 1], turn_s.at[n, j], turn_r.at[n, j], "col", partner)

    ride.step(1).start()
    ride.keep().start()
    for n in range(count):
        for j in range(1, z.half):
            send_same(n, j).start()
        send_part(n).start()
        keep(n).start()
    for s in range(2, z.rows):
        ride.step(s - 1).wait_recv()
        ride.step(s).start()
    for n in range(count):
        for j in range(1, z.half):
            send_same(n, j).wait_recv()
            send_turn(n, j).start()
    ride.keep().wait()
    ride.step(z.rows - 1).wait_recv()
    for s in range(1, z.rows):
        ride.step(s).wait_send()
    for n in range(count):
        keep(n).wait()
        send_part(n).wait()
        for j in range(1, z.half):
            send_same(n, j).wait_send()
            send_turn(n, j).wait()


def begin(z, owns, own, number):
    anywhere = pl.BlockSpec(memory_space=pl.ANY)
    dma = pltpu.SemaphoreType.DMA
    count = len(owns)
    shapes = [jax.ShapeDtypeStruct((z.cols,) + o.shape, o.dtype) for o in owns]
    shapes.append(jax.ShapeDtypeStruct((z.rows,) + own.shape, own.dtype))
    operands = [*owns, own]
    return pl.pallas_call(
        functools.partial(begin_kernel, z, count),
        in_specs=[anywhere] * len(operands),
        out_specs=[anywhere] * len(shapes),
        out_shape=shapes,
        scratch_shapes=[dma((count,))] + [dma((count, z.half))] * 2 + [dma((count,))] * 2
        + [dma((count, z.half))] * 2 + [dma(())] + [dma((z.rows,))] * 2,
        compiler_params=pltpu.CompilerParams(collective_id=number, has_side_effects=True),
        cost_estimate=cost(10**6, operands, shapes),
        name="begin",
    )(*operands)


def rows_product(first_op, second_op):
    return lax.dot_general(
        first_op, second_op, (((0,), (0,)), ((), ())), preferred_element_type=f32
    )


def on_device(
    hidden_in,
    seg_ids,
    cotangent,
    norm_mixer,
    w_query,
    w_key,
    w_value,
    w_gate,
    w_beta,
    w_decay,
    decay_log,
    conv_query,
    conv_key,
    conv_value,
    norm_gated,
    w_out,
    norm_ffn,
    w_ffn_gate,
    w_ffn_up,
    w_ffn_down,
):
    g = Grid()
    z = Sizes(g)
    tokens = seg_ids.shape[0]
    seqs = tokens // SEQ
    heads = decay_log.shape[0]
    local = jax.ShapeDtypeStruct((tokens, g.block), f32)
    sums = jax.ShapeDtypeStruct((tokens // TILE, 1, g.block), f32)

    def by_seq(values):
        return values.reshape(seqs, SEQ, values.shape[1])

    def flat(values):
        return values.reshape(tokens, values.shape[2])

    few = 2 * heads
    ins = (w_query, w_key, w_gate)
    widths = [w.shape[1] for w in ins]
    inw = g.gather_rows(jnp.concatenate(ins, axis=1))
    wide = max(w_value.shape[1], g.shard)
    value_in = jnp.pad(w_value, ((0, 16), (0, wide - w_value.shape[1])))
    value_in = lax.dynamic_update_slice(
        value_in, jnp.concatenate([w_beta, w_decay], axis=1).T, (g.shard, 0)
    )
    ow = g.gather_rows(w_out[None])
    ew, uw = g.gather_rows(w_ffn_gate), g.gather_rows(w_ffn_up)
    own_gains = jnp.stack([norm_mixer, norm_ffn])
    own_gains = jnp.pad(own_gains, ((0, 6), (0, 0)))
    blocks, tops, gains, vw = begin(z, [hidden_in, cotangent, own_gains], value_in, 3)
    order = jnp.arange(g.cols) ^ g.me
    gains = jnp.swapaxes(jnp.take(gains[:, :2], order, axis=0), 0, 1).reshape(2, D)

    normed, scale_mixer, pq, pk, pg, pv, proj_small = project(g, blocks, gains[:1], inw, vw, widths, few)
    down_own, _ = lax.optimization_barrier((w_ffn_down, proj_small))
    dw = g.spread(down_own)
    projected = [by_seq(p) for p in (pq, pk, pv, pg)]
    proj_beta, proj_decay = proj_small[:heads], proj_small[heads:]
    strength = jax.nn.sigmoid(proj_beta)
    rate = -jnp.exp(decay_log)[:, None]
    log_decay = rate * jax.nn.softplus(proj_decay)
    rows, cols = token_tables(seg_ids, strength, log_decay)
    gain_gated = norm_gated[None]
    gated, inv, upd, states = mixer_forward(
        *projected, cols, rows, conv_query, conv_key, conv_value, gain_gated
    )
    gated = flat(gated)
    middle, mids = exchange(
        z, [gated], [ow],
        [([("cols", 0, 0, gated.shape[1], 0)], finish_middle, [hidden_in, norm_ffn[None]], [local])],
        True, 0,
    )
    undo = 1.0 / (gains[1:] * gains[1:])
    xr, tr, inner, dgate, dup, weigh, scale_ffn = ffn(g, mids, tops, undo, ew, uw, dw)
    weigh = scale_ffn * scale_ffn * g.total(weigh[:, 0], "col")[:, None] / D
    wide = [rows_product(xr, dgate), rows_product(xr, dup), rows_product(inner, tr)]
    wide = [w.astype(bf16) for w in wide]
    weigh = lax.optimization_barrier((weigh, *wide))[0]
    gate_grad, up_grad = (g.sum_rows(w, 0) for w in wide[:2])
    hidden_units = dgate.shape[1]
    grad_middle, norm_sums, downs, dealt = exchange(
        z, [dgate, dup], [ew, uw],
        [(
            [("rows", 0, 0, hidden_units, 0), ("rows", 1, 0, hidden_units, 1)], finish_gradient,
            [cotangent, middle, norm_ffn[None], weigh], [local, sums],
        )],
        True, 1, [("deal", wide[2])],
    )
    down_grad = lax.dynamic_slice(wide[2], (0, g.at * g.shard), (hidden_units, g.shard)).astype(f32)
    down_grad = sum((dealt[n].astype(f32) for n in range(g.rows - 1)), start=down_grad)
    grad_norm_ffn = jnp.sum(norm_sums, axis=(0, 1))
    mr, grad_gated = back_gate(g, downs, ow)
    out_term = rows_product(gated, mr).astype(bf16)
    grad_gated = lax.optimization_barrier((grad_gated, out_term))[0]
    out_term, up_grad = lax.optimization_barrier((out_term, up_grad))
    out_grad = g.sum_rows(out_term, 1)
    dproj, dcols, dwq, dwk, dwv, dgain = mixer_backward(
        by_seq(grad_gated), *projected, cols, rows, inv, upd, states,
        conv_query, conv_key, conv_value, gain_gated,
    )
    dproj = flat(dproj)
    most = sum(widths)
    in_grads = g.sum_rows(rows_product(normed, dproj).astype(bf16), 0)
    dsmall = flat(dcols).T
    dstrength, dlog = dsmall[:heads], dsmall[heads:few]
    grad_small = jnp.concatenate(
        [dstrength * strength * (1.0 - strength), dlog * rate * jax.nn.sigmoid(proj_decay)], axis=0
    )
    weigh = g.total(dsmall[few] + jnp.sum(grad_small * proj_small, axis=0), "col")[:, None]
    weigh = scale_mixer * scale_mixer * weigh / D
    grad_small = grad_small.astype(bf16)
    small_grads = jnp.dot(grad_small, normed, preferred_element_type=f32)
    grad_decay_log = jnp.sum(dlog * log_decay, axis=1)
    pieces = [dwq, dwk, dwv, dgain, grad_norm_ffn, grad_decay_log, small_grads]
    count = sum(p.size for p in pieces)
    fill = jnp.zeros((-count % 1024,), f32)
    joined = jnp.concatenate([p.reshape(-1) for p in pieces] + [fill]).reshape(-1, 128)
    grad_input, mixer_sums, block_out, joined = exchange(
        z, [dproj, grad_small.T, inner], [inw, vw, dw],
        [
            (
                [("rows", 0, 0, most, 0), ("shards", 0, most, dproj.shape[1], 1), ("small", 1, 0, few, 1)],
                finish_input, [grad_middle, hidden_in, norm_mixer[None], scale_mixer, weigh], [local, sums],
            ),
            (
                [("ring", 2, 0, hidden_units, 2)], finish_out, [middle],
                [jax.ShapeDtypeStruct((tokens, g.block), bf16)],
            ),
        ],
        False, 2, [("share", joined)],
    )
    joined = joined.reshape(-1)
    grad_norm_mixer = g.total(jnp.sum(mixer_sums, axis=(0, 1)), "row")
    summed, at = [], 0
    for p in pieces:
        summed.append(joined[at : at + p.size].reshape(p.shape))
        at += p.size
    small_grads = lax.dynamic_slice(summed[6], (0, g.at * g.shard), (few, g.shard)).T
    grads, at = [], 0
    for w in widths + [w_value.shape[1]]:
        grads.append(in_grads[:, at : at + w].astype(f32))
        at += w
    return (
        block_out,
        grad_input,
        grad_norm_mixer,
        grads[0],
        grads[1],
        grads[3],
        grads[2],
        small_grads[:, :heads],
        small_grads[:, heads:],
        summed[5],
        summed[0],
        summed[1],
        summed[2],
        summed[3][0],
        out_grad.astype(f32),
        summed[4],
        gate_grad.astype(f32),
        up_grad.astype(f32),
        down_grad,
    )


def solution(mesh):
    placed = (
        P("row", "col"),
        P("row"),
        P("row", "col"),
        P("col"),
        P("row", "col"),
        P("row", "col"),
        P("row", "col"),
        P("row", "col"),
        P("row", "col"),
        P("row", "col"),
        P("col"),
        P(None, "col"),
        P(None, "col"),
        P(None, "col"),
        P("col"),
        P("col", "row"),
        P("col"),
        P("row", "col"),
        P("row", "col"),
        P("col", "row"),
    )
    return jax.shard_map(
        on_device,
        mesh=mesh,
        in_specs=placed,
        out_specs=(
            P("row", "col"),
            P("row", "col"),
            P("col"),
            P("row", "col"),
            P("row", "col"),
            P("row", "col"),
            P("row", "col"),
            P("row", "col"),
            P("row", "col"),
            P("col"),
            P(None, "col"),
            P(None, "col"),
            P(None, "col"),
            P("col"),
            P("col", "row"),
            P("col"),
            P("row", "col"),
            P("row", "col"),
            P("col", "row"),
        ),
        check_vma=False,
    )
```

```python
import functools

import jax
import jax.numpy as jnp
from jax import lax
from jax.experimental import pallas as pl
from jax.experimental.pallas import tpu as pltpu
from jax.sharding import PartitionSpec as P

D = 2048
DK = 128
DV = 256
CONV = 4
SEQ = 1024
CHUNK = 128
EPSILON = 1e-06
SCALE = DK ** (-0.5)
f32 = jnp.float32
bf16 = jnp.bfloat16


def mm(a, b, dims=((1,), (0,))):
    return lax.dot_general(a, b, (dims, ((), ())), preferred_element_type=f32)


def split(a):
    hi = a.astype(bf16)
    return hi, (a - hi.astype(f32)).astype(bf16)


def mm3(a, b):
    ah, al = split(a)
    bh, bl = split(b)
    return mm(ah, bh) + (mm(ah, bl) + mm(al, bh))


def sigmoid(u):
    return 1.0 / (1.0 + jnp.exp(-u))


def iotas(n):
    return (
        lax.broadcasted_iota(jnp.int32, (n, n), 0),
        lax.broadcasted_iota(jnp.int32, (n, n), 1),
    )


def unit_lower_inverses(many, row, col):
    n = many[0].shape[0]
    eye = (row == col).astype(f32)
    base = 8
    inside = row // base == col // base
    ds = [jnp.where(inside, a, 0.0) for a in many]
    squares = [mm3(d, d) for d in ds]
    xs = [eye - d for d in ds]
    xs = [x + mm3(x, d) for x, d in zip(xs, squares)]
    fourths = [mm3(d, d) for d in squares]
    xs = [x + mm3(x, d) for x, d in zip(xs, fourths)]
    size = base
    while size < n:
        at = (row // (2 * size) == col // (2 * size)) & (row // size != col // size)
        offs = [jnp.where(at, a, 0.0).astype(bf16) for a in many]
        highs = [x.astype(bf16) for x in xs]
        steps = [mm(off, x).astype(bf16) for off, x in zip(offs, highs)]
        xs = [x - mm(h, step) for x, h, step in zip(xs, highs, steps)]
        size *= 2
    return xs


def conv_taps(buf, s, width, weights, masks):
    pre = weights[0:1] * buf[s, 8 : 8 + CHUNK, :]
    for j in range(1, CONV):
        pre = pre + weights[j : j + 1] * buf[s, 8 - j : 8 - j + CHUNK, :] * masks[j - 1]
    return pre


def forward_kernel(heads, seqs, pq, pk, pv, pg, cols, rows, wq, wk, wv, gain,
                   gated, inv_out, upd_out, state_out, state, bq, bk, bv):
    step = pl.program_id(0)

    @pl.when(step == 0)
    def _():
        state[...] = jnp.zeros_like(state)
        for buf in (bq, bk, bv):
            buf[:, 0:8, :] = jnp.zeros_like(buf[:, 0:8, :])

    row, col = iotas(CHUNK)
    lower = row >= col
    tril = lower.astype(bf16)
    chains = []
    for s in range(seqs):
        cc = cols[s]
        rr = rows[s]
        masks = [cc[:, j : j + 1] for j in range(CONV - 1)]
        ch, cl = split(cc)
        csum = mm(tril, ch) + mm(tril, cl)
        rh, rl = split(rr)
        rsum = mm(rh, tril, ((1,), (1,))) + mm(rl, tril, ((1,), (1,)))
        same = (cc[:, 6:7] == rr[6:7, :]) & lower
        for src, buf in ((pq, bq), (pk, bk), (pv, bv)):
            buf[s, 8 : 8 + CHUNK, :] = src[s]
        cq = conv_taps(bq, s, heads * DK, wq, masks)
        ck = conv_taps(bk, s, heads * DK, wk, masks)
        cv = conv_taps(bv, s, heads * DV, wv, masks)
        for buf in (bq, bk, bv):
            buf[s, 0:8, :] = buf[s, CHUNK : CHUNK + 8, :]
        aq = cq * sigmoid(cq)
        ak = ck * sigmoid(ck)
        av = cv * sigmoid(cv)
        for h in range(heads):
            keys = slice(h * DK, (h + 1) * DK)
            vals = slice(h * DV, (h + 1) * DV)
            q = aq[:, keys]
            q = (q * lax.rsqrt(jnp.sum(q * q, axis=1, keepdims=True) + EPSILON)).astype(bf16)
            k = ak[:, keys]
            k = (k * lax.rsqrt(jnp.sum(k * k, axis=1, keepdims=True) + EPSILON)).astype(bf16)
            v = av[:, vals].astype(bf16).astype(f32)
            beta = cc[:, 8 + h : 9 + h]
            at = 8 + heads + h
            gcol = csum[:, at : at + 1]
            grow = rsum[at : at + 1, :]
            decay = jnp.where(same, jnp.exp(jnp.minimum(gcol - grow, 0.0)), 0.0)
            start = jnp.exp(gcol) * cc[:, 7:8]
            end = jnp.exp(jnp.minimum(gcol[CHUNK - 1 :, :] - gcol, 0.0)) * jnp.where(
                cc[:, 6:7] == cc[CHUNK - 1 :, 6:7], 1.0, 0.0
            )
            kk = mm(k, k, ((1,), (1,)))
            scores = (decay * mm(q, k, ((1,), (1,)))).astype(bf16)
            coupling = jnp.where(row > col, beta * decay * kk, 0.0)
            kend = (end * k.astype(f32)).astype(bf16)
            chains.append((s, h, vals, q, k, v, beta, start, scores, kend, coupling))
    inverses = unit_lower_inverses([c[-1] for c in chains], row, col)
    inverses = [x.astype(bf16) for x in inverses]
    begins = [state[c[0], c[1]] for c in chains]
    lows = [x.astype(bf16) for x in begins]
    rights = []
    for (s, h, vals, q, k, v, beta, start, scores, kend, _), inv, begin, low in zip(chains, inverses, begins, lows):
        inv_out[s, h] = inv
        state_out[0, s, h] = begin
        rights.append((beta * (v - start * mm(k, low))).astype(bf16))
    upds = [mm(inv, right).astype(bf16) for inv, right in zip(inverses, rights)]
    for (s, h, vals, q, k, v, beta, start, scores, kend, _), begin, low, upd in zip(chains, begins, lows, upds):
        upd_out[s, :, vals] = upd
        state[s, h] = start[CHUNK - 1 :, :] * begin + mm(kend, upd, ((0,), (0,)))
        mixed = (start * mm(q, low) + mm(scores, upd)) * SCALE
        gate = pg[s, :, vals]
        scaled = mixed * lax.rsqrt(jnp.mean(mixed * mixed, axis=1, keepdims=True) + EPSILON)
        gated[s, :, vals] = (scaled * gain[:, vals] * (gate * sigmoid(gate))).astype(bf16)


def backward_kernel(heads, seqs, dgated, pq, pk, pv, pg, hq, hk, hv, cols, rows, inv_in, upd_in, state_in,
                    wq, wk, wv, gain,
                    dproj, dcols, dwq, dwk, dwv, dgain,
                    dstate, bq, bk, bv, tq, tk, tv):
    step = pl.program_id(0)

    @pl.when(step == 0)
    def _():
        dstate[...] = jnp.zeros_like(dstate)
        for buf in (tq, tk, tv):
            buf[:, CHUNK : CHUNK + 8, :] = jnp.zeros_like(buf[:, CHUNK : CHUNK + 8, :])
        for out in (dwq, dwk, dwv, dgain):
            out[...] = jnp.zeros_like(out)

    row, col = iotas(CHUNK)
    lower = row >= col
    tril = lower.astype(bf16)
    lane = lax.broadcasted_iota(jnp.int32, (CHUNK, 2 * heads + 1), 1)
    last = lax.broadcasted_iota(jnp.int32, (CHUNK, 1), 0) == CHUNK - 1
    shared = []
    for s in range(seqs):
        cc = cols[s]
        rr = rows[s]
        masks = [cc[:, j : j + 1] for j in range(CONV - 1)]
        ch, cl = split(cc)
        csum = mm(tril, ch) + mm(tril, cl)
        rh, rl = split(rr)
        rsum = mm(rh, tril, ((1,), (1,))) + mm(rl, tril, ((1,), (1,)))
        same = (cc[:, 6:7] == rr[6:7, :]) & lower
        pres = []
        for src, halo, buf, weights in ((pq, hq, bq, wq), (pk, hk, bk, wk), (pv, hv, bv, wv)):
            buf[s, 0:8, :] = halo[s]
            buf[s, 8 : 8 + CHUNK, :] = src[s]
            pres.append(conv_taps(buf, s, None, weights, masks))
        sigs = [sigmoid(pre) for pre in pres]
        acts = [pre * sig for pre, sig in zip(pres, sigs)]
        shared.append((cc, masks, csum, rsum, same, pres, sigs, acts))
    found = {}

    def chain(s, h):
        cc, _, csum, rsum, same, pres, sigs, acts = shared[s]
        keys = slice(h * DK, (h + 1) * DK)
        vals = slice(h * DV, (h + 1) * DV)
        q = acts[0][:, keys]
        rq = lax.rsqrt(jnp.sum(q * q, axis=1, keepdims=True) + EPSILON)
        qn = q * rq
        q = qn.astype(bf16)
        k = acts[1][:, keys]
        rk = lax.rsqrt(jnp.sum(k * k, axis=1, keepdims=True) + EPSILON)
        kn = k * rk
        k = kn.astype(bf16)
        v = acts[2][:, vals].astype(bf16).astype(f32)
        beta = cc[:, 8 + h : 9 + h]
        at = 8 + heads + h
        gcol = csum[:, at : at + 1]
        grow = rsum[at : at + 1, :]
        decay = jnp.where(same, jnp.exp(jnp.minimum(gcol - grow, 0.0)), 0.0)
        start = jnp.exp(gcol) * cc[:, 7:8]
        end = jnp.exp(jnp.minimum(gcol[CHUNK - 1 :, :] - gcol, 0.0)) * jnp.where(
            cc[:, 6:7] == cc[CHUNK - 1 :, 6:7], 1.0, 0.0
        )
        begin = state_in[0, s, h]
        low = begin.astype(bf16)
        inv = inv_in[s, h]
        upd = upd_in[s, :, vals]
        ds = dstate[s, h]
        dsl = ds.astype(bf16)
        kf = k.astype(f32)
        kend = (end * kf).astype(bf16)
        kk = mm(k, k, ((1,), (1,)))
        qk = mm(q, k, ((1,), (1,)))
        ks = mm(k, low)
        qs = mm(q, low)
        uds = mm(upd, dsl, ((1,), (1,)))
        kds = mm(kend, dsl)
        yield
        plain = jnp.where(row > col, decay * kk, 0.0)
        scores = decay * qk
        scores_low = scores.astype(bf16)
        mixed = (start * qs + mm(scores_low, upd)) * SCALE
        yield
        gate = pg[s, :, vals]
        sg = sigmoid(gate)
        silu = gate * sg
        rm = lax.rsqrt(jnp.mean(mixed * mixed, axis=1, keepdims=True) + EPSILON)
        scaled = mixed * rm
        dy = dgated[s, :, vals]
        dyn = dy * scaled
        gains = gain[:, vals]
        dgain[:, vals] += jnp.sum(dyn * silu, axis=0, keepdims=True)
        dgate = dyn * gains * (sg * (1.0 + gate * (1.0 - sg)))
        dproj[s, :, 2 * heads * DK + h * DV : 2 * heads * DK + (h + 1) * DV] = dgate.astype(bf16)
        weigh = jnp.sum(dgate * gate, axis=1, keepdims=True)
        dscaled = dy * gains * silu
        dmixed = rm * (dscaled - scaled * jnp.mean(dscaled * scaled, axis=1, keepdims=True))
        dout = dmixed * SCALE
        dlow = dout.astype(bf16)
        dupd = mm(scores_low, dlow, ((0,), (0,))) + kds
        dscore = mm(dlow, upd, ((1,), (1,)))
        dqs = mm(dlow, low, ((1,), (1,)))
        dfirst = mm((start * q.astype(f32)).astype(bf16), dlow, ((0,), (0,)))
        yield
        dright = mm(inv, dupd.astype(bf16), ((0,), (0,)))
        dsc = (dscore * decay).astype(bf16)
        dqn = start * dqs + mm(dsc, k)
        dkn = end * uds + mm(dsc, q, ((0,), (0,)))
        yield
        drl = dright.astype(bf16)
        dcoup = -mm(drl, upd, ((1,), (1,)))
        w = beta * dright
        wa = (start * w).astype(bf16)
        dkn = dkn - mm(wa, low, ((1,), (1,)))
        final = start[CHUNK - 1 :, :]
        dstate[s, h] = dfirst + final * ds - mm(k, wa, ((0,), (0,)))
        yield
        g = jnp.where(row > col, beta * dcoup * decay, 0.0)
        dkn = dkn + mm((g + g.T).astype(bf16), k)
        dbeta = jnp.sum(dright * (v - start * ks), axis=1, keepdims=True) + jnp.sum(
            dcoup * plain, axis=1, keepdims=True
        )
        dstart = jnp.sum(dout * qs - w * ks, axis=1, keepdims=True)
        dend = jnp.sum(kf * uds, axis=1, keepdims=True) * end
        z = dscore * scores + dcoup * (beta * plain)
        carried = jnp.sum(jnp.sum(ds * begin, axis=1, keepdims=True), axis=0, keepdims=True) * final
        carried = carried + jnp.sum(dend, axis=0, keepdims=True)
        dg = jnp.sum(z - z.T, axis=1, keepdims=True) + dstart * start - dend
        dg = dg + jnp.where(last, carried, 0.0)
        found[s, h] = (dbeta, dg, weigh)
        yield
        dq = rq * (dqn - qn * jnp.sum(dqn * qn, axis=1, keepdims=True))
        dk = rk * (dkn - kn * jnp.sum(dkn * kn, axis=1, keepdims=True))
        for grad, n, buf, part in ((dq, 0, tq, keys), (dk, 1, tk, keys), (w, 2, tv, vals)):
            sig = sigs[n][:, part]
            buf[s, 0:CHUNK, part] = grad * (sig * (1.0 + pres[n][:, part] * (1.0 - sig)))

    chains = [chain(s, h) for s in range(seqs) for h in range(heads)]
    while chains:
        chains = [c for c in chains if next(c, chains) is None]

    kw, vw = heads * DK, heads * DV
    for s in range(seqs):
        cc, masks = shared[s][:2]
        ahead = [cc[:, 3 + j : 4 + j] for j in range(CONV - 1)]
        dcol = jnp.zeros((CHUNK, 2 * heads + 1), f32)
        weigh = jnp.zeros((CHUNK, 1), f32)
        for h in range(heads):
            dbeta, dg, more = found[s, h]
            dcol = dcol + jnp.where(lane == h, dbeta, 0.0) + jnp.where(lane == heads + h, dg, 0.0)
            weigh = weigh + more
        dh, dl = split(dcol)
        dl2 = (dcol - dh.astype(f32) - dl.astype(f32)).astype(bf16)
        tail = ((0,), (0,))
        rev = mm(tril, dh, tail) + (mm(tril, dl, tail) + mm(tril, dl2, tail))
        for buf, src, at, weights, dw in ((tq, bq, 0, wq, dwq), (tk, bk, kw, wk, dwk), (tv, bv, 2 * kw + vw, wv, dwv)):
            pre = buf[s, 0:CHUNK, :]
            total = weights[0:1] * pre
            dw[0:1, :] += jnp.sum(pre * src[s, 8 : 8 + CHUNK, :], axis=0, keepdims=True)
            for j in range(1, CONV):
                total = total + weights[j : j + 1] * buf[s, j : j + CHUNK, :] * ahead[j - 1]
                dw[j : j + 1, :] += jnp.sum(
                    pre * masks[j - 1] * src[s, 8 - j : 8 - j + CHUNK, :], axis=0, keepdims=True
                )
            dproj[s, :, at : at + total.shape[1]] = total.astype(bf16)
            weigh = weigh + jnp.sum(total * src[s, 8 : 8 + CHUNK, :], axis=1, keepdims=True)
            buf[s, CHUNK : CHUNK + 8, :] = buf[s, 0:8, :]
        dcols[s] = jnp.where(lane < heads, dcol, jnp.where(lane < 2 * heads, rev, weigh))


def whole(shape):
    return pl.BlockSpec(shape, lambda c: (0,) * len(shape))


def mixer_forward(pq, pk, pv, pg, cols, rows, wq, wk, wv, gain):
    seqs = pq.shape[0]
    heads = pq.shape[2] // DK
    steps = SEQ // CHUNK
    kw, vw = heads * DK, heads * DV

    def tok(width):
        return pl.BlockSpec((seqs, CHUNK, width), lambda c: (0, c, 0))

    return pl.pallas_call(
        functools.partial(forward_kernel, heads, seqs),
        grid=(steps,),
        in_specs=[tok(kw), tok(kw), tok(vw), tok(vw), tok(cols.shape[2]),
                  pl.BlockSpec((seqs, rows.shape[1], CHUNK), lambda c: (0, 0, c)),
                  whole((CONV, kw)), whole((CONV, kw)), whole((CONV, vw)), whole((1, vw))],
        out_specs=[tok(vw),
                   pl.BlockSpec((seqs, heads, CHUNK, CHUNK), lambda c: (0, 0, c, 0)),
                   tok(vw),
                   pl.BlockSpec((1, seqs, heads, DK, DV), lambda c: (c, 0, 0, 0, 0))],
        out_shape=[jax.ShapeDtypeStruct((seqs, SEQ, vw), bf16),
                   jax.ShapeDtypeStruct((seqs, heads, SEQ, CHUNK), bf16),
                   jax.ShapeDtypeStruct((seqs, SEQ, vw), bf16),
                   jax.ShapeDtypeStruct((steps, seqs, heads, DK, DV), f32)],
        scratch_shapes=[pltpu.VMEM((seqs, heads, DK, DV), f32),
                        pltpu.VMEM((seqs, 8 + CHUNK, kw), f32),
                        pltpu.VMEM((seqs, 8 + CHUNK, kw), f32),
                        pltpu.VMEM((seqs, 8 + CHUNK, vw), f32)],
        compiler_params=pltpu.CompilerParams(dimension_semantics=("arbitrary",), vmem_limit_bytes=48 << 20),
        name="mixer_forward",
    )(pq, pk, pv, pg, cols, rows, wq, wk, wv, gain)


def mixer_backward(dgated, pq, pk, pv, pg, cols, rows, inv, upd, states, wq, wk, wv, gain):
    seqs = pq.shape[0]
    heads = pq.shape[2] // DK
    steps = SEQ // CHUNK
    kw, vw = heads * DK, heads * DV

    def tok(width):
        return pl.BlockSpec((seqs, CHUNK, width), lambda c: (0, steps - 1 - c, 0))

    def halo(width):
        return pl.BlockSpec(
            (seqs, 8, width),
            lambda c: (0, jnp.maximum((steps - 1 - c) * (CHUNK // 8) - 1, 0), 0),
        )

    return pl.pallas_call(
        functools.partial(backward_kernel, heads, seqs),
        grid=(steps,),
        in_specs=[tok(vw), tok(kw), tok(kw), tok(vw), tok(vw), halo(kw), halo(kw), halo(vw), tok(cols.shape[2]),
                  pl.BlockSpec((seqs, rows.shape[1], CHUNK), lambda c: (0, 0, steps - 1 - c)),
                  pl.BlockSpec((seqs, heads, CHUNK, CHUNK), lambda c: (0, 0, steps - 1 - c, 0)),
                  tok(vw),
                  pl.BlockSpec((1, seqs, heads, DK, DV), lambda c: (steps - 1 - c, 0, 0, 0, 0)),
                  whole((CONV, kw)), whole((CONV, kw)), whole((CONV, vw)), whole((1, vw))],
        out_specs=[tok(2 * kw + 2 * vw), tok(2 * heads + 1),
                   whole((CONV, kw)), whole((CONV, kw)), whole((CONV, vw)), whole((1, vw))],
        out_shape=[jax.ShapeDtypeStruct((seqs, SEQ, 2 * kw + 2 * vw), bf16),
                   jax.ShapeDtypeStruct((seqs, SEQ, 2 * heads + 1), f32),
                   jax.ShapeDtypeStruct((CONV, kw), f32),
                   jax.ShapeDtypeStruct((CONV, kw), f32),
                   jax.ShapeDtypeStruct((CONV, vw), f32),
                   jax.ShapeDtypeStruct((1, vw), f32)],
        scratch_shapes=[pltpu.VMEM((seqs, heads, DK, DV), f32)]
        + [pltpu.VMEM((seqs, 8 + CHUNK, width), f32) for width in (kw, kw, vw)] * 2,
        compiler_params=pltpu.CompilerParams(dimension_semantics=("arbitrary",), vmem_limit_bytes=56 << 20),
        name="mixer_backward",
    )(dgated, pq, pk, pv, pg, pq, pk, pv, cols, rows, inv, upd, states, wq, wk, wv, gain)


def token_tables(seg_ids, strength, log_decay):
    seqs = seg_ids.shape[0] // SEQ
    seg = seg_ids.reshape(seqs, 1, SEQ)
    position = lax.broadcasted_iota(jnp.int32, (1, 1, SEQ), 2)
    back, ahead = [], []
    for j in range(1, CONV):
        same = seg[:, :, j:] == seg[:, :, : SEQ - j]
        none = jnp.zeros((seqs, 1, j), jnp.bool_)
        back.append(jnp.concatenate([none, same], axis=2))
        ahead.append(jnp.concatenate([same, none], axis=2))
    before = jnp.concatenate([jnp.full((seqs, 1, 1), -1, jnp.int32), seg[:, :, CHUNK - 1 : SEQ - 1 : CHUNK]], axis=2)
    carry = seg == jnp.repeat(before, CHUNK, axis=2)
    heads = strength.shape[0]
    tables = [m.astype(f32) for m in back + ahead] + [seg.astype(f32), carry.astype(f32)]
    tables += [
        jnp.swapaxes(strength.reshape(heads, seqs, SEQ), 0, 1),
        jnp.swapaxes(log_decay.reshape(heads, seqs, SEQ), 0, 1),
    ]
    pad = 16 - 8 - 2 * heads
    if pad:
        tables.append(jnp.zeros((seqs, pad, SEQ), f32))
    rows = jnp.concatenate(tables, axis=1)
    return rows, jnp.swapaxes(rows, 1, 2)

TILE = 256
STEP = 256
MESH = pl.DeviceIdType.MESH


def flip(value, bits):
    bit = 1
    while bit <= bits:
        if bits & bit:
            value = value + bit - 2 * bit * ((value // bit) % 2)
        bit *= 2
    return value


class Grid:
    def __init__(self):
        self.rows = lax.axis_size("row")
        self.cols = lax.axis_size("col")
        self.shard = D // self.rows
        self.block = D // self.cols
        self.parts = self.cols // self.rows
        self.half = self.cols // 2
        self.me = lax.axis_index("col")
        self.at = lax.axis_index("row")
        self.ids = jnp.stack([self.me, self.at]).astype(jnp.int32)
        self.slots = list(range(0, self.cols, 2)) + list(range(1, self.cols, 2))

    def swap(self, values, axis, bits):
        count = self.rows if axis == "row" else self.cols
        return lax.ppermute(values, axis, [(i, i ^ bits) for i in range(count)])

    def total(self, values, axis):
        bits = 1
        while bits < (self.rows if axis == "row" else self.cols):
            values = values + self.swap(values, axis, bits)
            bits *= 2
        return values

    def spread(self, values):
        return jnp.stack(
            [values]
            + [
                lax.ppermute(values, "row", [(i, (i + n) % self.rows) for i in range(self.rows)])
                for n in range(1, self.rows)
            ]
        )

    def gather_rows(self, values):
        return lax.all_gather(values, "row", axis=0, tiled=True)

    def sum_rows(self, term, axis):
        return lax.psum_scatter(term, "row", scatter_dimension=axis, tiled=True)


def fixed(array):
    return pl.BlockSpec(array.shape, lambda i, ids: (0,) * array.ndim, pipeline_mode=pl.Buffered(1))


def tokens_of(width, tile=TILE):
    return pl.BlockSpec((tile, width), lambda i, ids: (i, 0))


def slots_of(g):
    return pl.BlockSpec((g.cols, TILE, g.block), lambda i, ids: (0, i, 0))


def cost(flops, operands, outs):
    moved = sum(o.size * o.dtype.itemsize for o in operands)
    moved += sum(o.size * o.dtype.itemsize for o in outs)
    return pl.CostEstimate(flops=flops, bytes_accessed=moved, transcendentals=0)


def launch(kernel, grid, ids, operands, in_specs, out_specs, out_shape, scratch, name, flops):
    return pl.pallas_call(
        kernel,
        grid_spec=pltpu.PrefetchScalarGridSpec(
            num_scalar_prefetch=1, grid=grid, in_specs=in_specs, out_specs=out_specs, scratch_shapes=scratch
        ),
        out_shape=out_shape,
        compiler_params=pltpu.CompilerParams(
            dimension_semantics=("arbitrary",) * len(grid), vmem_limit_bytes=56 << 20
        ),
        cost_estimate=cost(flops, operands, out_shape),
        name=name,
    )(ids, *operands)


def place(g, ids, k):
    return pl.multiple_of((ids[0] ^ k) * g.block, g.block)


def dot_back(g, x, weights):
    return sum(
        mm(x[:, s * g.shard : (s + 1) * g.shard], weights[s], ((1,), (1,))) for s in range(g.rows)
    )


def ring_dot(g, ids, x, weights):
    total = 0.0
    for s in range(g.rows):
        shard = lax.rem(ids[1] - s + g.rows, g.rows)
        part = pl.ds(pl.multiple_of(shard * g.shard, g.shard), g.shard)
        total = total + mm(x[:, part], weights[s])
    return total


def project_kernel(g, widths, few, ids, blocks, gain, weight, ring, normed, scale, pq, pk, pg, pv, small):
    values = [blocks[k].astype(f32) for k in g.slots]
    squares = sum(jnp.sum(v * v, axis=1, keepdims=True) for v in values)
    scales = lax.rsqrt(squares / D + EPSILON)
    scale[...] = scales
    for k, v in zip(g.slots, values):
        at = place(g, ids, k)
        normed[:, pl.ds(at, g.block)] = (v * scales * gain[:, pl.ds(at, g.block)]).astype(bf16)
    x = normed[...]
    at = 0
    for out, width in zip((pq, pk, pg), widths):
        out[...] = mm(x, weight[:, at : at + width])
        at += width
    parts = [x[:, r * g.shard : (r + 1) * g.shard] for r in range(g.rows)]
    pv[...] = sum(mm(p, ring[r, : g.shard, :]) for r, p in enumerate(parts))
    small[...] = sum(
        mm(ring[r, g.shard : g.shard + few, : g.shard], p, ((1,), (1,))) for r, p in enumerate(parts)
    )


def project(g, blocks, gains, weight, ring, widths, few):
    tokens = blocks.shape[1]
    last = ring.shape[2]
    return launch(
        functools.partial(project_kernel, g, widths, few),
        (tokens // TILE,),
        g.ids,
        [blocks, gains, weight, ring],
        [slots_of(g)] + [fixed(w) for w in (gains, weight, ring)],
        [tokens_of(D), tokens_of(1)]
        + [tokens_of(w) for w in widths + [last]]
        + [pl.BlockSpec((few, TILE), lambda i, ids: (0, i))],
        [jax.ShapeDtypeStruct((tokens, D), bf16), jax.ShapeDtypeStruct((tokens, 1), f32)]
        + [jax.ShapeDtypeStruct((tokens, w), f32) for w in widths + [last]]
        + [jax.ShapeDtypeStruct((few, tokens), f32)],
        [],
        "project",
        2 * tokens * D * (sum(widths) + last + few),
    )


def inner_kernel(g, ids, ts, wd, tr, grad):
    for k in g.slots:
        tr[:, pl.ds(place(g, ids, k), g.block)] = ts[k]
    grad[...] = dot_back(g, tr, wd)


def inner_gradient(g, ts, wd):
    tokens = ts.shape[1]
    width = wd.shape[1]
    return launch(
        functools.partial(inner_kernel, g),
        (tokens // TILE,),
        g.ids,
        [ts, wd],
        [slots_of(g), fixed(wd)],
        [tokens_of(D), tokens_of(width)],
        [jax.ShapeDtypeStruct((tokens, D), bf16), jax.ShapeDtypeStruct((tokens, width), f32)],
        [],
        "inner_gradient",
        2 * tokens * D * width,
    )


def ffn_kernel(g, ids, xs, grads, undo, wg, wu, xr, inner, dgate, dup, total, scale):
    squares = 0.0
    for k in g.slots:
        at = place(g, ids, k)
        x = xs[k]
        xr[:, pl.ds(at, g.block)] = x
        v = x.astype(f32)
        squares = squares + jnp.sum(v * v * undo[:, pl.ds(at, g.block)], axis=1, keepdims=True)
    scales = lax.rsqrt(squares / D + EPSILON)
    scale[...] = scales
    gate = mm(xr[...], wg[...]) * scales
    up = ring_dot(g, ids, xr, wu) * scales
    grad = grads[...]
    sig = sigmoid(gate)
    silu = gate * sig
    inner[...] = (silu * up).astype(bf16)
    dg = grad * up * (sig * (1.0 + gate * (1.0 - sig)))
    du = grad * silu
    total[...] = jnp.sum(dg * gate + du * up, axis=1, keepdims=True)
    dgate[...] = (dg * scales).astype(bf16)
    dup[...] = (du * scales).astype(bf16)


def ffn(g, xs, grads, undo, wg, wu):
    tokens = xs.shape[1]
    width = wg.shape[1]
    return launch(
        functools.partial(ffn_kernel, g),
        (tokens // TILE,),
        g.ids,
        [xs, grads, undo, wg, wu],
        [slots_of(g), tokens_of(width)] + [fixed(w) for w in (undo, wg, wu)],
        [tokens_of(D)] + [tokens_of(width)] * 3 + [tokens_of(1)] * 2,
        [jax.ShapeDtypeStruct((tokens, D), bf16)]
        + [jax.ShapeDtypeStruct((tokens, width), bf16)] * 3
        + [jax.ShapeDtypeStruct((tokens, 1), f32)] * 2,
        [],
        "ffn",
        4 * tokens * D * width,
    )


def back_gate_kernel(g, ids, ms, wo, mr, out):
    for k in g.slots:
        mr[:, pl.ds(place(g, ids, k), g.block)] = ms[k]
    out[...] = dot_back(g, mr, wo)


def back_gate(g, ms, wo):
    tokens = ms.shape[1]
    width = wo.shape[1]
    return launch(
        functools.partial(back_gate_kernel, g),
        (tokens // TILE,),
        g.ids,
        [ms, wo],
        [slots_of(g), fixed(wo)],
        [tokens_of(D), tokens_of(width)],
        [jax.ShapeDtypeStruct((tokens, D), bf16), jax.ShapeDtypeStruct((tokens, width), f32)],
        [],
        "back_gate",
        2 * tokens * D * width,
    )


class Sizes:
    def __init__(self, g):
        self.rows, self.cols, self.block, self.parts, self.shard, self.half = (
            g.rows, g.cols, g.block, g.parts, g.shard, g.half
        )


def piece(z, kind, y, weight, owner):
    if kind == "rows":
        return mm(y, weight[pl.ds(pl.multiple_of(owner * z.block, z.block), z.block), :], ((1,), (1,)))
    shard = owner // z.parts
    part = pl.ds(pl.multiple_of((owner % z.parts) * z.block, z.block), z.block)
    if kind == "cols":
        return mm(y, weight[shard, :, part])
    slot = (lax.axis_index("row") - shard + z.rows) % z.rows
    if kind == "ring_rows":
        return mm(y, weight[slot, part, :], ((1,), (1,)))
    if kind == "shards":
        return mm(y, weight[shard, part, :], ((1,), (1,)))
    return mm(y, weight[shard, z.shard : z.shard + y.shape[1], part])


def greet(devices):
    barrier = pltpu.get_barrier_semaphore()
    for axis, index in devices:
        pl.semaphore_signal(barrier, inc=1, device_id={axis: index}, device_id_type=MESH)
    pl.semaphore_wait(barrier, len(devices))


def remote(source, target, send, receive, axis, index):
    return pltpu.make_async_remote_copy(
        src_ref=source, dst_ref=target, send_sem=send, recv_sem=receive,
        device_id={axis: index}, device_id_type=MESH,
    )


class Ride:
    def __init__(self, z, own, whole, keep, send, receive):
        self.z, self.own, self.whole, self.kept, self.send, self.receive = z, own, whole, keep, send, receive
        self.at = lax.axis_index("row")

    def neighbours(self):
        rows = self.z.rows
        return [("row", (self.at + 1) % rows), ("row", (self.at + rows - 1) % rows)]

    def keep(self):
        return pltpu.make_async_copy(self.own, self.whole.at[self.at], self.kept)

    def step(self, n):
        rows = self.z.rows
        shard = (self.at + rows + 1 - n) % rows
        source = self.own if n == 1 else self.whole.at[shard]
        return remote(
            source, self.whole.at[shard], self.send.at[n], self.receive.at[n], "row", (self.at + 1) % rows
        )


class Rider:
    def __init__(self, z, kind, own, given, refs):
        self.z, self.kind, self.own, self.given = z, kind, own, given
        self.at = lax.axis_index("row")
        self.send, self.receive, self.spare = refs

    def step(self, n):
        rows = self.z.rows
        to = (self.at + n) % rows
        if self.kind == "spread":
            source, target = self.own, self.given.at[self.at]
        elif self.kind in ("share", "late"):
            source = target = self.spare.at[self.at]
        else:
            part = pl.ds(pl.multiple_of(to * self.z.shard, self.z.shard), self.z.shard)
            source = self.own.at[:, part] if self.kind == "deal" else self.own.at[part, :]
            target = self.given.at[n - 1]
        return remote(source, target, self.send.at[n], self.receive.at[n], "row", to)

    def keep(self):
        return pltpu.make_async_copy(self.own, self.given.at[self.at], self.spare)

    def fill(self, values):
        self.spare[self.at] = jnp.broadcast_to(values, self.own.shape)
        for n in range(1, self.z.rows):
            self.step(n).start()

    def begin(self):
        if self.kind == "late":
            return
        if self.kind == "share":
            self.spare[self.at] = self.own[...]
        if self.kind == "spread":
            self.keep().start()
        for n in range(1, self.z.rows):
            self.step(n).start()

    def end(self):
        for n in range(1, self.z.rows):
            self.step(n).wait()
        if self.kind == "spread":
            self.keep().wait()
        if self.kind in ("share", "late"):
            total = self.spare[0]
            for n in range(1, self.z.rows):
                total = total + self.spare[n]
            self.given[...] = total


DEEP = 4


def exchange_kernel(z, plan, steps, tile, *refs):
    groups, arrays, weights, gathers, kinds = plan
    ys, refs = refs[:arrays], refs[arrays:]
    ws, refs = refs[:weights], refs[weights:]
    extras, outs = [], []
    for group in groups:
        extras.append(refs[: group[2]])
        refs = refs[group[2] :]
    own, refs = refs[: len(kinds)], refs[len(kinds) :]
    for group in groups:
        outs.append(refs[: group[3]])
        refs = refs[group[3] :]
    if gathers:
        slots, refs = refs[0], refs[1:]
    given, refs = refs[: len(kinds)], refs[len(kinds) :]
    near, far, far_got, pair_got, refs = *refs[:4], refs[4:]
    far_s, far_r, pair_s, pair_r, refs = *refs[:4], refs[4:]
    if gathers:
        block, own_s, same_s, same_r, turn_s, turn_r, part_s, part_r, refs = *refs[:8], refs[8:]
    me = lax.axis_index("col")
    partner = flip(me, 1)
    peers = [flip(me, 2 * j) for j in range(1, z.half)]
    met = [("col", device) for device in [partner] + peers]
    riders = [
        Rider(z, kind, own[n], given[n], refs[3 * n : 3 * n + 3]) for n, kind in enumerate(kinds)
    ]
    if riders:
        met = met + [("row", (riders[0].at + n) % z.rows) for n in range(1, z.rows)]
    greet(met)

    def rows_at(i):
        return pl.ds(pl.multiple_of(i * tile, tile), tile)

    def send_far(n, i):
        return remote(far.at[n, i % DEEP], far_got.at[n, i], far_s.at[n, i], far_r.at[n, i], "col", partner)

    def send_pair(n, i, j):
        return remote(
            near.at[n, i % DEEP, j], pair_got.at[n, i, j - 1], pair_s.at[n, i, j], pair_r.at[n, i, j],
            "col", peers[j - 1],
        )

    def keep(i):
        return pltpu.make_async_copy(block.at[i], slots.at[0, rows_at(i), :], own_s.at[i])

    def send_part(i):
        return remote(block.at[i], slots.at[1, rows_at(i), :], part_s.at[i], part_r.at[i], "col", partner)

    def send_same(i, j):
        return remote(
            block.at[i], slots.at[2 * j, rows_at(i), :], same_s.at[i, j], same_r.at[i, j], "col", peers[j - 1]
        )

    def send_turn(i, j):
        return remote(
            slots.at[2 * j, rows_at(i), :], slots.at[2 * j + 1, rows_at(i), :],
            turn_s.at[i, j], turn_r.at[i, j], "col", partner,
        )

    def sent(i):
        for n in range(len(groups)):
            send_far(n, i).wait_send()
            for j in range(1, z.half):
                send_pair(n, i, j).wait_send()

    lag = 4 if gathers else 3
    loops = steps + lag - 1
    for rider in riders:
        rider.begin()

    @pl.loop(0, loops)
    def _(it):
        @pl.when((it >= DEEP) & (it < steps))
        def _():
            sent(it - DEEP)

        @pl.when(it < steps)
        def _():
            for n, group in enumerate(groups):
                terms = group[0]
                tiles = [ys[t[1]][rows_at(it), t[2] : t[3]] for t in terms]
                for side, held in ((1, far), (0, near)):
                    for j in range(z.half):
                        owner = flip(me, 2 * j + side)
                        total = sum(piece(z, t[0], y, ws[t[4]], owner) for t, y in zip(terms, tiles))
                        held[n, it % DEEP, j] = total.astype(bf16)
                    if side == 1:
                        send_far(n, it).start()

        @pl.when((it >= 1) & (it < steps + 1))
        def _():
            i = it - 1
            for n in range(len(groups)):
                send_far(n, i).wait_recv()
                for j in range(1, z.half):
                    near[n, i % DEEP, j] = (
                        near[n, i % DEEP, j].astype(f32) + far_got[n, i, j].astype(f32)
                    ).astype(bf16)
                    send_pair(n, i, j).start()

        @pl.when((it >= 2) & (it < steps + 2))
        def _():
            i = it - 2
            for n, group in enumerate(groups):
                total = near[n, i % DEEP, 0].astype(f32) + far_got[n, i, 0].astype(f32)
                for j in range(1, z.half):
                    send_pair(n, i, j).wait_recv()
                    total = total + pair_got[n, i, j - 1].astype(f32)
                result = group[1](rows_at(i), i, total, extras[n], outs[n])
                if gathers and n == 0:
                    block[i] = result
                    for j in range(1, z.half):
                        send_same(i, j).start()
                    send_part(i).start()
                    keep(i).start()

        if gathers:
            @pl.when(it >= 3)
            def _():
                i = it - 3
                for j in range(1, z.half):
                    send_same(i, j).wait_recv()
                    send_turn(i, j).start()

    @pl.loop(max(0, steps - DEEP), steps)
    def _(i):
        sent(i)

    if gathers:
        @pl.loop(0, steps)
        def _(i):
            keep(i).wait()
            send_part(i).wait()
            for j in range(1, z.half):
                send_same(i, j).wait_send()
                send_turn(i, j).wait()

    for rider in riders:
        if rider.kind == "late":
            partial = outs[0][1]
            total = partial[0]
            for i in range(1, steps):
                total = total + partial[i]
            rider.fill(total)
    for rider in riders:
        rider.end()


def finish_middle(rows, i, total, extra, out):
    hidden, gain = extra
    middle = hidden[rows, :].astype(f32) + total
    out[0][rows, :] = middle
    return (middle * gain[...]).astype(bf16)


def finish_gradient(rows, i, total, extra, out):
    top, middle, gain, weigh = extra
    before = middle[rows, :]
    grad = top[rows, :].astype(f32) + gain[...] * total - before * weigh[rows, :]
    out[0][rows, :] = grad
    out[1][i] = jnp.sum(total * before, axis=0, keepdims=True)
    return grad.astype(bf16)


def finish_input(rows, i, total, extra, out):
    above, hidden, gain, scale, weigh = extra
    before = hidden[rows, :].astype(f32)
    scaled = scale[rows, :] * total
    out[0][rows, :] = above[rows, :] + gain[...] * scaled - before * weigh[rows, :]
    out[1][i] = jnp.sum(scaled * before, axis=0, keepdims=True)


def finish_out(rows, i, total, extra, out):
    (middle,) = extra
    out[0][rows, :] = (middle[rows, :] + total).astype(bf16)


def exchange(z, ys, ws, groups, gathers, number, riders=(), tile=STEP):
    tokens = ys[0].shape[0]
    steps = tokens // tile
    half, block, count = z.half, z.block, len(groups)
    vmem = pl.BlockSpec(memory_space=pltpu.VMEM)
    anywhere = pl.BlockSpec(memory_space=pl.ANY)
    dma = pltpu.SemaphoreType.DMA
    operands = [*ys, *ws]
    shapes = []
    for group in groups:
        operands += group[2]
        shapes += group[3]
    in_specs = [vmem] * len(operands)
    specs = [vmem] * len(shapes)
    scratch = [pltpu.VMEM((count, DEEP, half, tile, block), bf16)] * 2
    scratch += [pltpu.VMEM((count, steps, half, tile, block), bf16)]
    scratch += [pltpu.VMEM((count, steps, half - 1, tile, block), bf16)]
    scratch += [dma((count, steps))] * 2 + [dma((count, steps, half))] * 2
    if gathers:
        shapes.append(jax.ShapeDtypeStruct((z.cols, tokens, block), bf16))
        specs.append(anywhere)
        scratch += [pltpu.VMEM((steps, tile, block), bf16), dma((steps,))]
        scratch += [dma((steps, half))] * 4 + [dma((steps,))] * 2
    by_row = dma((z.rows,))
    for kind, own in riders:
        operands.append(own)
        in_specs.append(vmem if kind in ("share", "late") else anywhere)
        specs.append(in_specs[-1])
        scratch += [by_row] * 2
        if kind == "spread":
            shapes.append(jax.ShapeDtypeStruct((z.rows,) + own.shape, bf16))
            scratch.append(dma(()))
        elif kind in ("share", "late"):
            shapes.append(jax.ShapeDtypeStruct(own.shape, f32))
            scratch.append(pltpu.VMEM((z.rows,) + own.shape, f32))
        else:
            part = (own.shape[0], z.shard) if kind == "deal" else (z.shard, own.shape[1])
            shapes.append(jax.ShapeDtypeStruct((z.rows - 1,) + part, bf16))
            scratch.append(dma(()))
    kinds = [(group[0], group[1], len(group[2]), len(group[3])) for group in groups]
    depth = sum(t[3] - t[2] for group in groups for t in group[0])
    return pl.pallas_call(
        functools.partial(
            exchange_kernel, z, (kinds, len(ys), len(ws), gathers, [kind for kind, _ in riders]), steps, tile
        ),
        in_specs=in_specs,
        out_specs=specs,
        out_shape=shapes,
        scratch_shapes=scratch,
        compiler_params=pltpu.CompilerParams(
            collective_id=number, has_side_effects=True, vmem_limit_bytes=60 << 20
        ),
        cost_estimate=cost(2 * tokens * z.cols * block * depth, operands, shapes),
        name="exchange",
    )(*operands)


def begin_kernel(z, count, *refs):
    owns, own, slots, whole = refs[:count], refs[count], refs[count + 1 : 2 * count + 1], refs[2 * count + 1]
    kept, same_s, same_r, part_s, part_r, turn_s, turn_r, keep_s, step_s, step_r = refs[2 * count + 2 :]
    me = lax.axis_index("col")
    partner = flip(me, 1)
    peers = [flip(me, 2 * j) for j in range(1, z.half)]
    ride = Ride(z, own, whole, keep_s, step_s, step_r)
    greet([("col", device) for device in [partner] + peers] + ride.neighbours())

    def keep(n):
        return pltpu.make_async_copy(owns[n], slots[n].at[0], kept.at[n])

    def send_same(n, j):
        return remote(owns[n], slots[n].at[2 * j], same_s.at[n, j], same_r.at[n, j], "col", peers[j - 1])

    def send_part(n):
        return remote(owns[n], slots[n].at[1], part_s.at[n], part_r.at[n], "col", partner)

    def send_turn(n, j):
        return remote(slots[n].at[2 * j], slots[n].at[2 * j + 1], turn_s.at[n, j], turn_r.at[n, j], "col", partner)

    ride.step(1).start()
    ride.keep().start()
    for n in range(count):
        for j in range(1, z.half):
            send_same(n, j).start()
        send_part(n).start()
        keep(n).start()
    for s in range(2, z.rows):
        ride.step(s - 1).wait_recv()
        ride.step(s).start()
    for n in range(count):
        for j in range(1, z.half):
            send_same(n, j).wait_recv()
            send_turn(n, j).start()
    ride.keep().wait()
    ride.step(z.rows - 1).wait_recv()
    for s in range(1, z.rows):
        ride.step(s).wait_send()
    for n in range(count):
        keep(n).wait()
        send_part(n).wait()
        for j in range(1, z.half):
            send_same(n, j).wait_send()
            send_turn(n, j).wait()


def begin(z, owns, own, number):
    anywhere = pl.BlockSpec(memory_space=pl.ANY)
    dma = pltpu.SemaphoreType.DMA
    count = len(owns)
    shapes = [jax.ShapeDtypeStruct((z.cols,) + o.shape, o.dtype) for o in owns]
    shapes.append(jax.ShapeDtypeStruct((z.rows,) + own.shape, own.dtype))
    operands = [*owns, own]
    return pl.pallas_call(
        functools.partial(begin_kernel, z, count),
        in_specs=[anywhere] * len(operands),
        out_specs=[anywhere] * len(shapes),
        out_shape=shapes,
        scratch_shapes=[dma((count,))] + [dma((count, z.half))] * 2 + [dma((count,))] * 2
        + [dma((count, z.half))] * 2 + [dma(())] + [dma((z.rows,))] * 2,
        compiler_params=pltpu.CompilerParams(collective_id=number, has_side_effects=True),
        cost_estimate=cost(10**6, operands, shapes),
        name="begin",
    )(*operands)


def rows_product(first_op, second_op):
    return lax.dot_general(
        first_op, second_op, (((0,), (0,)), ((), ())), preferred_element_type=f32
    )


def on_device(
    hidden_in,
    seg_ids,
    cotangent,
    norm_mixer,
    w_query,
    w_key,
    w_value,
    w_gate,
    w_beta,
    w_decay,
    decay_log,
    conv_query,
    conv_key,
    conv_value,
    norm_gated,
    w_out,
    norm_ffn,
    w_ffn_gate,
    w_ffn_up,
    w_ffn_down,
):
    g = Grid()
    z = Sizes(g)
    tokens = seg_ids.shape[0]
    seqs = tokens // SEQ
    heads = decay_log.shape[0]
    local = jax.ShapeDtypeStruct((tokens, g.block), f32)
    sums = jax.ShapeDtypeStruct((tokens // STEP, 1, g.block), f32)

    def by_seq(values):
        return values.reshape(seqs, SEQ, values.shape[1])

    def flat(values):
        return values.reshape(tokens, values.shape[2])

    few = 2 * heads
    ins = (w_query, w_key, w_gate)
    widths = [w.shape[1] for w in ins]
    inw = g.gather_rows(jnp.concatenate(ins, axis=1))
    wide = max(w_value.shape[1], g.shard)
    value_in = jnp.pad(w_value, ((0, 16), (0, wide - w_value.shape[1])))
    value_in = lax.dynamic_update_slice(
        value_in, jnp.concatenate([w_beta, w_decay], axis=1).T, (g.shard, 0)
    )
    ow = g.gather_rows(w_out[None])
    dw = g.gather_rows(w_ffn_down[None])
    ew = g.gather_rows(w_ffn_gate)
    own_gains = jnp.stack([norm_mixer, norm_ffn])
    own_gains = jnp.pad(own_gains, ((0, 6), (0, 0)))
    blocks, tops, gains, vw = begin(z, [hidden_in, cotangent, own_gains], value_in, 3)
    order = jnp.arange(g.cols) ^ g.me
    gains = jnp.swapaxes(jnp.take(gains[:, :2], order, axis=0), 0, 1).reshape(2, D)

    normed, scale_mixer, pq, pk, pg, pv, proj_small = project(g, blocks, gains[:1], inw, vw, widths, few)
    up_own, _ = lax.optimization_barrier((w_ffn_up, proj_small))
    uw = g.spread(up_own)
    projected = [by_seq(p) for p in (pq, pk, pv, pg)]
    proj_beta, proj_decay = proj_small[:heads], proj_small[heads:]
    strength = jax.nn.sigmoid(proj_beta)
    rate = -jnp.exp(decay_log)[:, None]
    log_decay = rate * jax.nn.softplus(proj_decay)
    rows, cols = token_tables(seg_ids, strength, log_decay)
    gain_gated = norm_gated[None]
    gated, inv, upd, states = mixer_forward(
        *projected, cols, rows, conv_query, conv_key, conv_value, gain_gated
    )
    gated = flat(gated)
    middle, mids = exchange(
        z, [gated], [ow],
        [([("cols", 0, 0, gated.shape[1], 0)], finish_middle, [hidden_in, norm_ffn[None]], [local])],
        True, 0,
    )
    undo = 1.0 / (gains[1:] * gains[1:])
    tops = lax.optimization_barrier((tops, middle))[0]
    tr, grad_inner = inner_gradient(g, tops, dw)
    mids = lax.optimization_barrier((mids, grad_inner))[0]
    xr, inner, dgate, dup, weigh, scale_ffn = ffn(g, mids, grad_inner, undo, ew, uw)
    weigh = weigh[:, 0]
    wide = [rows_product(xr, dgate).astype(bf16)]
    weigh = weigh + g.swap(weigh, "col", 1)
    weigh, left = lax.optimization_barrier((weigh, dup))
    wide.append(rows_product(xr, left).astype(bf16))
    weigh = weigh + g.swap(weigh, "col", 2)
    weigh, left = lax.optimization_barrier((weigh, inner))
    wide.append(rows_product(left, tr).astype(bf16))
    bits = 4
    while bits < g.cols:
        weigh = weigh + g.swap(weigh, "col", bits)
        bits *= 2
    weigh = scale_ffn * scale_ffn * weigh[:, None] / D
    weigh = lax.optimization_barrier((weigh, *wide))[0]
    gate_grad, up_grad, down_grad = (g.sum_rows(w, axis) for w, axis in zip(wide, (0, 0, 1)))
    hidden_units = dgate.shape[1]
    grad_middle, norm_sums, downs = exchange(
        z, [dgate, dup], [ew, uw],
        [(
            [("rows", 0, 0, hidden_units, 0), ("ring_rows", 1, 0, hidden_units, 1)], finish_gradient,
            [cotangent, middle, norm_ffn[None], weigh], [local, sums],
        )],
        True, 1,
    )
    grad_norm_ffn = jnp.sum(norm_sums, axis=(0, 1))
    mr, grad_gated = back_gate(g, downs, ow)
    out_term = rows_product(gated, mr).astype(bf16)
    grad_gated = lax.optimization_barrier((grad_gated, out_term))[0]
    out_term, up_grad = lax.optimization_barrier((out_term, up_grad))
    out_grad = g.sum_rows(out_term, 1)
    dproj, dcols, dwq, dwk, dwv, dgain = mixer_backward(
        by_seq(grad_gated), *projected, cols, rows, inv, upd, states,
        conv_query, conv_key, conv_value, gain_gated,
    )
    dproj = flat(dproj)
    most = sum(widths)
    in_grads = g.sum_rows(rows_product(normed, dproj).astype(bf16), 0)
    dsmall = flat(dcols).T
    dstrength, dlog = dsmall[:heads], dsmall[heads:few]
    grad_small = jnp.concatenate(
        [dstrength * strength * (1.0 - strength), dlog * rate * jax.nn.sigmoid(proj_decay)], axis=0
    )
    weigh = g.total(dsmall[few] + jnp.sum(grad_small * proj_small, axis=0), "col")[:, None]
    weigh = scale_mixer * scale_mixer * weigh / D
    grad_small = grad_small.astype(bf16)
    small_grads = jnp.dot(grad_small, normed, preferred_element_type=f32)
    grad_decay_log = jnp.sum(dlog * log_decay, axis=1)
    pieces = [dwq, dwk, dwv, dgain, grad_norm_ffn, grad_decay_log, small_grads]
    count = sum(p.size for p in pieces)
    fill = jnp.zeros((-count % 1024,), f32)
    joined = jnp.concatenate([p.reshape(-1) for p in pieces] + [fill]).reshape(-1, 128)
    grad_input, _, block_out, joined, grad_norm_mixer = exchange(
        z, [dproj, grad_small.T, inner], [inw, vw, dw],
        [
            (
                [("rows", 0, 0, most, 0), ("shards", 0, most, dproj.shape[1], 1), ("small", 1, 0, few, 1)],
                finish_input, [grad_middle, hidden_in, norm_mixer[None], scale_mixer, weigh], [local, sums],
            ),
            (
                [("cols", 2, 0, hidden_units, 2)], finish_out, [middle],
                [jax.ShapeDtypeStruct((tokens, g.block), bf16)],
            ),
        ],
        False, 2, [("share", joined), ("late", jnp.zeros((8, g.block), f32))],
    )
    joined = joined.reshape(-1)
    grad_norm_mixer = grad_norm_mixer[0]
    summed, at = [], 0
    for p in pieces:
        summed.append(joined[at : at + p.size].reshape(p.shape))
        at += p.size
    small_grads = lax.dynamic_slice(summed[6], (0, g.at * g.shard), (few, g.shard)).T
    grads, at = [], 0
    for w in widths + [w_value.shape[1]]:
        grads.append(in_grads[:, at : at + w].astype(f32))
        at += w
    return (
        block_out,
        grad_input,
        grad_norm_mixer,
        grads[0],
        grads[1],
        grads[3],
        grads[2],
        small_grads[:, :heads],
        small_grads[:, heads:],
        summed[5],
        summed[0],
        summed[1],
        summed[2],
        summed[3][0],
        out_grad.astype(f32),
        summed[4],
        gate_grad.astype(f32),
        up_grad.astype(f32),
        down_grad.astype(f32),
    )


def solution(mesh):
    placed = (
        P("row", "col"),
        P("row"),
        P("row", "col"),
        P("col"),
        P("row", "col"),
        P("row", "col"),
        P("row", "col"),
        P("row", "col"),
        P("row", "col"),
        P("row", "col"),
        P("col"),
        P(None, "col"),
        P(None, "col"),
        P(None, "col"),
        P("col"),
        P("col", "row"),
        P("col"),
        P("row", "col"),
        P("row", "col"),
        P("col", "row"),
    )
    return jax.shard_map(
        on_device,
        mesh=mesh,
        in_specs=placed,
        out_specs=(
            P("row", "col"),
            P("row", "col"),
            P("col"),
            P("row", "col"),
            P("row", "col"),
            P("row", "col"),
            P("row", "col"),
            P("row", "col"),
            P("row", "col"),
            P("col"),
            P(None, "col"),
            P(None, "col"),
            P(None, "col"),
            P("col"),
            P("col", "row"),
            P("col"),
            P("row", "col"),
            P("row", "col"),
            P("col", "row"),
        ),
        check_vma=False,
    )
```

```python
import functools

import jax
import jax.numpy as jnp
from jax import lax
from jax.experimental import pallas as pl
from jax.experimental.pallas import tpu as pltpu
from jax.sharding import PartitionSpec as P

D = 2048
DK = 128
DV = 256
CONV = 4
SEQ = 1024
CHUNK = 128
EPSILON = 1e-06
SCALE = DK ** (-0.5)
f32 = jnp.float32
bf16 = jnp.bfloat16


def mm(a, b, dims=((1,), (0,))):
    return lax.dot_general(a, b, (dims, ((), ())), preferred_element_type=f32)


def split(a):
    hi = a.astype(bf16)
    return hi, (a - hi.astype(f32)).astype(bf16)


def mm3(a, b):
    ah, al = split(a)
    bh, bl = split(b)
    return mm(ah, bh) + (mm(ah, bl) + mm(al, bh))


def sigmoid(u):
    return 1.0 / (1.0 + jnp.exp(-u))


def iotas(n):
    return (
        lax.broadcasted_iota(jnp.int32, (n, n), 0),
        lax.broadcasted_iota(jnp.int32, (n, n), 1),
    )


def unit_lower_inverses(many, row, col):
    n = many[0].shape[0]
    eye = (row == col).astype(f32)
    base = 8
    inside = row // base == col // base
    ds = [jnp.where(inside, a, 0.0) for a in many]
    squares = [mm3(d, d) for d in ds]
    xs = [eye - d for d in ds]
    xs = [x + mm3(x, d) for x, d in zip(xs, squares)]
    fourths = [mm3(d, d) for d in squares]
    xs = [x + mm3(x, d) for x, d in zip(xs, fourths)]
    size = base
    while size < n:
        at = (row // (2 * size) == col // (2 * size)) & (row // size != col // size)
        offs = [jnp.where(at, a, 0.0).astype(bf16) for a in many]
        highs = [x.astype(bf16) for x in xs]
        steps = [mm(off, x).astype(bf16) for off, x in zip(offs, highs)]
        xs = [x - mm(h, step) for x, h, step in zip(xs, highs, steps)]
        size *= 2
    return xs


def conv_taps(buf, s, width, weights, masks):
    pre = weights[0:1] * buf[s, 8 : 8 + CHUNK, :]
    for j in range(1, CONV):
        pre = pre + weights[j : j + 1] * buf[s, 8 - j : 8 - j + CHUNK, :] * masks[j - 1]
    return pre


def forward_kernel(heads, seqs, pq, pk, pv, pg, cols, rows, wq, wk, wv, gain,
                   gated, inv_out, upd_out, state_out, state, bq, bk, bv):
    step = pl.program_id(0)

    @pl.when(step == 0)
    def _():
        state[...] = jnp.zeros_like(state)
        for buf in (bq, bk, bv):
            buf[:, 0:8, :] = jnp.zeros_like(buf[:, 0:8, :])

    row, col = iotas(CHUNK)
    lower = row >= col
    tril = lower.astype(bf16)
    chains = []
    for s in range(seqs):
        cc = cols[s]
        rr = rows[s]
        masks = [cc[:, j : j + 1] for j in range(CONV - 1)]
        ch, cl = split(cc)
        csum = mm(tril, ch) + mm(tril, cl)
        rh, rl = split(rr)
        rsum = mm(rh, tril, ((1,), (1,))) + mm(rl, tril, ((1,), (1,)))
        same = (cc[:, 6:7] == rr[6:7, :]) & lower
        for src, buf in ((pq, bq), (pk, bk), (pv, bv)):
            buf[s, 8 : 8 + CHUNK, :] = src[s]
        cq = conv_taps(bq, s, heads * DK, wq, masks)
        ck = conv_taps(bk, s, heads * DK, wk, masks)
        cv = conv_taps(bv, s, heads * DV, wv, masks)
        for buf in (bq, bk, bv):
            buf[s, 0:8, :] = buf[s, CHUNK : CHUNK + 8, :]
        aq = cq * sigmoid(cq)
        ak = ck * sigmoid(ck)
        av = cv * sigmoid(cv)
        for h in range(heads):
            keys = slice(h * DK, (h + 1) * DK)
            vals = slice(h * DV, (h + 1) * DV)
            q = aq[:, keys]
            q = (q * lax.rsqrt(jnp.sum(q * q, axis=1, keepdims=True) + EPSILON)).astype(bf16)
            k = ak[:, keys]
            k = (k * lax.rsqrt(jnp.sum(k * k, axis=1, keepdims=True) + EPSILON)).astype(bf16)
            v = av[:, vals].astype(bf16).astype(f32)
            beta = cc[:, 8 + h : 9 + h]
            at = 8 + heads + h
            gcol = csum[:, at : at + 1]
            grow = rsum[at : at + 1, :]
            decay = jnp.where(same, jnp.exp(jnp.minimum(gcol - grow, 0.0)), 0.0)
            start = jnp.exp(gcol) * cc[:, 7:8]
            end = jnp.exp(jnp.minimum(gcol[CHUNK - 1 :, :] - gcol, 0.0)) * jnp.where(
                cc[:, 6:7] == cc[CHUNK - 1 :, 6:7], 1.0, 0.0
            )
            kk = mm(k, k, ((1,), (1,)))
            scores = (decay * mm(q, k, ((1,), (1,)))).astype(bf16)
            coupling = jnp.where(row > col, beta * decay * kk, 0.0)
            kend = (end * k.astype(f32)).astype(bf16)
            chains.append((s, h, vals, q, k, v, beta, start, scores, kend, coupling))
    inverses = unit_lower_inverses([c[-1] for c in chains], row, col)
    inverses = [x.astype(bf16) for x in inverses]
    begins = [state[c[0], c[1]] for c in chains]
    lows = [x.astype(bf16) for x in begins]
    rights = []
    for (s, h, vals, q, k, v, beta, start, scores, kend, _), inv, begin, low in zip(chains, inverses, begins, lows):
        inv_out[s, h] = inv
        state_out[0, s, h] = begin
        rights.append((beta * (v - start * mm(k, low))).astype(bf16))
    upds = [mm(inv, right).astype(bf16) for inv, right in zip(inverses, rights)]
    for (s, h, vals, q, k, v, beta, start, scores, kend, _), begin, low, upd in zip(chains, begins, lows, upds):
        upd_out[s, :, vals] = upd
        state[s, h] = start[CHUNK - 1 :, :] * begin + mm(kend, upd, ((0,), (0,)))
        mixed = (start * mm(q, low) + mm(scores, upd)) * SCALE
        gate = pg[s, :, vals]
        scaled = mixed * lax.rsqrt(jnp.mean(mixed * mixed, axis=1, keepdims=True) + EPSILON)
        gated[s, :, vals] = (scaled * gain[:, vals] * (gate * sigmoid(gate))).astype(bf16)


def backward_kernel(heads, seqs, dgated, pq, pk, pv, pg, hq, hk, hv, cols, rows, inv_in, upd_in, state_in,
                    wq, wk, wv, gain,
                    dproj, dcols, dwq, dwk, dwv, dgain,
                    dstate, bq, bk, bv, tq, tk, tv):
    step = pl.program_id(0)

    @pl.when(step == 0)
    def _():
        dstate[...] = jnp.zeros_like(dstate)
        for buf in (tq, tk, tv):
            buf[:, CHUNK : CHUNK + 8, :] = jnp.zeros_like(buf[:, CHUNK : CHUNK + 8, :])
        for out in (dwq, dwk, dwv, dgain):
            out[...] = jnp.zeros_like(out)

    row, col = iotas(CHUNK)
    lower = row >= col
    tril = lower.astype(bf16)
    lane = lax.broadcasted_iota(jnp.int32, (CHUNK, 2 * heads + 1), 1)
    last = lax.broadcasted_iota(jnp.int32, (CHUNK, 1), 0) == CHUNK - 1
    shared = []
    for s in range(seqs):
        cc = cols[s]
        rr = rows[s]
        masks = [cc[:, j : j + 1] for j in range(CONV - 1)]
        ch, cl = split(cc)
        csum = mm(tril, ch) + mm(tril, cl)
        rh, rl = split(rr)
        rsum = mm(rh, tril, ((1,), (1,))) + mm(rl, tril, ((1,), (1,)))
        same = (cc[:, 6:7] == rr[6:7, :]) & lower
        pres = []
        for src, halo, buf, weights in ((pq, hq, bq, wq), (pk, hk, bk, wk), (pv, hv, bv, wv)):
            buf[s, 0:8, :] = halo[s]
            buf[s, 8 : 8 + CHUNK, :] = src[s]
            pres.append(conv_taps(buf, s, None, weights, masks))
        sigs = [sigmoid(pre) for pre in pres]
        acts = [pre * sig for pre, sig in zip(pres, sigs)]
        shared.append((cc, masks, csum, rsum, same, pres, sigs, acts))
    found = {}

    def chain(s, h):
        cc, _, csum, rsum, same, pres, sigs, acts = shared[s]
        keys = slice(h * DK, (h + 1) * DK)
        vals = slice(h * DV, (h + 1) * DV)
        q = acts[0][:, keys]
        rq = lax.rsqrt(jnp.sum(q * q, axis=1, keepdims=True) + EPSILON)
        qn = q * rq
        q = qn.astype(bf16)
        k = acts[1][:, keys]
        rk = lax.rsqrt(jnp.sum(k * k, axis=1, keepdims=True) + EPSILON)
        kn = k * rk
        k = kn.astype(bf16)
        v = acts[2][:, vals].astype(bf16).astype(f32)
        beta = cc[:, 8 + h : 9 + h]
        at = 8 + heads + h
        gcol = csum[:, at : at + 1]
        grow = rsum[at : at + 1, :]
        decay = jnp.where(same, jnp.exp(jnp.minimum(gcol - grow, 0.0)), 0.0)
        start = jnp.exp(gcol) * cc[:, 7:8]
        end = jnp.exp(jnp.minimum(gcol[CHUNK - 1 :, :] - gcol, 0.0)) * jnp.where(
            cc[:, 6:7] == cc[CHUNK - 1 :, 6:7], 1.0, 0.0
        )
        begin = state_in[0, s, h]
        low = begin.astype(bf16)
        inv = inv_in[s, h]
        upd = upd_in[s, :, vals]
        ds = dstate[s, h]
        dsl = ds.astype(bf16)
        kf = k.astype(f32)
        kend = (end * kf).astype(bf16)
        kk = mm(k, k, ((1,), (1,)))
        qk = mm(q, k, ((1,), (1,)))
        ks = mm(k, low)
        qs = mm(q, low)
        uds = mm(upd, dsl, ((1,), (1,)))
        kds = mm(kend, dsl)
        yield
        plain = jnp.where(row > col, decay * kk, 0.0)
        scores = decay * qk
        scores_low = scores.astype(bf16)
        mixed = (start * qs + mm(scores_low, upd)) * SCALE
        yield
        gate = pg[s, :, vals]
        sg = sigmoid(gate)
        silu = gate * sg
        rm = lax.rsqrt(jnp.mean(mixed * mixed, axis=1, keepdims=True) + EPSILON)
        scaled = mixed * rm
        dy = dgated[s, :, vals]
        dyn = dy * scaled
        gains = gain[:, vals]
        dgain[:, vals] += jnp.sum(dyn * silu, axis=0, keepdims=True)
        dgate = dyn * gains * (sg * (1.0 + gate * (1.0 - sg)))
        dproj[s, :, 2 * heads * DK + h * DV : 2 * heads * DK + (h + 1) * DV] = dgate.astype(bf16)
        weigh = jnp.sum(dgate * gate, axis=1, keepdims=True)
        dscaled = dy * gains * silu
        dmixed = rm * (dscaled - scaled * jnp.mean(dscaled * scaled, axis=1, keepdims=True))
        dout = dmixed * SCALE
        dlow = dout.astype(bf16)
        dupd = mm(scores_low, dlow, ((0,), (0,))) + kds
        dscore = mm(dlow, upd, ((1,), (1,)))
        dqs = mm(dlow, low, ((1,), (1,)))
        dfirst = mm((start * q.astype(f32)).astype(bf16), dlow, ((0,), (0,)))
        yield
        dright = mm(inv, dupd.astype(bf16), ((0,), (0,)))
        dsc = (dscore * decay).astype(bf16)
        dqn = start * dqs + mm(dsc, k)
        dkn = end * uds + mm(dsc, q, ((0,), (0,)))
        yield
        drl = dright.astype(bf16)
        dcoup = -mm(drl, upd, ((1,), (1,)))
        w = beta * dright
        wa = (start * w).astype(bf16)
        dkn = dkn - mm(wa, low, ((1,), (1,)))
        final = start[CHUNK - 1 :, :]
        dstate[s, h] = dfirst + final * ds - mm(k, wa, ((0,), (0,)))
        yield
        g = jnp.where(row > col, beta * dcoup * decay, 0.0)
        dkn = dkn + mm((g + g.T).astype(bf16), k)
        dbeta = jnp.sum(dright * (v - start * ks), axis=1, keepdims=True) + jnp.sum(
            dcoup * plain, axis=1, keepdims=True
        )
        dstart = jnp.sum(dout * qs - w * ks, axis=1, keepdims=True)
        dend = jnp.sum(kf * uds, axis=1, keepdims=True) * end
        z = dscore * scores + dcoup * (beta * plain)
        carried = jnp.sum(jnp.sum(ds * begin, axis=1, keepdims=True), axis=0, keepdims=True) * final
        carried = carried + jnp.sum(dend, axis=0, keepdims=True)
        dg = jnp.sum(z - z.T, axis=1, keepdims=True) + dstart * start - dend
        dg = dg + jnp.where(last, carried, 0.0)
        found[s, h] = (dbeta, dg, weigh)
        yield
        dq = rq * (dqn - qn * jnp.sum(dqn * qn, axis=1, keepdims=True))
        dk = rk * (dkn - kn * jnp.sum(dkn * kn, axis=1, keepdims=True))
        for grad, n, buf, part in ((dq, 0, tq, keys), (dk, 1, tk, keys), (w, 2, tv, vals)):
            sig = sigs[n][:, part]
            buf[s, 0:CHUNK, part] = grad * (sig * (1.0 + pres[n][:, part] * (1.0 - sig)))

    chains = [chain(s, h) for s in range(seqs) for h in range(heads)]
    while chains:
        chains = [c for c in chains if next(c, chains) is None]

    kw, vw = heads * DK, heads * DV
    for s in range(seqs):
        cc, masks = shared[s][:2]
        ahead = [cc[:, 3 + j : 4 + j] for j in range(CONV - 1)]
        dcol = jnp.zeros((CHUNK, 2 * heads + 1), f32)
        weigh = jnp.zeros((CHUNK, 1), f32)
        for h in range(heads):
            dbeta, dg, more = found[s, h]
            dcol = dcol + jnp.where(lane == h, dbeta, 0.0) + jnp.where(lane == heads + h, dg, 0.0)
            weigh = weigh + more
        dh, dl = split(dcol)
        dl2 = (dcol - dh.astype(f32) - dl.astype(f32)).astype(bf16)
        tail = ((0,), (0,))
        rev = mm(tril, dh, tail) + (mm(tril, dl, tail) + mm(tril, dl2, tail))
        for buf, src, at, weights, dw in ((tq, bq, 0, wq, dwq), (tk, bk, kw, wk, dwk), (tv, bv, 2 * kw + vw, wv, dwv)):
            pre = buf[s, 0:CHUNK, :]
            total = weights[0:1] * pre
            dw[0:1, :] += jnp.sum(pre * src[s, 8 : 8 + CHUNK, :], axis=0, keepdims=True)
            for j in range(1, CONV):
                total = total + weights[j : j + 1] * buf[s, j : j + CHUNK, :] * ahead[j - 1]
                dw[j : j + 1, :] += jnp.sum(
                    pre * masks[j - 1] * src[s, 8 - j : 8 - j + CHUNK, :], axis=0, keepdims=True
                )
            dproj[s, :, at : at + total.shape[1]] = total.astype(bf16)
            weigh = weigh + jnp.sum(total * src[s, 8 : 8 + CHUNK, :], axis=1, keepdims=True)
            buf[s, CHUNK : CHUNK + 8, :] = buf[s, 0:8, :]
        dcols[s] = jnp.where(lane < heads, dcol, jnp.where(lane < 2 * heads, rev, weigh))


def whole(shape):
    return pl.BlockSpec(shape, lambda c: (0,) * len(shape))


def mixer_forward(pq, pk, pv, pg, cols, rows, wq, wk, wv, gain):
    seqs = pq.shape[0]
    heads = pq.shape[2] // DK
    steps = SEQ // CHUNK
    kw, vw = heads * DK, heads * DV

    def tok(width):
        return pl.BlockSpec((seqs, CHUNK, width), lambda c: (0, c, 0))

    return pl.pallas_call(
        functools.partial(forward_kernel, heads, seqs),
        grid=(steps,),
        in_specs=[tok(kw), tok(kw), tok(vw), tok(vw), tok(cols.shape[2]),
                  pl.BlockSpec((seqs, rows.shape[1], CHUNK), lambda c: (0, 0, c)),
                  whole((CONV, kw)), whole((CONV, kw)), whole((CONV, vw)), whole((1, vw))],
        out_specs=[tok(vw),
                   pl.BlockSpec((seqs, heads, CHUNK, CHUNK), lambda c: (0, 0, c, 0)),
                   tok(vw),
                   pl.BlockSpec((1, seqs, heads, DK, DV), lambda c: (c, 0, 0, 0, 0))],
        out_shape=[jax.ShapeDtypeStruct((seqs, SEQ, vw), bf16),
                   jax.ShapeDtypeStruct((seqs, heads, SEQ, CHUNK), bf16),
                   jax.ShapeDtypeStruct((seqs, SEQ, vw), bf16),
                   jax.ShapeDtypeStruct((steps, seqs, heads, DK, DV), f32)],
        scratch_shapes=[pltpu.VMEM((seqs, heads, DK, DV), f32),
                        pltpu.VMEM((seqs, 8 + CHUNK, kw), f32),
                        pltpu.VMEM((seqs, 8 + CHUNK, kw), f32),
                        pltpu.VMEM((seqs, 8 + CHUNK, vw), f32)],
        compiler_params=pltpu.CompilerParams(dimension_semantics=("arbitrary",), vmem_limit_bytes=48 << 20),
        name="mixer_forward",
    )(pq, pk, pv, pg, cols, rows, wq, wk, wv, gain)


def mixer_backward(dgated, pq, pk, pv, pg, cols, rows, inv, upd, states, wq, wk, wv, gain):
    seqs = pq.shape[0]
    heads = pq.shape[2] // DK
    steps = SEQ // CHUNK
    kw, vw = heads * DK, heads * DV

    def tok(width):
        return pl.BlockSpec((seqs, CHUNK, width), lambda c: (0, steps - 1 - c, 0))

    def halo(width):
        return pl.BlockSpec(
            (seqs, 8, width),
            lambda c: (0, jnp.maximum((steps - 1 - c) * (CHUNK // 8) - 1, 0), 0),
        )

    return pl.pallas_call(
        functools.partial(backward_kernel, heads, seqs),
        grid=(steps,),
        in_specs=[tok(vw), tok(kw), tok(kw), tok(vw), tok(vw), halo(kw), halo(kw), halo(vw), tok(cols.shape[2]),
                  pl.BlockSpec((seqs, rows.shape[1], CHUNK), lambda c: (0, 0, steps - 1 - c)),
                  pl.BlockSpec((seqs, heads, CHUNK, CHUNK), lambda c: (0, 0, steps - 1 - c, 0)),
                  tok(vw),
                  pl.BlockSpec((1, seqs, heads, DK, DV), lambda c: (steps - 1 - c, 0, 0, 0, 0)),
                  whole((CONV, kw)), whole((CONV, kw)), whole((CONV, vw)), whole((1, vw))],
        out_specs=[tok(2 * kw + 2 * vw), tok(2 * heads + 1),
                   whole((CONV, kw)), whole((CONV, kw)), whole((CONV, vw)), whole((1, vw))],
        out_shape=[jax.ShapeDtypeStruct((seqs, SEQ, 2 * kw + 2 * vw), bf16),
                   jax.ShapeDtypeStruct((seqs, SEQ, 2 * heads + 1), f32),
                   jax.ShapeDtypeStruct((CONV, kw), f32),
                   jax.ShapeDtypeStruct((CONV, kw), f32),
                   jax.ShapeDtypeStruct((CONV, vw), f32),
                   jax.ShapeDtypeStruct((1, vw), f32)],
        scratch_shapes=[pltpu.VMEM((seqs, heads, DK, DV), f32)]
        + [pltpu.VMEM((seqs, 8 + CHUNK, width), f32) for width in (kw, kw, vw)] * 2,
        compiler_params=pltpu.CompilerParams(dimension_semantics=("arbitrary",), vmem_limit_bytes=56 << 20),
        name="mixer_backward",
    )(dgated, pq, pk, pv, pg, pq, pk, pv, cols, rows, inv, upd, states, wq, wk, wv, gain)


def token_tables(seg_ids, strength, log_decay):
    seqs = seg_ids.shape[0] // SEQ
    seg = seg_ids.reshape(seqs, 1, SEQ)
    position = lax.broadcasted_iota(jnp.int32, (1, 1, SEQ), 2)
    back, ahead = [], []
    for j in range(1, CONV):
        same = seg[:, :, j:] == seg[:, :, : SEQ - j]
        none = jnp.zeros((seqs, 1, j), jnp.bool_)
        back.append(jnp.concatenate([none, same], axis=2))
        ahead.append(jnp.concatenate([same, none], axis=2))
    before = jnp.concatenate([jnp.full((seqs, 1, 1), -1, jnp.int32), seg[:, :, CHUNK - 1 : SEQ - 1 : CHUNK]], axis=2)
    carry = seg == jnp.repeat(before, CHUNK, axis=2)
    heads = strength.shape[0]
    tables = [m.astype(f32) for m in back + ahead] + [seg.astype(f32), carry.astype(f32)]
    tables += [
        jnp.swapaxes(strength.reshape(heads, seqs, SEQ), 0, 1),
        jnp.swapaxes(log_decay.reshape(heads, seqs, SEQ), 0, 1),
    ]
    pad = 16 - 8 - 2 * heads
    if pad:
        tables.append(jnp.zeros((seqs, pad, SEQ), f32))
    rows = jnp.concatenate(tables, axis=1)
    return rows, jnp.swapaxes(rows, 1, 2)

TILE = 256
STEP = 256
MESH = pl.DeviceIdType.MESH


def flip(value, bits):
    bit = 1
    while bit <= bits:
        if bits & bit:
            value = value + bit - 2 * bit * ((value // bit) % 2)
        bit *= 2
    return value


class Grid:
    def __init__(self):
        self.rows = lax.axis_size("row")
        self.cols = lax.axis_size("col")
        self.shard = D // self.rows
        self.block = D // self.cols
        self.parts = self.cols // self.rows
        self.half = self.cols // 2
        self.me = lax.axis_index("col")
        self.at = lax.axis_index("row")
        self.ids = jnp.stack([self.me, self.at]).astype(jnp.int32)
        self.slots = list(range(0, self.cols, 2)) + list(range(1, self.cols, 2))

    def swap(self, values, axis, bits):
        count = self.rows if axis == "row" else self.cols
        return lax.ppermute(values, axis, [(i, i ^ bits) for i in range(count)])

    def total(self, values, axis):
        bits = 1
        while bits < (self.rows if axis == "row" else self.cols):
            values = values + self.swap(values, axis, bits)
            bits *= 2
        return values

    def spread(self, values):
        return jnp.stack(
            [values]
            + [
                lax.ppermute(values, "row", [(i, (i + n) % self.rows) for i in range(self.rows)])
                for n in range(1, self.rows)
            ]
        )

    def gather_rows(self, values):
        return lax.all_gather(values, "row", axis=0, tiled=True)

    def sum_rows(self, term, axis):
        return lax.psum_scatter(term, "row", scatter_dimension=axis, tiled=True)


def fixed(array):
    return pl.BlockSpec(array.shape, lambda i, ids: (0,) * array.ndim, pipeline_mode=pl.Buffered(1))


def tokens_of(width, tile=TILE):
    return pl.BlockSpec((tile, width), lambda i, ids: (i, 0))


def slots_of(g):
    return pl.BlockSpec((g.cols, TILE, g.block), lambda i, ids: (0, i, 0))


def cost(flops, operands, outs):
    moved = sum(o.size * o.dtype.itemsize for o in operands)
    moved += sum(o.size * o.dtype.itemsize for o in outs)
    return pl.CostEstimate(flops=flops, bytes_accessed=moved, transcendentals=0)


def launch(kernel, grid, ids, operands, in_specs, out_specs, out_shape, scratch, name, flops):
    return pl.pallas_call(
        kernel,
        grid_spec=pltpu.PrefetchScalarGridSpec(
            num_scalar_prefetch=1, grid=grid, in_specs=in_specs, out_specs=out_specs, scratch_shapes=scratch
        ),
        out_shape=out_shape,
        compiler_params=pltpu.CompilerParams(
            dimension_semantics=("arbitrary",) * len(grid), vmem_limit_bytes=56 << 20
        ),
        cost_estimate=cost(flops, operands, out_shape),
        name=name,
    )(ids, *operands)


def place(g, ids, k):
    return pl.multiple_of((ids[0] ^ k) * g.block, g.block)


def dot_back(g, x, weights):
    return sum(
        mm(x[:, s * g.shard : (s + 1) * g.shard], weights[s], ((1,), (1,))) for s in range(g.rows)
    )


def ring_dot(g, ids, x, weights):
    total = 0.0
    for s in range(g.rows):
        shard = lax.rem(ids[1] - s + g.rows, g.rows)
        part = pl.ds(pl.multiple_of(shard * g.shard, g.shard), g.shard)
        total = total + mm(x[:, part], weights[s])
    return total


def project_kernel(g, widths, few, ids, blocks, gain, weight, ring, normed, scale, pq, pk, pg, pv, small):
    values = [blocks[k].astype(f32) for k in g.slots]
    squares = sum(jnp.sum(v * v, axis=1, keepdims=True) for v in values)
    scales = lax.rsqrt(squares / D + EPSILON)
    scale[...] = scales
    for k, v in zip(g.slots, values):
        at = place(g, ids, k)
        normed[:, pl.ds(at, g.block)] = (v * scales * gain[:, pl.ds(at, g.block)]).astype(bf16)
    x = normed[...]
    at = 0
    for out, width in zip((pq, pk, pg), widths):
        out[...] = mm(x, weight[:, at : at + width])
        at += width
    parts = [x[:, r * g.shard : (r + 1) * g.shard] for r in range(g.rows)]
    pv[...] = sum(mm(p, ring[r, : g.shard, :]) for r, p in enumerate(parts))
    small[...] = sum(
        mm(ring[r, g.shard : g.shard + few, : g.shard], p, ((1,), (1,))) for r, p in enumerate(parts)
    )


def project(g, blocks, gains, weight, ring, widths, few):
    tokens = blocks.shape[1]
    last = ring.shape[2]
    return launch(
        functools.partial(project_kernel, g, widths, few),
        (tokens // TILE,),
        g.ids,
        [blocks, gains, weight, ring],
        [slots_of(g)] + [fixed(w) for w in (gains, weight, ring)],
        [tokens_of(D), tokens_of(1)]
        + [tokens_of(w) for w in widths + [last]]
        + [pl.BlockSpec((few, TILE), lambda i, ids: (0, i))],
        [jax.ShapeDtypeStruct((tokens, D), bf16), jax.ShapeDtypeStruct((tokens, 1), f32)]
        + [jax.ShapeDtypeStruct((tokens, w), f32) for w in widths + [last]]
        + [jax.ShapeDtypeStruct((few, tokens), f32)],
        [],
        "project",
        2 * tokens * D * (sum(widths) + last + few),
    )


def inner_kernel(g, ids, ts, wd, tr, grad):
    for k in g.slots:
        tr[:, pl.ds(place(g, ids, k), g.block)] = ts[k]
    grad[...] = dot_back(g, tr, wd)


def inner_gradient(g, ts, wd):
    tokens = ts.shape[1]
    width = wd.shape[1]
    return launch(
        functools.partial(inner_kernel, g),
        (tokens // TILE,),
        g.ids,
        [ts, wd],
        [slots_of(g), fixed(wd)],
        [tokens_of(D), tokens_of(width)],
        [jax.ShapeDtypeStruct((tokens, D), bf16), jax.ShapeDtypeStruct((tokens, width), f32)],
        [],
        "inner_gradient",
        2 * tokens * D * width,
    )


def ffn_kernel(g, ids, xs, grads, undo, wg, wu, xr, inner, dgate, dup, total, scale):
    squares = 0.0
    for k in g.slots:
        at = place(g, ids, k)
        x = xs[k]
        xr[:, pl.ds(at, g.block)] = x
        v = x.astype(f32)
        squares = squares + jnp.sum(v * v * undo[:, pl.ds(at, g.block)], axis=1, keepdims=True)
    scales = lax.rsqrt(squares / D + EPSILON)
    scale[...] = scales
    gate = mm(xr[...], wg[...]) * scales
    up = ring_dot(g, ids, xr, wu) * scales
    grad = grads[...]
    sig = sigmoid(gate)
    silu = gate * sig
    inner[...] = (silu * up).astype(bf16)
    dg = grad * up * (sig * (1.0 + gate * (1.0 - sig)))
    du = grad * silu
    total[...] = jnp.sum(dg * gate + du * up, axis=1, keepdims=True)
    dgate[...] = (dg * scales).astype(bf16)
    dup[...] = (du * scales).astype(bf16)


def ffn(g, xs, grads, undo, wg, wu):
    tokens = xs.shape[1]
    width = wg.shape[1]
    return launch(
        functools.partial(ffn_kernel, g),
        (tokens // TILE,),
        g.ids,
        [xs, grads, undo, wg, wu],
        [slots_of(g), tokens_of(width)] + [fixed(w) for w in (undo, wg, wu)],
        [tokens_of(D)] + [tokens_of(width)] * 3 + [tokens_of(1)] * 2,
        [jax.ShapeDtypeStruct((tokens, D), bf16)]
        + [jax.ShapeDtypeStruct((tokens, width), bf16)] * 3
        + [jax.ShapeDtypeStruct((tokens, 1), f32)] * 2,
        [],
        "ffn",
        4 * tokens * D * width,
    )


def back_gate_kernel(g, ids, ms, wo, mr, out):
    for k in g.slots:
        mr[:, pl.ds(place(g, ids, k), g.block)] = ms[k]
    out[...] = dot_back(g, mr, wo)


def back_gate(g, ms, wo):
    tokens = ms.shape[1]
    width = wo.shape[1]
    return launch(
        functools.partial(back_gate_kernel, g),
        (tokens // TILE,),
        g.ids,
        [ms, wo],
        [slots_of(g), fixed(wo)],
        [tokens_of(D), tokens_of(width)],
        [jax.ShapeDtypeStruct((tokens, D), bf16), jax.ShapeDtypeStruct((tokens, width), f32)],
        [],
        "back_gate",
        2 * tokens * D * width,
    )


class Sizes:
    def __init__(self, g):
        self.rows, self.cols, self.block, self.parts, self.shard, self.half = (
            g.rows, g.cols, g.block, g.parts, g.shard, g.half
        )


def piece(z, kind, y, weight, owner):
    if kind == "rows":
        return mm(y, weight[pl.ds(pl.multiple_of(owner * z.block, z.block), z.block), :], ((1,), (1,)))
    shard = owner // z.parts
    part = pl.ds(pl.multiple_of((owner % z.parts) * z.block, z.block), z.block)
    if kind == "cols":
        return mm(y, weight[shard, :, part])
    slot = (lax.axis_index("row") - shard + z.rows) % z.rows
    if kind == "ring_rows":
        return mm(y, weight[slot, part, :], ((1,), (1,)))
    if kind == "shards":
        return mm(y, weight[shard, part, :], ((1,), (1,)))
    return mm(y, weight[shard, z.shard : z.shard + y.shape[1], part])


def greet(devices):
    barrier = pltpu.get_barrier_semaphore()
    for axis, index in devices:
        pl.semaphore_signal(barrier, inc=1, device_id={axis: index}, device_id_type=MESH)
    pl.semaphore_wait(barrier, len(devices))


def remote(source, target, send, receive, axis, index):
    return pltpu.make_async_remote_copy(
        src_ref=source, dst_ref=target, send_sem=send, recv_sem=receive,
        device_id={axis: index}, device_id_type=MESH,
    )


class Ride:
    def __init__(self, z, own, whole, keep, send, receive):
        self.z, self.own, self.whole, self.kept, self.send, self.receive = z, own, whole, keep, send, receive
        self.at = lax.axis_index("row")

    def neighbours(self):
        rows = self.z.rows
        return [("row", (self.at + 1) % rows), ("row", (self.at + rows - 1) % rows)]

    def keep(self):
        return pltpu.make_async_copy(self.own, self.whole.at[self.at], self.kept)

    def step(self, n):
        rows = self.z.rows
        shard = (self.at + rows + 1 - n) % rows
        source = self.own if n == 1 else self.whole.at[shard]
        return remote(
            source, self.whole.at[shard], self.send.at[n], self.receive.at[n], "row", (self.at + 1) % rows
        )


class Rider:
    def __init__(self, z, kind, own, given, refs):
        self.z, self.kind, self.own, self.given = z, kind, own, given
        self.at = lax.axis_index("row")
        self.send, self.receive, self.spare = refs

    def step(self, n):
        rows = self.z.rows
        to = (self.at + n) % rows
        if self.kind == "spread":
            source, target = self.own, self.given.at[self.at]
        elif self.kind in ("share", "late"):
            source = target = self.spare.at[self.at]
        else:
            part = pl.ds(pl.multiple_of(to * self.z.shard, self.z.shard), self.z.shard)
            source = self.own.at[:, part] if self.kind == "deal" else self.own.at[part, :]
            target = self.given.at[n - 1]
        return remote(source, target, self.send.at[n], self.receive.at[n], "row", to)

    def keep(self):
        return pltpu.make_async_copy(self.own, self.given.at[self.at], self.spare)

    def fill(self, values):
        self.spare[self.at] = jnp.broadcast_to(values, self.own.shape)
        for n in range(1, self.z.rows):
            self.step(n).start()

    def begin(self):
        if self.kind == "late":
            return
        if self.kind == "share":
            self.spare[self.at] = self.own[...]
        if self.kind == "spread":
            self.keep().start()
        for n in range(1, self.z.rows):
            self.step(n).start()

    def end(self):
        for n in range(1, self.z.rows):
            self.step(n).wait()
        if self.kind == "spread":
            self.keep().wait()
        if self.kind in ("share", "late"):
            total = self.spare[0]
            for n in range(1, self.z.rows):
                total = total + self.spare[n]
            self.given[...] = total


DEEP = 4


def exchange_kernel(z, plan, steps, tile, *refs):
    groups, arrays, weights, gathers, kinds = plan
    ys, refs = refs[:arrays], refs[arrays:]
    ws, refs = refs[:weights], refs[weights:]
    extras, outs = [], []
    for group in groups:
        extras.append(refs[: group[2]])
        refs = refs[group[2] :]
    own, refs = refs[: len(kinds)], refs[len(kinds) :]
    for group in groups:
        outs.append(refs[: group[3]])
        refs = refs[group[3] :]
    if gathers:
        slots, refs = refs[0], refs[1:]
    given, refs = refs[: len(kinds)], refs[len(kinds) :]
    near, far, far_got, pair_got, relay_got, refs = *refs[:5], refs[5:]
    far_s, far_r, pair_s, pair_r, relay_s, relay_r, refs = *refs[:6], refs[6:]
    if gathers:
        block, own_s, same_s, same_r, turn_s, turn_r, part_s, part_r, refs = *refs[:8], refs[8:]
        cross_s, cross_r, refs = *refs[:2], refs[2:]
    me = lax.axis_index("col")
    partner = flip(me, 1)
    peers = [flip(me, 2 * j) for j in range(1, z.half)]
    met = [("col", device) for device in [partner] + peers]
    riders = [
        Rider(z, kind, own[n], given[n], refs[3 * n : 3 * n + 3]) for n, kind in enumerate(kinds)
    ]
    if riders:
        met = met + [("row", (riders[0].at + n) % z.rows) for n in range(1, z.rows)]
    greet(met)

    def rows_at(i):
        return pl.ds(pl.multiple_of(i * tile, tile), tile)

    def send_far(n, i):
        return remote(far.at[n, i % DEEP], far_got.at[n, i], far_s.at[n, i], far_r.at[n, i], "col", partner)

    def send_pair(n, i, j):
        return remote(
            near.at[n, i % DEEP, j], pair_got.at[n, i, j - 1], pair_s.at[n, i, j], pair_r.at[n, i, j],
            "col", peers[j - 1],
        )

    def keep(i):
        return pltpu.make_async_copy(block.at[i], slots.at[0, rows_at(i), :], own_s.at[i])

    def send_relay(n, i, side):
        part = pl.ds(side * (tile // 2), tile // 2)
        return remote(
            near.at[n, i % DEEP, 3, part], relay_got.at[n, i, side], relay_s.at[n, i, side], relay_r.at[n, i, side],
            "col", peers[side],
        )

    def send_cross(i, side):
        part = pl.ds(pl.multiple_of(i * tile + side * (tile // 2), tile // 2), tile // 2)
        return remote(
            slots.at[2 + 2 * side, part, :], slots.at[6, part, :], cross_s.at[i, side], cross_r.at[i, side],
            "col", peers[1 - side],
        )

    def send_part(i):
        return remote(block.at[i], slots.at[1, rows_at(i), :], part_s.at[i], part_r.at[i], "col", partner)

    def send_same(i, j):
        return remote(
            block.at[i], slots.at[2 * j, rows_at(i), :], same_s.at[i, j], same_r.at[i, j], "col", peers[j - 1]
        )

    def send_turn(i, j):
        return remote(
            slots.at[2 * j, rows_at(i), :], slots.at[2 * j + 1, rows_at(i), :],
            turn_s.at[i, j], turn_r.at[i, j], "col", partner,
        )

    def sent(i):
        for n in range(len(groups)):
            send_far(n, i).wait_send()
            for j in direct:
                send_pair(n, i, j).wait_send()
            for side in sides:
                send_relay(n, i, side).wait_send()

    fold = z.half == 4
    direct = (1, 2) if fold else tuple(range(1, z.half))
    sides = (0, 1) if fold else ()
    late = 1 if fold else 0
    lag = 3 + late + ((1 + late) if gathers else 0)
    loops = steps + lag - 1
    for rider in riders:
        rider.begin()

    @pl.loop(0, loops)
    def _(it):
        @pl.when((it >= DEEP) & (it < steps))
        def _():
            sent(it - DEEP)

        @pl.when(it < steps)
        def _():
            for n, group in enumerate(groups):
                terms = group[0]
                tiles = [ys[t[1]][rows_at(it), t[2] : t[3]] for t in terms]
                for side, held in ((1, far), (0, near)):
                    for j in range(z.half):
                        owner = flip(me, 2 * j + side)
                        total = sum(piece(z, t[0], y, ws[t[4]], owner) for t, y in zip(terms, tiles))
                        held[n, it % DEEP, j] = total.astype(bf16)
                    if side == 1:
                        send_far(n, it).start()

        @pl.when((it >= 1) & (it < steps + 1))
        def _():
            i = it - 1
            for n in range(len(groups)):
                send_far(n, i).wait_recv()
                for j in range(1, z.half):
                    near[n, i % DEEP, j] = (
                        near[n, i % DEEP, j].astype(f32) + far_got[n, i, j].astype(f32)
                    ).astype(bf16)
                    if not fold:
                        send_pair(n, i, j).start()
                for side in sides:
                    send_relay(n, i, side).start()

        if fold:
            @pl.when((it >= 2) & (it < steps + 2))
            def _():
                i = it - 2
                for n in range(len(groups)):
                    for side in sides:
                        send_relay(n, i, side).wait_recv()
                        at = (n, i % DEEP, 2 - side, slice(side * (tile // 2), (side + 1) * (tile // 2)))
                        near[at] = (near[at].astype(f32) + relay_got[n, i, side].astype(f32)).astype(bf16)
                        send_pair(n, i, 2 - side).start()

        @pl.when((it >= 2 + late) & (it < steps + 2 + late))
        def _():
            i = it - 2 - late
            for n, group in enumerate(groups):
                total = near[n, i % DEEP, 0].astype(f32) + far_got[n, i, 0].astype(f32)
                for j in direct:
                    send_pair(n, i, j).wait_recv()
                    total = total + pair_got[n, i, j - 1].astype(f32)
                result = group[1](rows_at(i), i, total, extras[n], outs[n])
                if gathers and n == 0:
                    block[i] = result
                    for j in direct:
                        send_same(i, j).start()
                    send_part(i).start()
                    keep(i).start()

        if gathers:
            @pl.when((it >= 3 + late) & (it < steps + 3 + late))
            def _():
                i = it - 3 - late
                for j in direct:
                    send_same(i, j).wait_recv()
                for side in sides:
                    send_cross(i, side).start()
                for j in direct:
                    send_turn(i, j).start()

            if fold:
                @pl.when(it >= 5)
                def _():
                    i = it - 5
                    for side in sides:
                        send_cross(i, side).wait_recv()
                    send_turn(i, 3).start()

    @pl.loop(max(0, steps - DEEP), steps)
    def _(i):
        sent(i)

    if gathers:
        @pl.loop(0, steps)
        def _(i):
            keep(i).wait()
            send_part(i).wait()
            for j in direct:
                send_same(i, j).wait_send()
            for side in sides:
                send_cross(i, side).wait_send()
            for j in range(1, z.half):
                send_turn(i, j).wait()

    for rider in riders:
        if rider.kind == "late":
            partial = outs[0][1]
            total = partial[0]
            for i in range(1, steps):
                total = total + partial[i]
            rider.fill(total)
    for rider in riders:
        rider.end()


def finish_middle(rows, i, total, extra, out):
    hidden, gain = extra
    middle = hidden[rows, :].astype(f32) + total
    out[0][rows, :] = middle
    return (middle * gain[...]).astype(bf16)


def finish_gradient(rows, i, total, extra, out):
    top, middle, gain, weigh = extra
    before = middle[rows, :]
    grad = top[rows, :].astype(f32) + gain[...] * total - before * weigh[rows, :]
    out[0][rows, :] = grad
    out[1][i] = jnp.sum(total * before, axis=0, keepdims=True)
    return grad.astype(bf16)


def finish_input(rows, i, total, extra, out):
    above, hidden, gain, scale, weigh = extra
    before = hidden[rows, :].astype(f32)
    scaled = scale[rows, :] * total
    out[0][rows, :] = above[rows, :] + gain[...] * scaled - before * weigh[rows, :]
    out[1][i] = jnp.sum(scaled * before, axis=0, keepdims=True)


def finish_out(rows, i, total, extra, out):
    (middle,) = extra
    out[0][rows, :] = (middle[rows, :] + total).astype(bf16)


def exchange(z, ys, ws, groups, gathers, number, riders=(), tile=STEP):
    tokens = ys[0].shape[0]
    steps = tokens // tile
    half, block, count = z.half, z.block, len(groups)
    vmem = pl.BlockSpec(memory_space=pltpu.VMEM)
    anywhere = pl.BlockSpec(memory_space=pl.ANY)
    dma = pltpu.SemaphoreType.DMA
    operands = [*ys, *ws]
    shapes = []
    for group in groups:
        operands += group[2]
        shapes += group[3]
    in_specs = [vmem] * len(operands)
    specs = [vmem] * len(shapes)
    scratch = [pltpu.VMEM((count, DEEP, half, tile, block), bf16)] * 2
    scratch += [pltpu.VMEM((count, steps, half, tile, block), bf16)]
    scratch += [pltpu.VMEM((count, steps, 2 if half == 4 else half - 1, tile, block), bf16)]
    scratch += [pltpu.VMEM((count, steps if half == 4 else 1, 2, tile // 2, block), bf16)]
    scratch += [dma((count, steps))] * 2 + [dma((count, steps, half))] * 2 + [dma((count, steps, 2))] * 2
    if gathers:
        shapes.append(jax.ShapeDtypeStruct((z.cols, tokens, block), bf16))
        specs.append(anywhere)
        scratch += [pltpu.VMEM((steps, tile, block), bf16), dma((steps,))]
        scratch += [dma((steps, half))] * 4 + [dma((steps,))] * 2 + [dma((steps, 2))] * 2
    by_row = dma((z.rows,))
    for kind, own in riders:
        operands.append(own)
        in_specs.append(vmem if kind in ("share", "late") else anywhere)
        specs.append(in_specs[-1])
        scratch += [by_row] * 2
        if kind == "spread":
            shapes.append(jax.ShapeDtypeStruct((z.rows,) + own.shape, bf16))
            scratch.append(dma(()))
        elif kind in ("share", "late"):
            shapes.append(jax.ShapeDtypeStruct(own.shape, f32))
            scratch.append(pltpu.VMEM((z.rows,) + own.shape, f32))
        else:
            part = (own.shape[0], z.shard) if kind == "deal" else (z.shard, own.shape[1])
            shapes.append(jax.ShapeDtypeStruct((z.rows - 1,) + part, bf16))
            scratch.append(dma(()))
    kinds = [(group[0], group[1], len(group[2]), len(group[3])) for group in groups]
    depth = sum(t[3] - t[2] for group in groups for t in group[0])
    return pl.pallas_call(
        functools.partial(
            exchange_kernel, z, (kinds, len(ys), len(ws), gathers, [kind for kind, _ in riders]), steps, tile
        ),
        in_specs=in_specs,
        out_specs=specs,
        out_shape=shapes,
        scratch_shapes=scratch,
        compiler_params=pltpu.CompilerParams(
            collective_id=number, has_side_effects=True, vmem_limit_bytes=60 << 20
        ),
        cost_estimate=cost(2 * tokens * z.cols * block * depth, operands, shapes),
        name="exchange",
    )(*operands)


def begin_kernel(z, count, *refs):
    owns, own, slots, whole = refs[:count], refs[count], refs[count + 1 : 2 * count + 1], refs[2 * count + 1]
    kept, same_s, same_r, part_s, part_r, turn_s, turn_r, keep_s, step_s, step_r = refs[2 * count + 2 :]
    me = lax.axis_index("col")
    partner = flip(me, 1)
    peers = [flip(me, 2 * j) for j in range(1, z.half)]
    ride = Ride(z, own, whole, keep_s, step_s, step_r)
    greet([("col", device) for device in [partner] + peers] + ride.neighbours())

    def keep(n):
        return pltpu.make_async_copy(owns[n], slots[n].at[0], kept.at[n])

    def send_same(n, j):
        return remote(owns[n], slots[n].at[2 * j], same_s.at[n, j], same_r.at[n, j], "col", peers[j - 1])

    def send_part(n):
        return remote(owns[n], slots[n].at[1], part_s.at[n], part_r.at[n], "col", partner)

    def send_turn(n, j):
        return remote(slots[n].at[2 * j], slots[n].at[2 * j + 1], turn_s.at[n, j], turn_r.at[n, j], "col", partner)

    ride.step(1).start()
    ride.keep().start()
    for n in range(count):
        for j in range(1, z.half):
            send_same(n, j).start()
        send_part(n).start()
        keep(n).start()
    for s in range(2, z.rows):
        ride.step(s - 1).wait_recv()
        ride.step(s).start()
    for n in range(count):
        for j in range(1, z.half):
            send_same(n, j).wait_recv()
            send_turn(n, j).start()
    ride.keep().wait()
    ride.step(z.rows - 1).wait_recv()
    for s in range(1, z.rows):
        ride.step(s).wait_send()
    for n in range(count):
        keep(n).wait()
        send_part(n).wait()
        for j in range(1, z.half):
            send_same(n, j).wait_send()
            send_turn(n, j).wait()


def begin(z, owns, own, number):
    anywhere = pl.BlockSpec(memory_space=pl.ANY)
    dma = pltpu.SemaphoreType.DMA
    count = len(owns)
    shapes = [jax.ShapeDtypeStruct((z.cols,) + o.shape, o.dtype) for o in owns]
    shapes.append(jax.ShapeDtypeStruct((z.rows,) + own.shape, own.dtype))
    operands = [*owns, own]
    return pl.pallas_call(
        functools.partial(begin_kernel, z, count),
        in_specs=[anywhere] * len(operands),
        out_specs=[anywhere] * len(shapes),
        out_shape=shapes,
        scratch_shapes=[dma((count,))] + [dma((count, z.half))] * 2 + [dma((count,))] * 2
        + [dma((count, z.half))] * 2 + [dma(())] + [dma((z.rows,))] * 2,
        compiler_params=pltpu.CompilerParams(collective_id=number, has_side_effects=True),
        cost_estimate=cost(10**6, operands, shapes),
        name="begin",
    )(*operands)


def rows_product(first_op, second_op):
    return lax.dot_general(
        first_op, second_op, (((0,), (0,)), ((), ())), preferred_element_type=f32
    )


def on_device(
    hidden_in,
    seg_ids,
    cotangent,
    norm_mixer,
    w_query,
    w_key,
    w_value,
    w_gate,
    w_beta,
    w_decay,
    decay_log,
    conv_query,
    conv_key,
    conv_value,
    norm_gated,
    w_out,
    norm_ffn,
    w_ffn_gate,
    w_ffn_up,
    w_ffn_down,
):
    g = Grid()
    z = Sizes(g)
    tokens = seg_ids.shape[0]
    seqs = tokens // SEQ
    heads = decay_log.shape[0]
    local = jax.ShapeDtypeStruct((tokens, g.block), f32)
    sums = jax.ShapeDtypeStruct((tokens // STEP, 1, g.block), f32)

    def by_seq(values):
        return values.reshape(seqs, SEQ, values.shape[1])

    def flat(values):
        return values.reshape(tokens, values.shape[2])

    few = 2 * heads
    ins = (w_query, w_key, w_gate)
    widths = [w.shape[1] for w in ins]
    inw = g.gather_rows(jnp.concatenate(ins, axis=1))
    wide = max(w_value.shape[1], g.shard)
    value_in = jnp.pad(w_value, ((0, 16), (0, wide - w_value.shape[1])))
    value_in = lax.dynamic_update_slice(
        value_in, jnp.concatenate([w_beta, w_decay], axis=1).T, (g.shard, 0)
    )
    ow = g.gather_rows(w_out[None])
    dw = g.gather_rows(w_ffn_down[None])
    ew = g.gather_rows(w_ffn_gate)
    own_gains = jnp.stack([norm_mixer, norm_ffn])
    own_gains = jnp.pad(own_gains, ((0, 6), (0, 0)))
    blocks, tops, gains, vw = begin(z, [hidden_in, cotangent, own_gains], value_in, 3)
    order = jnp.arange(g.cols) ^ g.me
    gains = jnp.swapaxes(jnp.take(gains[:, :2], order, axis=0), 0, 1).reshape(2, D)

    normed, scale_mixer, pq, pk, pg, pv, proj_small = project(g, blocks, gains[:1], inw, vw, widths, few)
    up_own, _ = lax.optimization_barrier((w_ffn_up, proj_small))
    uw = g.spread(up_own)
    projected = [by_seq(p) for p in (pq, pk, pv, pg)]
    proj_beta, proj_decay = proj_small[:heads], proj_small[heads:]
    strength = jax.nn.sigmoid(proj_beta)
    rate = -jnp.exp(decay_log)[:, None]
    log_decay = rate * jax.nn.softplus(proj_decay)
    rows, cols = token_tables(seg_ids, strength, log_decay)
    gain_gated = norm_gated[None]
    gated, inv, upd, states = mixer_forward(
        *projected, cols, rows, conv_query, conv_key, conv_value, gain_gated
    )
    gated = flat(gated)
    middle, mids = exchange(
        z, [gated], [ow],
        [([("cols", 0, 0, gated.shape[1], 0)], finish_middle, [hidden_in, norm_ffn[None]], [local])],
        True, 0,
    )
    undo = 1.0 / (gains[1:] * gains[1:])
    tops = lax.optimization_barrier((tops, middle))[0]
    tr, grad_inner = inner_gradient(g, tops, dw)
    mids = lax.optimization_barrier((mids, grad_inner))[0]
    xr, inner, dgate, dup, weigh, scale_ffn = ffn(g, mids, grad_inner, undo, ew, uw)
    weigh = weigh[:, 0]
    wide = [rows_product(xr, dgate).astype(bf16)]
    weigh = weigh + g.swap(weigh, "col", 1)
    weigh, left = lax.optimization_barrier((weigh, dup))
    wide.append(rows_product(xr, left).astype(bf16))
    weigh = weigh + g.swap(weigh, "col", 2)
    weigh, left = lax.optimization_barrier((weigh, inner))
    wide.append(rows_product(left, tr).astype(bf16))
    bits = 4
    while bits < g.cols:
        weigh = weigh + g.swap(weigh, "col", bits)
        bits *= 2
    weigh = scale_ffn * scale_ffn * weigh[:, None] / D
    weigh = lax.optimization_barrier((weigh, *wide))[0]
    gate_grad, up_grad, down_grad = (g.sum_rows(w, axis) for w, axis in zip(wide, (0, 0, 1)))
    hidden_units = dgate.shape[1]
    grad_middle, norm_sums, downs = exchange(
        z, [dgate, dup], [ew, uw],
        [(
            [("rows", 0, 0, hidden_units, 0), ("ring_rows", 1, 0, hidden_units, 1)], finish_gradient,
            [cotangent, middle, norm_ffn[None], weigh], [local, sums],
        )],
        True, 1,
    )
    grad_norm_ffn = jnp.sum(norm_sums, axis=(0, 1))
    mr, grad_gated = back_gate(g, downs, ow)
    out_term = rows_product(gated, mr).astype(bf16)
    grad_gated = lax.optimization_barrier((grad_gated, out_term))[0]
    out_term, up_grad = lax.optimization_barrier((out_term, up_grad))
    out_grad = g.sum_rows(out_term, 1)
    dproj, dcols, dwq, dwk, dwv, dgain = mixer_backward(
        by_seq(grad_gated), *projected, cols, rows, inv, upd, states,
        conv_query, conv_key, conv_value, gain_gated,
    )
    dproj = flat(dproj)
    most = sum(widths)
    in_grads = g.sum_rows(rows_product(normed, dproj).astype(bf16), 0)
    dsmall = flat(dcols).T
    dstrength, dlog = dsmall[:heads], dsmall[heads:few]
    grad_small = jnp.concatenate(
        [dstrength * strength * (1.0 - strength), dlog * rate * jax.nn.sigmoid(proj_decay)], axis=0
    )
    weigh = g.total(dsmall[few] + jnp.sum(grad_small * proj_small, axis=0), "col")[:, None]
    weigh = scale_mixer * scale_mixer * weigh / D
    grad_small = grad_small.astype(bf16)
    small_grads = jnp.dot(grad_small, normed, preferred_element_type=f32)
    grad_decay_log = jnp.sum(dlog * log_decay, axis=1)
    pieces = [dwq, dwk, dwv, dgain, grad_norm_ffn, grad_decay_log, small_grads]
    count = sum(p.size for p in pieces)
    fill = jnp.zeros((-count % 1024,), f32)
    joined = jnp.concatenate([p.reshape(-1) for p in pieces] + [fill]).reshape(-1, 128)
    grad_input, _, block_out, joined, grad_norm_mixer = exchange(
        z, [dproj, grad_small.T, inner], [inw, vw, dw],
        [
            (
                [("rows", 0, 0, most, 0), ("shards", 0, most, dproj.shape[1], 1), ("small", 1, 0, few, 1)],
                finish_input, [grad_middle, hidden_in, norm_mixer[None], scale_mixer, weigh], [local, sums],
            ),
            (
                [("cols", 2, 0, hidden_units, 2)], finish_out, [middle],
                [jax.ShapeDtypeStruct((tokens, g.block), bf16)],
            ),
        ],
        False, 2, [("share", joined), ("late", jnp.zeros((8, g.block), f32))],
    )
    joined = joined.reshape(-1)
    grad_norm_mixer = grad_norm_mixer[0]
    summed, at = [], 0
    for p in pieces:
        summed.append(joined[at : at + p.size].reshape(p.shape))
        at += p.size
    small_grads = lax.dynamic_slice(summed[6], (0, g.at * g.shard), (few, g.shard)).T
    grads, at = [], 0
    for w in widths + [w_value.shape[1]]:
        grads.append(in_grads[:, at : at + w].astype(f32))
        at += w
    return (
        block_out,
        grad_input,
        grad_norm_mixer,
        grads[0],
        grads[1],
        grads[3],
        grads[2],
        small_grads[:, :heads],
        small_grads[:, heads:],
        summed[5],
        summed[0],
        summed[1],
        summed[2],
        summed[3][0],
        out_grad.astype(f32),
        summed[4],
        gate_grad.astype(f32),
        up_grad.astype(f32),
        down_grad.astype(f32),
    )


def solution(mesh):
    placed = (
        P("row", "col"),
        P("row"),
        P("row", "col"),
        P("col"),
        P("row", "col"),
        P("row", "col"),
        P("row", "col"),
        P("row", "col"),
        P("row", "col"),
        P("row", "col"),
        P("col"),
        P(None, "col"),
        P(None, "col"),
        P(None, "col"),
        P("col"),
        P("col", "row"),
        P("col"),
        P("row", "col"),
        P("row", "col"),
        P("col", "row"),
    )
    return jax.shard_map(
        on_device,
        mesh=mesh,
        in_specs=placed,
        out_specs=(
            P("row", "col"),
            P("row", "col"),
            P("col"),
            P("row", "col"),
            P("row", "col"),
            P("row", "col"),
            P("row", "col"),
            P("row", "col"),
            P("row", "col"),
            P("col"),
            P(None, "col"),
            P(None, "col"),
            P(None, "col"),
            P("col"),
            P("col", "row"),
            P("col"),
            P("row", "col"),
            P("row", "col"),
            P("col", "row"),
        ),
        check_vma=False,
    )
```

```python
import functools

import jax
import jax.numpy as jnp
from jax import lax
from jax.experimental import pallas as pl
from jax.experimental.pallas import tpu as pltpu
from jax.sharding import PartitionSpec as P

D = 2048
DK = 128
DV = 256
CONV = 4
SEQ = 1024
CHUNK = 128
EPSILON = 1e-06
SCALE = DK ** (-0.5)
f32 = jnp.float32
bf16 = jnp.bfloat16


def mm(a, b, dims=((1,), (0,))):
    return lax.dot_general(a, b, (dims, ((), ())), preferred_element_type=f32)


def split(a):
    hi = a.astype(bf16)
    return hi, (a - hi.astype(f32)).astype(bf16)


def mm3(a, b):
    ah, al = split(a)
    bh, bl = split(b)
    return mm(ah, bh) + (mm(ah, bl) + mm(al, bh))


def sigmoid(u):
    return 1.0 / (1.0 + jnp.exp(-u))


def iotas(n):
    return (
        lax.broadcasted_iota(jnp.int32, (n, n), 0),
        lax.broadcasted_iota(jnp.int32, (n, n), 1),
    )


def unit_lower_inverses(many, row, col):
    n = many[0].shape[0]
    eye = (row == col).astype(f32)
    base = 8
    inside = row // base == col // base
    ds = [jnp.where(inside, a, 0.0) for a in many]
    squares = [mm3(d, d) for d in ds]
    xs = [eye - d for d in ds]
    xs = [x + mm3(x, d) for x, d in zip(xs, squares)]
    fourths = [mm3(d, d) for d in squares]
    xs = [x + mm3(x, d) for x, d in zip(xs, fourths)]
    size = base
    while size < n:
        at = (row // (2 * size) == col // (2 * size)) & (row // size != col // size)
        offs = [jnp.where(at, a, 0.0).astype(bf16) for a in many]
        highs = [x.astype(bf16) for x in xs]
        steps = [mm(off, x).astype(bf16) for off, x in zip(offs, highs)]
        xs = [x - mm(h, step) for x, h, step in zip(xs, highs, steps)]
        size *= 2
    return xs


def conv_taps(buf, s, width, weights, masks):
    pre = weights[0:1] * buf[s, 8 : 8 + CHUNK, :]
    for j in range(1, CONV):
        pre = pre + weights[j : j + 1] * buf[s, 8 - j : 8 - j + CHUNK, :] * masks[j - 1]
    return pre


def forward_kernel(heads, seqs, pq, pk, pv, pg, cols, rows, wq, wk, wv, gain,
                   gated, inv_out, upd_out, state_out, state, bq, bk, bv):
    step = pl.program_id(0)

    @pl.when(step == 0)
    def _():
        state[...] = jnp.zeros_like(state)
        for buf in (bq, bk, bv):
            buf[:, 0:8, :] = jnp.zeros_like(buf[:, 0:8, :])

    row, col = iotas(CHUNK)
    lower = row >= col
    tril = lower.astype(bf16)
    chains = []
    for s in range(seqs):
        cc = cols[s]
        rr = rows[s]
        masks = [cc[:, j : j + 1] for j in range(CONV - 1)]
        ch, cl = split(cc)
        csum = mm(tril, ch) + mm(tril, cl)
        rh, rl = split(rr)
        rsum = mm(rh, tril, ((1,), (1,))) + mm(rl, tril, ((1,), (1,)))
        same = (cc[:, 6:7] == rr[6:7, :]) & lower
        for src, buf in ((pq, bq), (pk, bk), (pv, bv)):
            buf[s, 8 : 8 + CHUNK, :] = src[s]
        cq = conv_taps(bq, s, heads * DK, wq, masks)
        ck = conv_taps(bk, s, heads * DK, wk, masks)
        cv = conv_taps(bv, s, heads * DV, wv, masks)
        for buf in (bq, bk, bv):
            buf[s, 0:8, :] = buf[s, CHUNK : CHUNK + 8, :]
        aq = cq * sigmoid(cq)
        ak = ck * sigmoid(ck)
        av = cv * sigmoid(cv)
        for h in range(heads):
            keys = slice(h * DK, (h + 1) * DK)
            vals = slice(h * DV, (h + 1) * DV)
            q = aq[:, keys]
            q = (q * lax.rsqrt(jnp.sum(q * q, axis=1, keepdims=True) + EPSILON)).astype(bf16)
            k = ak[:, keys]
            k = (k * lax.rsqrt(jnp.sum(k * k, axis=1, keepdims=True) + EPSILON)).astype(bf16)
            v = av[:, vals].astype(bf16).astype(f32)
            beta = cc[:, 8 + h : 9 + h]
            at = 8 + heads + h
            gcol = csum[:, at : at + 1]
            grow = rsum[at : at + 1, :]
            decay = jnp.where(same, jnp.exp(jnp.minimum(gcol - grow, 0.0)), 0.0)
            start = jnp.exp(gcol) * cc[:, 7:8]
            end = jnp.exp(jnp.minimum(gcol[CHUNK - 1 :, :] - gcol, 0.0)) * jnp.where(
                cc[:, 6:7] == cc[CHUNK - 1 :, 6:7], 1.0, 0.0
            )
            kk = mm(k, k, ((1,), (1,)))
            scores = (decay * mm(q, k, ((1,), (1,)))).astype(bf16)
            coupling = jnp.where(row > col, beta * decay * kk, 0.0)
            kend = (end * k.astype(f32)).astype(bf16)
            chains.append((s, h, vals, q, k, v, beta, start, scores, kend, coupling))
    inverses = unit_lower_inverses([c[-1] for c in chains], row, col)
    inverses = [x.astype(bf16) for x in inverses]
    begins = [state[c[0], c[1]] for c in chains]
    lows = [x.astype(bf16) for x in begins]
    rights = []
    for (s, h, vals, q, k, v, beta, start, scores, kend, _), inv, begin, low in zip(chains, inverses, begins, lows):
        inv_out[s, h] = inv
        state_out[0, s, h] = begin
        rights.append((beta * (v - start * mm(k, low))).astype(bf16))
    upds = [mm(inv, right).astype(bf16) for inv, right in zip(inverses, rights)]
    for (s, h, vals, q, k, v, beta, start, scores, kend, _), begin, low, upd in zip(chains, begins, lows, upds):
        upd_out[s, :, vals] = upd
        state[s, h] = start[CHUNK - 1 :, :] * begin + mm(kend, upd, ((0,), (0,)))
        mixed = (start * mm(q, low) + mm(scores, upd)) * SCALE
        gate = pg[s, :, vals]
        scaled = mixed * lax.rsqrt(jnp.mean(mixed * mixed, axis=1, keepdims=True) + EPSILON)
        gated[s, :, vals] = (scaled * gain[:, vals] * (gate * sigmoid(gate))).astype(bf16)


def backward_kernel(heads, seqs, dgated, pq, pk, pv, pg, hq, hk, hv, cols, rows, inv_in, upd_in, state_in,
                    wq, wk, wv, gain,
                    dproj, dcols, dwq, dwk, dwv, dgain,
                    dstate, bq, bk, bv, tq, tk, tv):
    step = pl.program_id(0)

    @pl.when(step == 0)
    def _():
        dstate[...] = jnp.zeros_like(dstate)
        for buf in (tq, tk, tv):
            buf[:, CHUNK : CHUNK + 8, :] = jnp.zeros_like(buf[:, CHUNK : CHUNK + 8, :])
        for out in (dwq, dwk, dwv, dgain):
            out[...] = jnp.zeros_like(out)

    row, col = iotas(CHUNK)
    lower = row >= col
    tril = lower.astype(bf16)
    lane = lax.broadcasted_iota(jnp.int32, (CHUNK, 2 * heads + 1), 1)
    last = lax.broadcasted_iota(jnp.int32, (CHUNK, 1), 0) == CHUNK - 1
    shared = []
    for s in range(seqs):
        cc = cols[s]
        rr = rows[s]
        masks = [cc[:, j : j + 1] for j in range(CONV - 1)]
        ch, cl = split(cc)
        csum = mm(tril, ch) + mm(tril, cl)
        rh, rl = split(rr)
        rsum = mm(rh, tril, ((1,), (1,))) + mm(rl, tril, ((1,), (1,)))
        same = (cc[:, 6:7] == rr[6:7, :]) & lower
        pres = []
        for src, halo, buf, weights in ((pq, hq, bq, wq), (pk, hk, bk, wk), (pv, hv, bv, wv)):
            buf[s, 0:8, :] = halo[s]
            buf[s, 8 : 8 + CHUNK, :] = src[s]
            pres.append(conv_taps(buf, s, None, weights, masks))
        sigs = [sigmoid(pre) for pre in pres]
        acts = [pre * sig for pre, sig in zip(pres, sigs)]
        shared.append((cc, masks, csum, rsum, same, pres, sigs, acts))
    found = {}

    def chain(s, h):
        cc, _, csum, rsum, same, pres, sigs, acts = shared[s]
        keys = slice(h * DK, (h + 1) * DK)
        vals = slice(h * DV, (h + 1) * DV)
        q = acts[0][:, keys]
        rq = lax.rsqrt(jnp.sum(q * q, axis=1, keepdims=True) + EPSILON)
        qn = q * rq
        q = qn.astype(bf16)
        k = acts[1][:, keys]
        rk = lax.rsqrt(jnp.sum(k * k, axis=1, keepdims=True) + EPSILON)
        kn = k * rk
        k = kn.astype(bf16)
        v = acts[2][:, vals].astype(bf16).astype(f32)
        beta = cc[:, 8 + h : 9 + h]
        at = 8 + heads + h
        gcol = csum[:, at : at + 1]
        grow = rsum[at : at + 1, :]
        decay = jnp.where(same, jnp.exp(jnp.minimum(gcol - grow, 0.0)), 0.0)
        start = jnp.exp(gcol) * cc[:, 7:8]
        end = jnp.exp(jnp.minimum(gcol[CHUNK - 1 :, :] - gcol, 0.0)) * jnp.where(
            cc[:, 6:7] == cc[CHUNK - 1 :, 6:7], 1.0, 0.0
        )
        begin = state_in[0, s, h]
        low = begin.astype(bf16)
        inv = inv_in[s, h]
        upd = upd_in[s, :, vals]
        ds = dstate[s, h]
        dsl = ds.astype(bf16)
        kf = k.astype(f32)
        kend = (end * kf).astype(bf16)
        kk = mm(k, k, ((1,), (1,)))
        qk = mm(q, k, ((1,), (1,)))
        ks = mm(k, low)
        qs = mm(q, low)
        uds = mm(upd, dsl, ((1,), (1,)))
        kds = mm(kend, dsl)
        yield
        plain = jnp.where(row > col, decay * kk, 0.0)
        scores = decay * qk
        scores_low = scores.astype(bf16)
        mixed = (start * qs + mm(scores_low, upd)) * SCALE
        yield
        gate = pg[s, :, vals]
        sg = sigmoid(gate)
        silu = gate * sg
        rm = lax.rsqrt(jnp.mean(mixed * mixed, axis=1, keepdims=True) + EPSILON)
        scaled = mixed * rm
        dy = dgated[s, :, vals]
        dyn = dy * scaled
        gains = gain[:, vals]
        dgain[:, vals] += jnp.sum(dyn * silu, axis=0, keepdims=True)
        dgate = dyn * gains * (sg * (1.0 + gate * (1.0 - sg)))
        dproj[s, :, 2 * heads * DK + h * DV : 2 * heads * DK + (h + 1) * DV] = dgate.astype(bf16)
        weigh = jnp.sum(dgate * gate, axis=1, keepdims=True)
        dscaled = dy * gains * silu
        dmixed = rm * (dscaled - scaled * jnp.mean(dscaled * scaled, axis=1, keepdims=True))
        dout = dmixed * SCALE
        dlow = dout.astype(bf16)
        dupd = mm(scores_low, dlow, ((0,), (0,))) + kds
        dscore = mm(dlow, upd, ((1,), (1,)))
        dqs = mm(dlow, low, ((1,), (1,)))
        dfirst = mm((start * q.astype(f32)).astype(bf16), dlow, ((0,), (0,)))
        yield
        dright = mm(inv, dupd.astype(bf16), ((0,), (0,)))
        dsc = (dscore * decay).astype(bf16)
        dqn = start * dqs + mm(dsc, k)
        dkn = end * uds + mm(dsc, q, ((0,), (0,)))
        yield
        drl = dright.astype(bf16)
        dcoup = -mm(drl, upd, ((1,), (1,)))
        w = beta * dright
        wa = (start * w).astype(bf16)
        dkn = dkn - mm(wa, low, ((1,), (1,)))
        final = start[CHUNK - 1 :, :]
        dstate[s, h] = dfirst + final * ds - mm(k, wa, ((0,), (0,)))
        yield
        g = jnp.where(row > col, beta * dcoup * decay, 0.0)
        dkn = dkn + mm((g + g.T).astype(bf16), k)
        dbeta = jnp.sum(dright * (v - start * ks), axis=1, keepdims=True) + jnp.sum(
            dcoup * plain, axis=1, keepdims=True
        )
        dstart = jnp.sum(dout * qs - w * ks, axis=1, keepdims=True)
        dend = jnp.sum(kf * uds, axis=1, keepdims=True) * end
        z = dscore * scores + dcoup * (beta * plain)
        carried = jnp.sum(jnp.sum(ds * begin, axis=1, keepdims=True), axis=0, keepdims=True) * final
        carried = carried + jnp.sum(dend, axis=0, keepdims=True)
        dg = jnp.sum(z - z.T, axis=1, keepdims=True) + dstart * start - dend
        dg = dg + jnp.where(last, carried, 0.0)
        found[s, h] = (dbeta, dg, weigh)
        yield
        dq = rq * (dqn - qn * jnp.sum(dqn * qn, axis=1, keepdims=True))
        dk = rk * (dkn - kn * jnp.sum(dkn * kn, axis=1, keepdims=True))
        for grad, n, buf, part in ((dq, 0, tq, keys), (dk, 1, tk, keys), (w, 2, tv, vals)):
            sig = sigs[n][:, part]
            buf[s, 0:CHUNK, part] = grad * (sig * (1.0 + pres[n][:, part] * (1.0 - sig)))

    chains = [chain(s, h) for s in range(seqs) for h in range(heads)]
    while chains:
        chains = [c for c in chains if next(c, chains) is None]

    kw, vw = heads * DK, heads * DV
    for s in range(seqs):
        cc, masks = shared[s][:2]
        ahead = [cc[:, 3 + j : 4 + j] for j in range(CONV - 1)]
        dcol = jnp.zeros((CHUNK, 2 * heads + 1), f32)
        weigh = jnp.zeros((CHUNK, 1), f32)
        for h in range(heads):
            dbeta, dg, more = found[s, h]
            dcol = dcol + jnp.where(lane == h, dbeta, 0.0) + jnp.where(lane == heads + h, dg, 0.0)
            weigh = weigh + more
        dh, dl = split(dcol)
        dl2 = (dcol - dh.astype(f32) - dl.astype(f32)).astype(bf16)
        tail = ((0,), (0,))
        rev = mm(tril, dh, tail) + (mm(tril, dl, tail) + mm(tril, dl2, tail))
        for buf, src, at, weights, dw in ((tq, bq, 0, wq, dwq), (tk, bk, kw, wk, dwk), (tv, bv, 2 * kw + vw, wv, dwv)):
            pre = buf[s, 0:CHUNK, :]
            total = weights[0:1] * pre
            dw[0:1, :] += jnp.sum(pre * src[s, 8 : 8 + CHUNK, :], axis=0, keepdims=True)
            for j in range(1, CONV):
                total = total + weights[j : j + 1] * buf[s, j : j + CHUNK, :] * ahead[j - 1]
                dw[j : j + 1, :] += jnp.sum(
                    pre * masks[j - 1] * src[s, 8 - j : 8 - j + CHUNK, :], axis=0, keepdims=True
                )
            dproj[s, :, at : at + total.shape[1]] = total.astype(bf16)
            weigh = weigh + jnp.sum(total * src[s, 8 : 8 + CHUNK, :], axis=1, keepdims=True)
            buf[s, CHUNK : CHUNK + 8, :] = buf[s, 0:8, :]
        dcols[s] = jnp.where(lane < heads, dcol, jnp.where(lane < 2 * heads, rev, weigh))


def whole(shape):
    return pl.BlockSpec(shape, lambda c: (0,) * len(shape))


def mixer_forward(pq, pk, pv, pg, cols, rows, wq, wk, wv, gain):
    seqs = pq.shape[0]
    heads = pq.shape[2] // DK
    steps = SEQ // CHUNK
    kw, vw = heads * DK, heads * DV

    def tok(width):
        return pl.BlockSpec((seqs, CHUNK, width), lambda c: (0, c, 0))

    return pl.pallas_call(
        functools.partial(forward_kernel, heads, seqs),
        grid=(steps,),
        in_specs=[tok(kw), tok(kw), tok(vw), tok(vw), tok(cols.shape[2]),
                  pl.BlockSpec((seqs, rows.shape[1], CHUNK), lambda c: (0, 0, c)),
                  whole((CONV, kw)), whole((CONV, kw)), whole((CONV, vw)), whole((1, vw))],
        out_specs=[tok(vw),
                   pl.BlockSpec((seqs, heads, CHUNK, CHUNK), lambda c: (0, 0, c, 0)),
                   tok(vw),
                   pl.BlockSpec((1, seqs, heads, DK, DV), lambda c: (c, 0, 0, 0, 0))],
        out_shape=[jax.ShapeDtypeStruct((seqs, SEQ, vw), bf16),
                   jax.ShapeDtypeStruct((seqs, heads, SEQ, CHUNK), bf16),
                   jax.ShapeDtypeStruct((seqs, SEQ, vw), bf16),
                   jax.ShapeDtypeStruct((steps, seqs, heads, DK, DV), f32)],
        scratch_shapes=[pltpu.VMEM((seqs, heads, DK, DV), f32),
                        pltpu.VMEM((seqs, 8 + CHUNK, kw), f32),
                        pltpu.VMEM((seqs, 8 + CHUNK, kw), f32),
                        pltpu.VMEM((seqs, 8 + CHUNK, vw), f32)],
        compiler_params=pltpu.CompilerParams(dimension_semantics=("arbitrary",), vmem_limit_bytes=48 << 20),
        name="mixer_forward",
    )(pq, pk, pv, pg, cols, rows, wq, wk, wv, gain)


def mixer_backward(dgated, pq, pk, pv, pg, cols, rows, inv, upd, states, wq, wk, wv, gain):
    seqs = pq.shape[0]
    heads = pq.shape[2] // DK
    steps = SEQ // CHUNK
    kw, vw = heads * DK, heads * DV

    def tok(width):
        return pl.BlockSpec((seqs, CHUNK, width), lambda c: (0, steps - 1 - c, 0))

    def halo(width):
        return pl.BlockSpec(
            (seqs, 8, width),
            lambda c: (0, jnp.maximum((steps - 1 - c) * (CHUNK // 8) - 1, 0), 0),
        )

    return pl.pallas_call(
        functools.partial(backward_kernel, heads, seqs),
        grid=(steps,),
        in_specs=[tok(vw), tok(kw), tok(kw), tok(vw), tok(vw), halo(kw), halo(kw), halo(vw), tok(cols.shape[2]),
                  pl.BlockSpec((seqs, rows.shape[1], CHUNK), lambda c: (0, 0, steps - 1 - c)),
                  pl.BlockSpec((seqs, heads, CHUNK, CHUNK), lambda c: (0, 0, steps - 1 - c, 0)),
                  tok(vw),
                  pl.BlockSpec((1, seqs, heads, DK, DV), lambda c: (steps - 1 - c, 0, 0, 0, 0)),
                  whole((CONV, kw)), whole((CONV, kw)), whole((CONV, vw)), whole((1, vw))],
        out_specs=[tok(2 * kw + 2 * vw), tok(2 * heads + 1),
                   whole((CONV, kw)), whole((CONV, kw)), whole((CONV, vw)), whole((1, vw))],
        out_shape=[jax.ShapeDtypeStruct((seqs, SEQ, 2 * kw + 2 * vw), bf16),
                   jax.ShapeDtypeStruct((seqs, SEQ, 2 * heads + 1), f32),
                   jax.ShapeDtypeStruct((CONV, kw), f32),
                   jax.ShapeDtypeStruct((CONV, kw), f32),
                   jax.ShapeDtypeStruct((CONV, vw), f32),
                   jax.ShapeDtypeStruct((1, vw), f32)],
        scratch_shapes=[pltpu.VMEM((seqs, heads, DK, DV), f32)]
        + [pltpu.VMEM((seqs, 8 + CHUNK, width), f32) for width in (kw, kw, vw)] * 2,
        compiler_params=pltpu.CompilerParams(dimension_semantics=("arbitrary",), vmem_limit_bytes=56 << 20),
        name="mixer_backward",
    )(dgated, pq, pk, pv, pg, pq, pk, pv, cols, rows, inv, upd, states, wq, wk, wv, gain)


def token_tables(seg_ids, strength, log_decay):
    seqs = seg_ids.shape[0] // SEQ
    seg = seg_ids.reshape(seqs, 1, SEQ)
    position = lax.broadcasted_iota(jnp.int32, (1, 1, SEQ), 2)
    back, ahead = [], []
    for j in range(1, CONV):
        same = seg[:, :, j:] == seg[:, :, : SEQ - j]
        none = jnp.zeros((seqs, 1, j), jnp.bool_)
        back.append(jnp.concatenate([none, same], axis=2))
        ahead.append(jnp.concatenate([same, none], axis=2))
    before = jnp.concatenate([jnp.full((seqs, 1, 1), -1, jnp.int32), seg[:, :, CHUNK - 1 : SEQ - 1 : CHUNK]], axis=2)
    carry = seg == jnp.repeat(before, CHUNK, axis=2)
    heads = strength.shape[0]
    tables = [m.astype(f32) for m in back + ahead] + [seg.astype(f32), carry.astype(f32)]
    tables += [
        jnp.swapaxes(strength.reshape(heads, seqs, SEQ), 0, 1),
        jnp.swapaxes(log_decay.reshape(heads, seqs, SEQ), 0, 1),
    ]
    pad = 16 - 8 - 2 * heads
    if pad:
        tables.append(jnp.zeros((seqs, pad, SEQ), f32))
    rows = jnp.concatenate(tables, axis=1)
    return rows, jnp.swapaxes(rows, 1, 2)

TILE = 256
STEP = 256
MESH = pl.DeviceIdType.MESH


def flip(value, bits):
    bit = 1
    while bit <= bits:
        if bits & bit:
            value = value + bit - 2 * bit * ((value // bit) % 2)
        bit *= 2
    return value


class Grid:
    def __init__(self):
        self.rows = lax.axis_size("row")
        self.cols = lax.axis_size("col")
        self.shard = D // self.rows
        self.block = D // self.cols
        self.parts = self.cols // self.rows
        self.half = self.cols // 2
        self.me = lax.axis_index("col")
        self.at = lax.axis_index("row")
        self.ids = jnp.stack([self.me, self.at]).astype(jnp.int32)
        self.slots = list(range(0, self.cols, 2)) + list(range(1, self.cols, 2))

    def swap(self, values, axis, bits):
        count = self.rows if axis == "row" else self.cols
        return lax.ppermute(values, axis, [(i, i ^ bits) for i in range(count)])

    def total(self, values, axis):
        bits = 1
        while bits < (self.rows if axis == "row" else self.cols):
            values = values + self.swap(values, axis, bits)
            bits *= 2
        return values

    def spread(self, values):
        return jnp.stack(
            [values]
            + [
                lax.ppermute(values, "row", [(i, (i + n) % self.rows) for i in range(self.rows)])
                for n in range(1, self.rows)
            ]
        )

    def gather_rows(self, values):
        return lax.all_gather(values, "row", axis=0, tiled=True)

    def sum_rows(self, term, axis):
        return lax.psum_scatter(term, "row", scatter_dimension=axis, tiled=True)


def fixed(array):
    return pl.BlockSpec(array.shape, lambda i, ids: (0,) * array.ndim, pipeline_mode=pl.Buffered(1))


def tokens_of(width, tile=TILE):
    return pl.BlockSpec((tile, width), lambda i, ids: (i, 0))


def slots_of(g):
    return pl.BlockSpec((g.cols, TILE, g.block), lambda i, ids: (0, i, 0))


def cost(flops, operands, outs):
    moved = sum(o.size * o.dtype.itemsize for o in operands)
    moved += sum(o.size * o.dtype.itemsize for o in outs)
    return pl.CostEstimate(flops=flops, bytes_accessed=moved, transcendentals=0)


def launch(kernel, grid, ids, operands, in_specs, out_specs, out_shape, scratch, name, flops):
    return pl.pallas_call(
        kernel,
        grid_spec=pltpu.PrefetchScalarGridSpec(
            num_scalar_prefetch=1, grid=grid, in_specs=in_specs, out_specs=out_specs, scratch_shapes=scratch
        ),
        out_shape=out_shape,
        compiler_params=pltpu.CompilerParams(
            dimension_semantics=("arbitrary",) * len(grid), vmem_limit_bytes=56 << 20
        ),
        cost_estimate=cost(flops, operands, out_shape),
        name=name,
    )(ids, *operands)


def place(g, ids, k):
    return pl.multiple_of((ids[0] ^ k) * g.block, g.block)


def dot_back(g, x, weights):
    return sum(
        mm(x[:, s * g.shard : (s + 1) * g.shard], weights[s], ((1,), (1,))) for s in range(g.rows)
    )


def ring_dot(g, ids, x, weights):
    total = 0.0
    for s in range(g.rows):
        shard = lax.rem(ids[1] - s + g.rows, g.rows)
        part = pl.ds(pl.multiple_of(shard * g.shard, g.shard), g.shard)
        total = total + mm(x[:, part], weights[s])
    return total


def project_kernel(g, widths, few, ids, blocks, gain, weight, ring, normed, scale, pq, pk, pg, pv, small):
    values = [blocks[k].astype(f32) for k in g.slots]
    squares = sum(jnp.sum(v * v, axis=1, keepdims=True) for v in values)
    scales = lax.rsqrt(squares / D + EPSILON)
    scale[...] = scales
    for k, v in zip(g.slots, values):
        at = place(g, ids, k)
        normed[:, pl.ds(at, g.block)] = (v * scales * gain[:, pl.ds(at, g.block)]).astype(bf16)
    x = normed[...]
    at = 0
    for out, width in zip((pq, pk, pg), widths):
        out[...] = mm(x, weight[:, at : at + width])
        at += width
    parts = [x[:, r * g.shard : (r + 1) * g.shard] for r in range(g.rows)]
    pv[...] = sum(mm(p, ring[r, : g.shard, :]) for r, p in enumerate(parts))
    small[...] = sum(
        mm(ring[r, g.shard : g.shard + few, : g.shard], p, ((1,), (1,))) for r, p in enumerate(parts)
    )


def project(g, blocks, gains, weight, ring, widths, few):
    tokens = blocks.shape[1]
    last = ring.shape[2]
    return launch(
        functools.partial(project_kernel, g, widths, few),
        (tokens // TILE,),
        g.ids,
        [blocks, gains, weight, ring],
        [slots_of(g)] + [fixed(w) for w in (gains, weight, ring)],
        [tokens_of(D), tokens_of(1)]
        + [tokens_of(w) for w in widths + [last]]
        + [pl.BlockSpec((few, TILE), lambda i, ids: (0, i))],
        [jax.ShapeDtypeStruct((tokens, D), bf16), jax.ShapeDtypeStruct((tokens, 1), f32)]
        + [jax.ShapeDtypeStruct((tokens, w), f32) for w in widths + [last]]
        + [jax.ShapeDtypeStruct((few, tokens), f32)],
        [],
        "project",
        2 * tokens * D * (sum(widths) + last + few),
    )


def ffn_kernel(g, ids, xs, ts, undo, wg, wu, xr, tr, gate_out, up_out, inner, scale):
    squares = 0.0
    for k in g.slots:
        at = place(g, ids, k)
        x = xs[k]
        xr[:, pl.ds(at, g.block)] = x
        tr[:, pl.ds(at, g.block)] = ts[k]
        v = x.astype(f32)
        squares = squares + jnp.sum(v * v * undo[:, pl.ds(at, g.block)], axis=1, keepdims=True)
    scales = lax.rsqrt(squares / D + EPSILON)
    scale[...] = scales
    gate = mm(xr[...], wg[...]) * scales
    up = ring_dot(g, ids, xr, wu) * scales
    gate_out[...] = gate
    up_out[...] = up
    inner[...] = (gate * sigmoid(gate) * up).astype(bf16)


def ffn(g, xs, ts, undo, wg, wu):
    tokens = xs.shape[1]
    width = wg.shape[1]
    return launch(
        functools.partial(ffn_kernel, g),
        (tokens // TILE,),
        g.ids,
        [xs, ts, undo, wg, wu],
        [slots_of(g)] * 2 + [fixed(w) for w in (undo, wg, wu)],
        [tokens_of(D)] * 2 + [tokens_of(width)] * 3 + [tokens_of(1)],
        [jax.ShapeDtypeStruct((tokens, D), bf16)] * 2
        + [jax.ShapeDtypeStruct((tokens, width), f32)] * 2
        + [jax.ShapeDtypeStruct((tokens, width), bf16), jax.ShapeDtypeStruct((tokens, 1), f32)],
        [],
        "ffn",
        4 * tokens * D * width,
    )


def ffn_back_kernel(g, ids, tr, gates, ups, scale, wd, dgate, dup, total):
    scales = scale[...]
    grad = dot_back(g, tr, wd)
    gate = gates[...]
    up = ups[...]
    sig = sigmoid(gate)
    dg = grad * up * (sig * (1.0 + gate * (1.0 - sig)))
    du = grad * gate * sig
    total[...] = jnp.sum(dg * gate + du * up, axis=1, keepdims=True)
    dgate[...] = (dg * scales).astype(bf16)
    dup[...] = (du * scales).astype(bf16)


def ffn_back(g, tr, gates, ups, scale, wd):
    tokens = tr.shape[0]
    width = gates.shape[1]
    return launch(
        functools.partial(ffn_back_kernel, g),
        (tokens // TILE,),
        g.ids,
        [tr, gates, ups, scale, wd],
        [tokens_of(D), tokens_of(width), tokens_of(width), tokens_of(1), fixed(wd)],
        [tokens_of(width)] * 2 + [tokens_of(1)],
        [jax.ShapeDtypeStruct((tokens, width), bf16)] * 2 + [jax.ShapeDtypeStruct((tokens, 1), f32)],
        [],
        "ffn_back",
        2 * tokens * D * width,
    )


def back_gate_kernel(g, ids, ms, wo, mr, out):
    for k in g.slots:
        mr[:, pl.ds(place(g, ids, k), g.block)] = ms[k]
    out[...] = dot_back(g, mr, wo)


def back_gate(g, ms, wo):
    tokens = ms.shape[1]
    width = wo.shape[1]
    return launch(
        functools.partial(back_gate_kernel, g),
        (tokens // TILE,),
        g.ids,
        [ms, wo],
        [slots_of(g), fixed(wo)],
        [tokens_of(D), tokens_of(width)],
        [jax.ShapeDtypeStruct((tokens, D), bf16), jax.ShapeDtypeStruct((tokens, width), f32)],
        [],
        "back_gate",
        2 * tokens * D * width,
    )


class Sizes:
    def __init__(self, g):
        self.rows, self.cols, self.block, self.parts, self.shard, self.half = (
            g.rows, g.cols, g.block, g.parts, g.shard, g.half
        )


def piece(z, kind, y, weight, owner):
    if kind == "rows":
        return mm(y, weight[pl.ds(pl.multiple_of(owner * z.block, z.block), z.block), :], ((1,), (1,)))
    shard = owner // z.parts
    part = pl.ds(pl.multiple_of((owner % z.parts) * z.block, z.block), z.block)
    if kind == "cols":
        return mm(y, weight[shard, :, part])
    slot = (lax.axis_index("row") - shard + z.rows) % z.rows
    if kind == "ring_rows":
        return mm(y, weight[slot, part, :], ((1,), (1,)))
    if kind == "shards":
        return mm(y, weight[shard, part, :], ((1,), (1,)))
    return mm(y, weight[shard, z.shard : z.shard + y.shape[1], part])


def greet(devices):
    barrier = pltpu.get_barrier_semaphore()
    for axis, index in devices:
        pl.semaphore_signal(barrier, inc=1, device_id={axis: index}, device_id_type=MESH)
    pl.semaphore_wait(barrier, len(devices))


def remote(source, target, send, receive, axis, index):
    return pltpu.make_async_remote_copy(
        src_ref=source, dst_ref=target, send_sem=send, recv_sem=receive,
        device_id={axis: index}, device_id_type=MESH,
    )


class Ride:
    def __init__(self, z, own, whole, keep, send, receive):
        self.z, self.own, self.whole, self.kept, self.send, self.receive = z, own, whole, keep, send, receive
        self.at = lax.axis_index("row")

    def neighbours(self):
        rows = self.z.rows
        return [("row", (self.at + 1) % rows), ("row", (self.at + rows - 1) % rows)]

    def keep(self):
        return pltpu.make_async_copy(self.own, self.whole.at[self.at], self.kept)

    def step(self, n):
        rows = self.z.rows
        shard = (self.at + rows + 1 - n) % rows
        source = self.own if n == 1 else self.whole.at[shard]
        return remote(
            source, self.whole.at[shard], self.send.at[n], self.receive.at[n], "row", (self.at + 1) % rows
        )


class Rider:
    def __init__(self, z, kind, own, given, refs):
        self.z, self.kind, self.own, self.given = z, kind, own, given
        self.at = lax.axis_index("row")
        self.send, self.receive, self.spare = refs

    def step(self, n):
        rows = self.z.rows
        to = (self.at + n) % rows
        if self.kind == "spread":
            source, target = self.own, self.given.at[self.at]
        elif self.kind in ("share", "late"):
            source = target = self.spare.at[self.at]
        else:
            part = pl.ds(pl.multiple_of(to * self.z.shard, self.z.shard), self.z.shard)
            source = self.own.at[:, part] if self.kind == "deal" else self.own.at[part, :]
            target = self.given.at[n - 1]
        return remote(source, target, self.send.at[n], self.receive.at[n], "row", to)

    def keep(self):
        return pltpu.make_async_copy(self.own, self.given.at[self.at], self.spare)

    def fill(self, values):
        self.spare[self.at] = jnp.broadcast_to(values, self.own.shape)
        for n in range(1, self.z.rows):
            self.step(n).start()

    def begin(self):
        if self.kind == "late":
            return
        if self.kind == "share":
            self.spare[self.at] = self.own[...]
        if self.kind == "spread":
            self.keep().start()
        for n in range(1, self.z.rows):
            self.step(n).start()

    def end(self):
        for n in range(1, self.z.rows):
            self.step(n).wait()
        if self.kind == "spread":
            self.keep().wait()
        if self.kind in ("share", "late"):
            total = self.spare[0]
            for n in range(1, self.z.rows):
                total = total + self.spare[n]
            self.given[...] = total


DEEP = 4


def exchange_kernel(z, plan, steps, tile, *refs):
    groups, arrays, weights, gathers, kinds = plan
    ys, refs = refs[:arrays], refs[arrays:]
    ws, refs = refs[:weights], refs[weights:]
    extras, outs = [], []
    for group in groups:
        extras.append(refs[: group[2]])
        refs = refs[group[2] :]
    own, refs = refs[: len(kinds)], refs[len(kinds) :]
    for group in groups:
        outs.append(refs[: group[3]])
        refs = refs[group[3] :]
    if gathers:
        slots, refs = refs[0], refs[1:]
    given, refs = refs[: len(kinds)], refs[len(kinds) :]
    near, far, far_got, pair_got, relay_got, refs = *refs[:5], refs[5:]
    far_s, far_r, pair_s, pair_r, relay_s, relay_r, refs = *refs[:6], refs[6:]
    if gathers:
        block, own_s, same_s, same_r, turn_s, turn_r, part_s, part_r, refs = *refs[:8], refs[8:]
        cross_s, cross_r, refs = *refs[:2], refs[2:]
    me = lax.axis_index("col")
    partner = flip(me, 1)
    peers = [flip(me, 2 * j) for j in range(1, z.half)]
    met = [("col", device) for device in [partner] + peers]
    riders = [
        Rider(z, kind, own[n], given[n], refs[3 * n : 3 * n + 3]) for n, kind in enumerate(kinds)
    ]
    if riders:
        met = met + [("row", (riders[0].at + n) % z.rows) for n in range(1, z.rows)]
    greet(met)

    def rows_at(i):
        return pl.ds(pl.multiple_of(i * tile, tile), tile)

    def send_far(n, i):
        return remote(far.at[n, i % DEEP], far_got.at[n, i], far_s.at[n, i], far_r.at[n, i], "col", partner)

    def send_pair(n, i, j):
        return remote(
            near.at[n, i % DEEP, j], pair_got.at[n, i, j - 1], pair_s.at[n, i, j], pair_r.at[n, i, j],
            "col", peers[j - 1],
        )

    def keep(i):
        return pltpu.make_async_copy(block.at[i], slots.at[0, rows_at(i), :], own_s.at[i])

    def send_relay(n, i, side):
        part = pl.ds(side * (tile // 2), tile // 2)
        return remote(
            near.at[n, i % DEEP, 3, part], relay_got.at[n, i, side], relay_s.at[n, i, side], relay_r.at[n, i, side],
            "col", peers[side],
        )

    def send_cross(i, side):
        part = pl.ds(pl.multiple_of(i * tile + side * (tile // 2), tile // 2), tile // 2)
        return remote(
            slots.at[2 + 2 * side, part, :], slots.at[6, part, :], cross_s.at[i, side], cross_r.at[i, side],
            "col", peers[1 - side],
        )

    def send_part(i):
        return remote(block.at[i], slots.at[1, rows_at(i), :], part_s.at[i], part_r.at[i], "col", partner)

    def send_same(i, j):
        return remote(
            block.at[i], slots.at[2 * j, rows_at(i), :], same_s.at[i, j], same_r.at[i, j], "col", peers[j - 1]
        )

    def send_turn(i, j):
        return remote(
            slots.at[2 * j, rows_at(i), :], slots.at[2 * j + 1, rows_at(i), :],
            turn_s.at[i, j], turn_r.at[i, j], "col", partner,
        )

    def sent(i):
        for n in range(len(groups)):
            send_far(n, i).wait_send()
            for j in direct:
                send_pair(n, i, j).wait_send()
            for side in sides:
                send_relay(n, i, side).wait_send()

    fold = z.half == 4
    direct = (1, 2) if fold else tuple(range(1, z.half))
    sides = (0, 1) if fold else ()
    late = 1 if fold else 0
    lag = 3 + late + ((1 + late) if gathers else 0)
    loops = steps + lag - 1
    for rider in riders:
        rider.begin()

    @pl.loop(0, loops)
    def _(it):
        @pl.when((it >= DEEP) & (it < steps))
        def _():
            sent(it - DEEP)

        @pl.when(it < steps)
        def _():
            for n, group in enumerate(groups):
                terms = group[0]
                tiles = [ys[t[1]][rows_at(it), t[2] : t[3]] for t in terms]
                for side, held in ((1, far), (0, near)):
                    for j in range(z.half):
                        owner = flip(me, 2 * j + side)
                        total = sum(piece(z, t[0], y, ws[t[4]], owner) for t, y in zip(terms, tiles))
                        held[n, it % DEEP, j] = total.astype(bf16)
                    if side == 1:
                        send_far(n, it).start()

        @pl.when((it >= 1) & (it < steps + 1))
        def _():
            i = it - 1
            for n in range(len(groups)):
                send_far(n, i).wait_recv()
                for j in range(1, z.half):
                    near[n, i % DEEP, j] = (
                        near[n, i % DEEP, j].astype(f32) + far_got[n, i, j].astype(f32)
                    ).astype(bf16)
                    if not fold:
                        send_pair(n, i, j).start()
                for side in sides:
                    send_relay(n, i, side).start()

        if fold:
            @pl.when((it >= 2) & (it < steps + 2))
            def _():
                i = it - 2
                for n in range(len(groups)):
                    for side in sides:
                        send_relay(n, i, side).wait_recv()
                        at = (n, i % DEEP, 2 - side, slice(side * (tile // 2), (side + 1) * (tile // 2)))
                        near[at] = (near[at].astype(f32) + relay_got[n, i, side].astype(f32)).astype(bf16)
                        send_pair(n, i, 2 - side).start()

        @pl.when((it >= 2 + late) & (it < steps + 2 + late))
        def _():
            i = it - 2 - late
            for n, group in enumerate(groups):
                total = near[n, i % DEEP, 0].astype(f32) + far_got[n, i, 0].astype(f32)
                for j in direct:
                    send_pair(n, i, j).wait_recv()
                    total = total + pair_got[n, i, j - 1].astype(f32)
                result = group[1](rows_at(i), i, total, extras[n], outs[n])
                if gathers and n == 0:
                    block[i] = result
                    for j in direct:
                        send_same(i, j).start()
                    send_part(i).start()
                    keep(i).start()

        if gathers:
            @pl.when((it >= 3 + late) & (it < steps + 3 + late))
            def _():
                i = it - 3 - late
                for j in direct:
                    send_same(i, j).wait_recv()
                for side in sides:
                    send_cross(i, side).start()
                for j in direct:
                    send_turn(i, j).start()

            if fold:
                @pl.when(it >= 5)
                def _():
                    i = it - 5
                    for side in sides:
                        send_cross(i, side).wait_recv()
                    send_turn(i, 3).start()

    @pl.loop(max(0, steps - DEEP), steps)
    def _(i):
        sent(i)

    if gathers:
        @pl.loop(0, steps)
        def _(i):
            keep(i).wait()
            send_part(i).wait()
            for j in direct:
                send_same(i, j).wait_send()
            for side in sides:
                send_cross(i, side).wait_send()
            for j in range(1, z.half):
                send_turn(i, j).wait()

    for rider in riders:
        if rider.kind == "late":
            partial = outs[0][1]
            total = partial[0]
            for i in range(1, steps):
                total = total + partial[i]
            rider.fill(total)
    for rider in riders:
        rider.end()


def finish_middle(rows, i, total, extra, out):
    hidden, gain = extra
    middle = hidden[rows, :].astype(f32) + total
    out[0][rows, :] = middle
    return (middle * gain[...]).astype(bf16)


def finish_gradient(rows, i, total, extra, out):
    top, middle, gain, weigh = extra
    before = middle[rows, :]
    grad = top[rows, :].astype(f32) + gain[...] * total - before * weigh[rows, :]
    out[0][rows, :] = grad
    out[1][i] = jnp.sum(total * before, axis=0, keepdims=True)
    return grad.astype(bf16)


def finish_input(rows, i, total, extra, out):
    above, hidden, gain, scale, weigh = extra
    before = hidden[rows, :].astype(f32)
    scaled = scale[rows, :] * total
    out[0][rows, :] = above[rows, :] + gain[...] * scaled - before * weigh[rows, :]
    out[1][i] = jnp.sum(scaled * before, axis=0, keepdims=True)


def finish_out(rows, i, total, extra, out):
    (middle,) = extra
    out[0][rows, :] = (middle[rows, :] + total).astype(bf16)


def exchange(z, ys, ws, groups, gathers, number, riders=(), tile=STEP):
    tokens = ys[0].shape[0]
    steps = tokens // tile
    half, block, count = z.half, z.block, len(groups)
    vmem = pl.BlockSpec(memory_space=pltpu.VMEM)
    anywhere = pl.BlockSpec(memory_space=pl.ANY)
    dma = pltpu.SemaphoreType.DMA
    operands = [*ys, *ws]
    shapes = []
    for group in groups:
        operands += group[2]
        shapes += group[3]
    in_specs = [vmem] * len(operands)
    specs = [vmem] * len(shapes)
    scratch = [pltpu.VMEM((count, DEEP, half, tile, block), bf16)] * 2
    scratch += [pltpu.VMEM((count, steps, half, tile, block), bf16)]
    scratch += [pltpu.VMEM((count, steps, 2 if half == 4 else half - 1, tile, block), bf16)]
    scratch += [pltpu.VMEM((count, steps if half == 4 else 1, 2, tile // 2, block), bf16)]
    scratch += [dma((count, steps))] * 2 + [dma((count, steps, half))] * 2 + [dma((count, steps, 2))] * 2
    if gathers:
        shapes.append(jax.ShapeDtypeStruct((z.cols, tokens, block), bf16))
        specs.append(anywhere)
        scratch += [pltpu.VMEM((steps, tile, block), bf16), dma((steps,))]
        scratch += [dma((steps, half))] * 4 + [dma((steps,))] * 2 + [dma((steps, 2))] * 2
    by_row = dma((z.rows,))
    for kind, own in riders:
        operands.append(own)
        in_specs.append(vmem if kind in ("share", "late") else anywhere)
        specs.append(in_specs[-1])
        scratch += [by_row] * 2
        if kind == "spread":
            shapes.append(jax.ShapeDtypeStruct((z.rows,) + own.shape, bf16))
            scratch.append(dma(()))
        elif kind in ("share", "late"):
            shapes.append(jax.ShapeDtypeStruct(own.shape, f32))
            scratch.append(pltpu.VMEM((z.rows,) + own.shape, f32))
        else:
            part = (own.shape[0], z.shard) if kind == "deal" else (z.shard, own.shape[1])
            shapes.append(jax.ShapeDtypeStruct((z.rows - 1,) + part, bf16))
            scratch.append(dma(()))
    kinds = [(group[0], group[1], len(group[2]), len(group[3])) for group in groups]
    depth = sum(t[3] - t[2] for group in groups for t in group[0])
    return pl.pallas_call(
        functools.partial(
            exchange_kernel, z, (kinds, len(ys), len(ws), gathers, [kind for kind, _ in riders]), steps, tile
        ),
        in_specs=in_specs,
        out_specs=specs,
        out_shape=shapes,
        scratch_shapes=scratch,
        compiler_params=pltpu.CompilerParams(
            collective_id=number, has_side_effects=True, vmem_limit_bytes=60 << 20
        ),
        cost_estimate=cost(2 * tokens * z.cols * block * depth, operands, shapes),
        name="exchange",
    )(*operands)


def begin_kernel(z, count, *refs):
    owns, own, slots, whole = refs[:count], refs[count], refs[count + 1 : 2 * count + 1], refs[2 * count + 1]
    kept, same_s, same_r, part_s, part_r, turn_s, turn_r, keep_s, step_s, step_r = refs[2 * count + 2 :]
    me = lax.axis_index("col")
    partner = flip(me, 1)
    peers = [flip(me, 2 * j) for j in range(1, z.half)]
    ride = Ride(z, own, whole, keep_s, step_s, step_r)
    greet([("col", device) for device in [partner] + peers] + ride.neighbours())

    def keep(n):
        return pltpu.make_async_copy(owns[n], slots[n].at[0], kept.at[n])

    def send_same(n, j):
        return remote(owns[n], slots[n].at[2 * j], same_s.at[n, j], same_r.at[n, j], "col", peers[j - 1])

    def send_part(n):
        return remote(owns[n], slots[n].at[1], part_s.at[n], part_r.at[n], "col", partner)

    def send_turn(n, j):
        return remote(slots[n].at[2 * j], slots[n].at[2 * j + 1], turn_s.at[n, j], turn_r.at[n, j], "col", partner)

    ride.step(1).start()
    ride.keep().start()
    for n in range(count):
        for j in range(1, z.half):
            send_same(n, j).start()
        send_part(n).start()
        keep(n).start()
    for s in range(2, z.rows):
        ride.step(s - 1).wait_recv()
        ride.step(s).start()
    for n in range(count):
        for j in range(1, z.half):
            send_same(n, j).wait_recv()
            send_turn(n, j).start()
    ride.keep().wait()
    ride.step(z.rows - 1).wait_recv()
    for s in range(1, z.rows):
        ride.step(s).wait_send()
    for n in range(count):
        keep(n).wait()
        send_part(n).wait()
        for j in range(1, z.half):
            send_same(n, j).wait_send()
            send_turn(n, j).wait()


def begin(z, owns, own, number):
    anywhere = pl.BlockSpec(memory_space=pl.ANY)
    dma = pltpu.SemaphoreType.DMA
    count = len(owns)
    shapes = [jax.ShapeDtypeStruct((z.cols,) + o.shape, o.dtype) for o in owns]
    shapes.append(jax.ShapeDtypeStruct((z.rows,) + own.shape, own.dtype))
    operands = [*owns, own]
    return pl.pallas_call(
        functools.partial(begin_kernel, z, count),
        in_specs=[anywhere] * len(operands),
        out_specs=[anywhere] * len(shapes),
        out_shape=shapes,
        scratch_shapes=[dma((count,))] + [dma((count, z.half))] * 2 + [dma((count,))] * 2
        + [dma((count, z.half))] * 2 + [dma(())] + [dma((z.rows,))] * 2,
        compiler_params=pltpu.CompilerParams(collective_id=number, has_side_effects=True),
        cost_estimate=cost(10**6, operands, shapes),
        name="begin",
    )(*operands)


def rows_product(first_op, second_op):
    return lax.dot_general(
        first_op, second_op, (((0,), (0,)), ((), ())), preferred_element_type=f32
    )


def on_device(
    hidden_in,
    seg_ids,
    cotangent,
    norm_mixer,
    w_query,
    w_key,
    w_value,
    w_gate,
    w_beta,
    w_decay,
    decay_log,
    conv_query,
    conv_key,
    conv_value,
    norm_gated,
    w_out,
    norm_ffn,
    w_ffn_gate,
    w_ffn_up,
    w_ffn_down,
):
    g = Grid()
    z = Sizes(g)
    tokens = seg_ids.shape[0]
    seqs = tokens // SEQ
    heads = decay_log.shape[0]
    local = jax.ShapeDtypeStruct((tokens, g.block), f32)
    sums = jax.ShapeDtypeStruct((tokens // STEP, 1, g.block), f32)

    def by_seq(values):
        return values.reshape(seqs, SEQ, values.shape[1])

    def flat(values):
        return values.reshape(tokens, values.shape[2])

    few = 2 * heads
    ins = (w_query, w_key, w_gate)
    widths = [w.shape[1] for w in ins]
    inw = g.gather_rows(jnp.concatenate(ins, axis=1))
    wide = max(w_value.shape[1], g.shard)
    value_in = jnp.pad(w_value, ((0, 16), (0, wide - w_value.shape[1])))
    value_in = lax.dynamic_update_slice(
        value_in, jnp.concatenate([w_beta, w_decay], axis=1).T, (g.shard, 0)
    )
    ow = g.gather_rows(w_out[None])
    dw = g.gather_rows(w_ffn_down[None])
    ew = g.gather_rows(w_ffn_gate)
    own_gains = jnp.stack([norm_mixer, norm_ffn])
    own_gains = jnp.pad(own_gains, ((0, 6), (0, 0)))
    blocks, tops, gains, vw = begin(z, [hidden_in, cotangent, own_gains], value_in, 3)
    order = jnp.arange(g.cols) ^ g.me
    gains = jnp.swapaxes(jnp.take(gains[:, :2], order, axis=0), 0, 1).reshape(2, D)

    normed, scale_mixer, pq, pk, pg, pv, proj_small = project(g, blocks, gains[:1], inw, vw, widths, few)
    up_own, _ = lax.optimization_barrier((w_ffn_up, proj_small))
    uw = g.spread(up_own)
    projected = [by_seq(p) for p in (pq, pk, pv, pg)]
    proj_beta, proj_decay = proj_small[:heads], proj_small[heads:]
    strength = jax.nn.sigmoid(proj_beta)
    rate = -jnp.exp(decay_log)[:, None]
    log_decay = rate * jax.nn.softplus(proj_decay)
    rows, cols = token_tables(seg_ids, strength, log_decay)
    gain_gated = norm_gated[None]
    gated, inv, upd, states = mixer_forward(
        *projected, cols, rows, conv_query, conv_key, conv_value, gain_gated
    )
    gated = flat(gated)
    middle, mids = exchange(
        z, [gated], [ow],
        [([("cols", 0, 0, gated.shape[1], 0)], finish_middle, [hidden_in, norm_ffn[None]], [local])],
        True, 0,
    )
    undo = 1.0 / (gains[1:] * gains[1:])
    xr, tr, gates, ups, inner, scale_ffn = ffn(g, mids, tops, undo, ew, uw)
    down_term = rows_product(inner, tr).astype(bf16)
    gates, held = lax.optimization_barrier((gates, down_term))
    dgate, dup, weigh = ffn_back(g, tr, gates, ups, scale_ffn, dw)
    weigh = weigh[:, 0]
    wide = [rows_product(xr, dgate).astype(bf16)]
    weigh = weigh + g.swap(weigh, "col", 1)
    weigh, left = lax.optimization_barrier((weigh, dup))
    wide.append(rows_product(xr, left).astype(bf16))
    weigh = weigh + g.swap(weigh, "col", 2)
    bits = 4
    while bits < g.cols:
        weigh = weigh + g.swap(weigh, "col", bits)
        bits *= 2
    weigh = scale_ffn * scale_ffn * weigh[:, None] / D
    weigh = lax.optimization_barrier((weigh, *wide))[0]
    gate_grad, up_grad = (g.sum_rows(w, 0) for w in wide)
    down_grad = g.sum_rows(down_term, 1)
    hidden_units = dgate.shape[1]
    grad_middle, norm_sums, downs = exchange(
        z, [dgate, dup], [ew, uw],
        [(
            [("rows", 0, 0, hidden_units, 0), ("ring_rows", 1, 0, hidden_units, 1)], finish_gradient,
            [cotangent, middle, norm_ffn[None], weigh], [local, sums],
        )],
        True, 1,
    )
    grad_norm_ffn = jnp.sum(norm_sums, axis=(0, 1))
    mr, grad_gated = back_gate(g, downs, ow)
    out_term = rows_product(gated, mr).astype(bf16)
    grad_gated = lax.optimization_barrier((grad_gated, out_term))[0]
    out_term, up_grad = lax.optimization_barrier((out_term, up_grad))
    out_grad = g.sum_rows(out_term, 1)
    dproj, dcols, dwq, dwk, dwv, dgain = mixer_backward(
        by_seq(grad_gated), *projected, cols, rows, inv, upd, states,
        conv_query, conv_key, conv_value, gain_gated,
    )
    dproj = flat(dproj)
    most = sum(widths)
    in_grads = g.sum_rows(rows_product(normed, dproj).astype(bf16), 0)
    dsmall = flat(dcols).T
    dstrength, dlog = dsmall[:heads], dsmall[heads:few]
    grad_small = jnp.concatenate(
        [dstrength * strength * (1.0 - strength), dlog * rate * jax.nn.sigmoid(proj_decay)], axis=0
    )
    weigh = g.total(dsmall[few] + jnp.sum(grad_small * proj_small, axis=0), "col")[:, None]
    weigh = scale_mixer * scale_mixer * weigh / D
    grad_small = grad_small.astype(bf16)
    small_grads = jnp.dot(grad_small, normed, preferred_element_type=f32)
    grad_decay_log = jnp.sum(dlog * log_decay, axis=1)
    pieces = [dwq, dwk, dwv, dgain, grad_norm_ffn, grad_decay_log, small_grads]
    count = sum(p.size for p in pieces)
    fill = jnp.zeros((-count % 1024,), f32)
    joined = jnp.concatenate([p.reshape(-1) for p in pieces] + [fill]).reshape(-1, 128)
    grad_input, _, block_out, joined, grad_norm_mixer = exchange(
        z, [dproj, grad_small.T, inner], [inw, vw, dw],
        [
            (
                [("rows", 0, 0, most, 0), ("shards", 0, most, dproj.shape[1], 1), ("small", 1, 0, few, 1)],
                finish_input, [grad_middle, hidden_in, norm_mixer[None], scale_mixer, weigh], [local, sums],
            ),
            (
                [("cols", 2, 0, hidden_units, 2)], finish_out, [middle],
                [jax.ShapeDtypeStruct((tokens, g.block), bf16)],
            ),
        ],
        False, 2, [("share", joined), ("late", jnp.zeros((8, g.block), f32))],
    )
    joined = joined.reshape(-1)
    grad_norm_mixer = grad_norm_mixer[0]
    summed, at = [], 0
    for p in pieces:
        summed.append(joined[at : at + p.size].reshape(p.shape))
        at += p.size
    small_grads = lax.dynamic_slice(summed[6], (0, g.at * g.shard), (few, g.shard)).T
    grads, at = [], 0
    for w in widths + [w_value.shape[1]]:
        grads.append(in_grads[:, at : at + w].astype(f32))
        at += w
    return (
        block_out,
        grad_input,
        grad_norm_mixer,
        grads[0],
        grads[1],
        grads[3],
        grads[2],
        small_grads[:, :heads],
        small_grads[:, heads:],
        summed[5],
        summed[0],
        summed[1],
        summed[2],
        summed[3][0],
        out_grad.astype(f32),
        summed[4],
        gate_grad.astype(f32),
        up_grad.astype(f32),
        down_grad.astype(f32),
    )


def solution(mesh):
    placed = (
        P("row", "col"),
        P("row"),
        P("row", "col"),
        P("col"),
        P("row", "col"),
        P("row", "col"),
        P("row", "col"),
        P("row", "col"),
        P("row", "col"),
        P("row", "col"),
        P("col"),
        P(None, "col"),
        P(None, "col"),
        P(None, "col"),
        P("col"),
        P("col", "row"),
        P("col"),
        P("row", "col"),
        P("row", "col"),
        P("col", "row"),
    )
    return jax.shard_map(
        on_device,
        mesh=mesh,
        in_specs=placed,
        out_specs=(
            P("row", "col"),
            P("row", "col"),
            P("col"),
            P("row", "col"),
            P("row", "col"),
            P("row", "col"),
            P("row", "col"),
            P("row", "col"),
            P("row", "col"),
            P("col"),
            P(None, "col"),
            P(None, "col"),
            P(None, "col"),
            P("col"),
            P("col", "row"),
            P("col"),
            P("row", "col"),
            P("row", "col"),
            P("col", "row"),
        ),
        check_vma=False,
    )
```
